32 devices in a mesh: rows: 8 (over z, y), cent: 4 (over x, core).
Axes of the slice: x: 2, y: 2, z: 4, core: 2. Of those that a mesh axis runs over, the one named last changes fastest.
Arguments:
- samples: bfloat16 [8192, 512], P('rows'), may hold values from -6 to 6
- weights: float32 [8192], P('rows'), may hold values from 0.2 to 18, as said below
- targets: float32 [16, 8192], P(None, 'rows'), may hold values from -6 to 6
- predictions: float32 [16, 8192], P(None, 'rows'), may hold values from -3 to 3
- centres: bfloat16 [32768, 512], P('rows'), may hold values from -6 to 6
- coefs: float32 [16, 32768], P(None, 'rows'), may hold values from -7 to 7
- block_index: int32 [2, 12288], P(None, 'cent'), may hold values from 0 to 32767, as said below
Outputs:
- new_coefs: float32 [16, 32768], P(None, 'rows')
- new_predictions: float32 [16, 8192], P(None, 'rows')
The draws below stay inside these ranges and needn't reach their ends.
Inputs may be any that keep to these rules, and one draw needn't show every extreme that they name: Positive sample weights. `block_index`: no pool index appears twice in the whole array. In every step each aligned block of 3072 entries starting at a multiple of 3072 takes exactly 384 indices from each pool shard (index // 4096).
All inputs are finite; a program needn't handle non-finite values.
Results may differ from the reference program's by a relative error of at most 0.008.
Values may be sent and summed in bfloat16 or wider, within the bound.
No kernel may reach another device: no remote copies, remote signals or barrier semaphores. Data moves between devices by JAX's collectives and lax.ppermute only.
A program may use at most 64 MiB of HBM per device.

```python
import math
import jax
import jax.numpy as jnp
from jax import lax

F = 512
TARGETS = 16
BLOCK = 12288
STEPS = 2
POOL_DEV = 4096
ROWS = 8192
POOL = 32768
SLICE = 3072


def draw_samples(key, part):
    values = jax.random.truncated_normal(key, -6.0, 6.0, (ROWS, F), jnp.float32)
    return values.astype(jnp.bfloat16)


def draw_centres(key, part):
    values = jax.random.truncated_normal(key, -6.0, 6.0, (POOL, F), jnp.float32)
    return values.astype(jnp.bfloat16)


def draw_targets(key, part):
    return jax.random.truncated_normal(key, -6.0, 6.0, (TARGETS, ROWS), jnp.float32)


def draw_coefs(key, part):
    return jax.random.truncated_normal(key, -6.0, 6.0, (TARGETS, POOL), jnp.float32)


def draw_weights(key, part):
    ramp = jnp.arange(ROWS, dtype=jnp.float32) / ROWS
    base = jnp.exp(jax.random.uniform(key, (ROWS,), jnp.float32, math.log(0.3), math.log(3.0)))
    return base * jnp.exp(math.log(3.0) * ramp)


def draw_block_index(key, part):
    owners_count = POOL // POOL_DEV
    slices_count = BLOCK // SLICE
    share = SLICE // owners_count
    taken = STEPS * slices_count * share

    def one_owner(owner_id):
        order = jax.random.permutation(jax.random.fold_in(key, owner_id), POOL_DEV)
        return order[:taken].astype(jnp.int32) + owner_id * POOL_DEV
    chosen = jax.vmap(one_owner)(jnp.arange(owners_count, dtype=jnp.int32))
    chosen = chosen.reshape(owners_count, STEPS, slices_count, share)
    chosen = chosen.transpose(1, 2, 0, 3).reshape(STEPS * slices_count, SLICE)
    mixer = jax.random.fold_in(key, 7919 + owners_count)

    def shuffle(group_id, entries):
        order = jax.random.permutation(jax.random.fold_in(mixer, group_id), SLICE)
        return entries[order]
    mixed = jax.vmap(shuffle)(jnp.arange(STEPS * slices_count, dtype=jnp.int32), chosen)
    return mixed.reshape(STEPS, BLOCK).astype(jnp.int32)


def steps_of(own_key, shape, split, least, top_value):
    factor_of, own = 1.0, jax.random.fold_in(own_key, 6)
    for dim, shards_of in split:
        steps = jnp.exp(jax.random.uniform(jax.random.fold_in(own, dim), (shards_of,), jnp.float32, least / len(split), top_value / len(split)))
        factor_of = factor_of * jnp.repeat(steps, shape[dim] // shards_of).reshape([-1 if axis == dim else 1 for axis in range(len(shape))])
    return factor_of


def scatter_about(key, shape, width, bound, cuts=(), kind=jnp.bfloat16):
    result = width * jax.random.normal(key, shape, jnp.float32)
    if cuts:
        result = result * steps_of(key, shape, cuts, -0.22, 0.18)
    return jnp.clip(result, -bound, bound).astype(kind)


def setup_inputs(seed: int = 0) -> dict:
    keys = jax.random.split(jax.random.key(seed), 8)
    samples = draw_samples(jax.random.fold_in(keys[7], 71), 0)
    weights = draw_weights(jax.random.fold_in(keys[7], 71), 0)
    targets = draw_targets(jax.random.fold_in(keys[7], 71), 0)
    predictions = scatter_about(keys[3], (TARGETS, ROWS), 0.5, 3.0, ((1, 8),), jnp.float32)
    centres = draw_centres(jax.random.fold_in(keys[7], 71), 0)
    coefs = draw_coefs(jax.random.fold_in(keys[7], 71), 0)
    block_index = draw_block_index(jax.random.fold_in(keys[7], 71), 0)
    return dict(samples=samples, weights=weights, targets=targets, predictions=predictions, centres=centres, coefs=coefs, block_index=block_index)


RIDGE = 1.0

def kernel_tile(rows_x, rows_norm, centre_rows, centre_norm, sharpness, offset):
    products = lax.dot_general(rows_x, centre_rows, (((1,), (1,)), ((), ())), preferred_element_type=jnp.float32)
    exponent = offset + sharpness * (2.0 * products - rows_norm[:, None] - centre_norm[None, :])
    return jnp.exp(exponent).astype(jnp.bfloat16)

def reference(samples, weights, targets, predictions, centres, coefs, block_index):
    sharpness = 1.3 / math.sqrt(8.0 * F)
    offset = 2.0 * F * sharpness - 1.5 - 0.5 * math.log(ROWS)
    block_rows = math.gcd(ROWS, 512)
    blocks = ROWS // block_rows
    row_norm = lax.optimization_barrier(jnp.sum(jnp.square(samples.astype(jnp.float32)), axis=1))
    sample_blocks = samples.reshape(blocks, block_rows, F)
    norm_blocks = row_norm.reshape(blocks, block_rows)
    weight_blocks = weights.reshape(blocks, block_rows)
    coef = coefs
    pred = predictions
    for step_idx in range(STEPS):
        chosen_idx = block_index[step_idx]
        chosen = centres[chosen_idx]
        centre_norm = lax.optimization_barrier(jnp.sum(jnp.square(chosen.astype(jnp.float32)), axis=1))
        old_coef = coef[:, chosen_idx]
        weighted = (weights[None, :] * (targets - pred)).astype(jnp.bfloat16)
        weighted_blocks = weighted.reshape(TARGETS, blocks, block_rows).transpose(1, 0, 2)

        def first_pass(carry, item):
            gradient, col_square = carry
            rows_x, rows_norm, row_weight, resid = item
            kernel = kernel_tile(rows_x, rows_norm, chosen, centre_norm, sharpness, offset)
            gradient = gradient + jnp.dot(resid, kernel, preferred_element_type=jnp.float32)
            kernel_wide = kernel.astype(jnp.float32)
            col_square = col_square + lax.optimization_barrier(jnp.sum(row_weight[:, None] * kernel_wide * kernel_wide, axis=0))
            return ((gradient, col_square), None)
        start = (jnp.zeros((TARGETS, BLOCK), jnp.float32), jnp.zeros((BLOCK,), jnp.float32))
        (gradient, col_square), _ = lax.scan(first_pass, start, (sample_blocks, norm_blocks, weight_blocks, weighted_blocks))
        gradient = gradient - RIDGE * old_coef
        delta = gradient / (col_square + RIDGE)[None, :]
        coef = coef.at[:, chosen_idx].add(delta)
        delta_low = delta.astype(jnp.bfloat16)

        def second_pass(carry, item):
            rows_x, rows_norm = item
            kernel = kernel_tile(rows_x, rows_norm, chosen, centre_norm, sharpness, offset)
            change = lax.dot_general(delta_low, kernel, (((1,), (1,)), ((), ())), preferred_element_type=jnp.float32)
            return (carry, change)
        _, changes = lax.scan(second_pass, jnp.zeros((), jnp.float32), (sample_blocks, norm_blocks))
        pred = pred + changes.transpose(1, 0, 2).reshape(TARGETS, ROWS)
    return (coef, pred)
```

```python
import functools
import math

import jax
import jax.numpy as jnp
from jax import lax
from jax.experimental import pallas as pl
from jax.experimental.pallas import tpu as pltpu
from jax.sharding import PartitionSpec as P

RIDGE = 1.0
LANES = 128
POOL_BLOCK = 256
LOG2E = math.log2(math.e)
NT = (((1,), (1,)), ((), ()))
F32 = jnp.float32
BF16 = jnp.bfloat16


def split3(x):
    first = x.astype(BF16)
    rest = x - first.astype(F32)
    second = rest.astype(BF16)
    third = (rest - second.astype(F32)).astype(BF16)
    return first, second, third


def split3_outside(x):
    first = lax.reduce_precision(x, 8, 7)
    rest = x - first
    second = lax.reduce_precision(rest, 8, 7)
    third = rest - second
    return first.astype(BF16), second.astype(BF16), third.astype(BF16)


def round_up(value, multiple):
    return -(-value // multiple) * multiple


def compact_kernel(steps, per_step, targets, tile, off_ref, dest_ref, pool_ref, side_ref, out_ref, side_out, norm_ref, coef_ref):
    group = pl.program_id(0)
    blocks = pool_ref.shape[0] // POOL_BLOCK

    @pl.when(group == 0)
    def _():
        out_ref[...] = jnp.zeros_like(out_ref)
        side_out[...] = jnp.zeros_like(side_out)

    for i in range(blocks):
        pool_rows = pool_ref[i * POOL_BLOCK : (i + 1) * POOL_BLOCK, :]
        side_rows = side_ref[i * POOL_BLOCK : (i + 1) * POOL_BLOCK, :]
        for step in range(steps):
            start = off_ref[step, group * blocks + i]
            end = off_ref[step, group * blocks + i + 1]
            base = pl.multiple_of((start // 16) * 16, 16)
            need = end - base
            dest = jnp.concatenate(
                [dest_ref[step, 2 * i : 2 * i + 1, :], dest_ref[step, 2 * i + 1 : 2 * i + 2, :]], axis=1
            ) - base
            for first, size in ((0, 128), (128, 144)):

                @pl.when((need > first) & (end > start))
                def _(first=first, size=size):
                    slots = lax.broadcasted_iota(jnp.int32, (size, POOL_BLOCK), 0) + first
                    pick = jnp.where(slots == dest, 1.0, 0.0).astype(BF16)
                    rows = jnp.dot(pick, pool_rows, preferred_element_type=F32)
                    side = jnp.dot(pick, side_rows, preferred_element_type=F32)
                    at = pl.ds(pl.multiple_of(base + first, 16), size)
                    out_ref[step, at, :] += rows.astype(BF16)
                    side_out[step, at, :] += side.astype(BF16)

    @pl.when(group == pl.num_programs(0) - 1)
    def _():
        features = out_ref.shape[2]
        ones = jnp.ones((8, features), BF16)
        eye = (
            lax.broadcasted_iota(jnp.int32, (3 * targets, LANES), 0)
            == lax.broadcasted_iota(jnp.int32, (3 * targets, LANES), 1)
        )
        eye = jnp.where(eye, 1.0, 0.0).astype(BF16)
        for step in range(steps):
            for first in range(0, per_step, tile):
                rows = out_ref[step, first : first + tile, :].astype(F32)
                square = rows * rows
                high = square.astype(BF16)
                low = (square - high.astype(F32)).astype(BF16)
                norm = lax.dot_general(ones, high, NT, preferred_element_type=F32)
                norm = norm + lax.dot_general(ones, low, NT, preferred_element_type=F32)
                norm_ref[step, :, first : first + tile] = norm
                side = side_out[step, first : first + tile, :]
                parts = lax.dot_general(eye, side, NT, preferred_element_type=F32)
                coef_ref[step, :, first : first + tile] = (
                    parts[:targets] + parts[targets : 2 * targets] + parts[2 * targets :]
                )


def compact(off, dest, pool, side, per_step, targets):
    steps = dest.shape[0]
    pool_dev, features = pool.shape
    groups = pool_dev // (8 * LANES)
    length = round_up(per_step, 16) + POOL_BLOCK + 16
    tile = math.gcd(per_step, 512)
    whole = lambda *shape: pl.BlockSpec(shape, lambda g, off: (0,) * len(shape))
    return pl.pallas_call(
        functools.partial(compact_kernel, steps, per_step, targets, tile),
        name="compact",
        out_shape=(
            jax.ShapeDtypeStruct((steps, length, features), BF16),
            jax.ShapeDtypeStruct((steps, length, LANES), BF16),
            jax.ShapeDtypeStruct((steps, 8, per_step), F32),
            jax.ShapeDtypeStruct((steps, targets, per_step), F32),
        ),
        grid_spec=pltpu.PrefetchScalarGridSpec(
            num_scalar_prefetch=1,
            grid=(groups,),
            in_specs=[
                pl.BlockSpec((steps, 8, LANES), lambda g, off: (0, g, 0)),
                pl.BlockSpec((8 * LANES, features), lambda g, off: (g, 0)),
                pl.BlockSpec((8 * LANES, LANES), lambda g, off: (g, 0)),
            ],
            out_specs=[
                whole(steps, length, features),
                whole(steps, length, LANES),
                whole(steps, 8, per_step),
                whole(steps, targets, per_step),
            ],
        ),
        cost_estimate=pl.CostEstimate(flops=10**10, bytes_accessed=8 * 10**6, transcendentals=0),
    )(off, dest, pool, side)


def block_kernel(steps, targets, quarter, scale, offset, slot_ref, rows_ref, chosen_ref, norm_ref, *refs):
    sums_in, (k_ref, sums_ref, side_ref, row_ref, weight_ref) = refs[-6 - 0], refs[-5:]
    tile, step = pl.program_id(0), pl.program_id(1)

    @pl.when((tile == 0) & (step == 0))
    def _():
        rows = rows_ref[:quarter, :].astype(F32)
        row_ref[...] = jnp.sum(rows * rows, axis=1, keepdims=True) * (scale * LOG2E) - offset * LOG2E
        parts = rows_ref[quarter : quarter + 3, quarter : 2 * quarter].astype(F32)
        weight = jnp.sum(parts, axis=0, keepdims=True)
        weight_ref[...] = jnp.transpose(jnp.broadcast_to(weight, (8, quarter)))[:, :1]
        side_ref[:targets, :] = rows_ref[quarter : quarter + targets, :quarter].astype(F32)
        side_ref[targets:, :] = jnp.broadcast_to(weight, (side_ref.shape[0] - targets, quarter))

    dots = lax.dot_general(rows_ref[:quarter, :], chosen_ref[0], NT, preferred_element_type=F32)
    centre = norm_ref[0, :1, :] * (scale * LOG2E)
    k_low = jnp.exp2(dots * (2.0 * scale * LOG2E) - row_ref[...] - centre).astype(BF16)
    k_ref[0] = k_low
    wide = k_low.astype(F32)
    square = jnp.sum(weight_ref[...] * (wide * wide), axis=0, keepdims=True)

    @pl.when(step == 0)
    def _():
        weighted = rows_ref[quarter : quarter + targets, :quarter]
        share = jnp.dot(weighted, k_low, preferred_element_type=F32)
        if sums_in is None:
            sums_ref[...] = jnp.zeros_like(sums_ref)
            sums_ref[:targets, :] = share
        else:
            sums_ref[...] = sums_in[...]
            sums_ref[:targets, :] += share

    for s in range(steps):

        @pl.when(step == s)
        def _(s=s):
            sums_ref[targets + s : targets + s + 1, :] += square


def block_call(slot, rows, chosen, norm, state, per_step, targets, row_devices, scale, offset):
    steps = chosen.shape[0]
    features = chosen.shape[2]
    quarter = rows.shape[0] - round_up(targets, 16)
    tile = math.gcd(per_step, 512)
    tiles = per_step // tile
    sum_rows = round_up(targets + steps, 8)
    side_rows = round_up(targets + 1, 8)
    in_specs = [
        pl.BlockSpec(rows.shape, lambda j, s, slot: (0, 0)),
        pl.BlockSpec((1, tile, features), lambda j, s, slot: (s, j, 0)),
        pl.BlockSpec((1, 8, tile), lambda j, s, slot: (s, 0, j)),
    ]
    sums_spec = pl.BlockSpec((sum_rows, tile), lambda j, s, slot: (0, j))
    operands = [slot, rows, chosen, norm]
    aliases = {}
    if state is not None:
        in_specs += [pl.BlockSpec(memory_space=pl.ANY), pl.BlockSpec(memory_space=pl.ANY), sums_spec]
        k_all, sums, side = state
        operands += [k_all, side, sums]
        aliases = {4: 0, 5: 2, 6: 1}

    def body(slot_ref, rows_ref, chosen_ref, norm_ref, *refs):
        if state is None:
            refs = (None,) + refs
        else:
            refs = refs[2:]
        block_kernel(
            steps, targets, quarter, scale, offset, slot_ref, rows_ref, chosen_ref, norm_ref, *refs
        )

    entries = quarter * per_step * steps
    return pl.pallas_call(
        body,
        name="kernel_block",
        out_shape=(
            jax.ShapeDtypeStruct((row_devices, quarter, steps * per_step), BF16),
            jax.ShapeDtypeStruct((sum_rows, per_step), F32),
            jax.ShapeDtypeStruct((side_rows, row_devices * quarter), F32),
        ),
        grid_spec=pltpu.PrefetchScalarGridSpec(
            num_scalar_prefetch=1,
            grid=(tiles, steps),
            in_specs=in_specs,
            out_specs=[
                pl.BlockSpec((1, quarter, tile), lambda j, s, slot: (slot[0], 0, s * tiles + j)),
                sums_spec,
                pl.BlockSpec((side_rows, quarter), lambda j, s, slot: (0, slot[0])),
            ],
            scratch_shapes=[pltpu.VMEM((quarter, 1), F32), pltpu.VMEM((quarter, 1), F32)],
        ),
        input_output_aliases=aliases,
        cost_estimate=pl.CostEstimate(
            flops=2 * entries * features, bytes_accessed=2 * entries, transcendentals=entries
        ),
    )(*operands)


def change_kernel(targets, step, sums_ref, square_ref, coef_ref, k_ref, *refs):
    delta_ref, change_ref, low_ref = refs[-3:]
    part = pl.program_id(0)

    @pl.when(part == 0)
    def _():
        total = jnp.sum(sums_ref[:, :targets, :], axis=0)
        square = jnp.sum(square_ref[:, targets + step : targets + step + 1, :], axis=0)
        delta = (total - RIDGE * coef_ref[0]) / (square + RIDGE)
        delta_ref[...] = delta
        low_ref[...] = delta.astype(BF16)

    change = lax.dot_general(low_ref[...], k_ref[0], NT, preferred_element_type=F32)
    if len(refs) > 3:
        change = change + refs[0][0]
    change_ref[0] = change


def change_call(sums, squares, coef, k_all, step, targets, before=None):
    row_devices, quarter, width = k_all.shape
    per_step = sums.shape[2]
    whole = lambda shape: pl.BlockSpec(shape, lambda i: (0,) * len(shape))
    change_spec = pl.BlockSpec((1, targets, quarter), lambda i: (i, 0, 0))
    more = [] if before is None else [before]
    return pl.pallas_call(
        functools.partial(change_kernel, targets, step),
        name="change",
        grid=(row_devices,),
        in_specs=[
            whole(sums.shape),
            whole(squares.shape),
            pl.BlockSpec((1, targets, per_step), lambda i: (step, 0, 0)),
            pl.BlockSpec((1, quarter, per_step), lambda i: (i, 0, step)),
        ]
        + [change_spec] * len(more),
        out_specs=[whole((targets, per_step)), change_spec],
        out_shape=(
            jax.ShapeDtypeStruct((targets, per_step), F32),
            jax.ShapeDtypeStruct((row_devices, targets, quarter), F32),
        ),
        scratch_shapes=[pltpu.VMEM((targets, per_step), BF16)],
        cost_estimate=pl.CostEstimate(
            flops=2 * targets * row_devices * quarter * per_step,
            bytes_accessed=2 * row_devices * quarter * per_step,
            transcendentals=0,
        ),
    )(sums, squares, coef, k_all, *more)


def gradient_kernel(targets, moved_ref, side_ref, k_ref, out_ref):
    part = pl.program_id(0)
    weighted = (side_ref[:targets, :] - moved_ref[0]).astype(BF16)
    share = jnp.dot(weighted, k_ref[0], preferred_element_type=F32)

    @pl.when(part == 0)
    def _():
        out_ref[...] = share

    @pl.when(part > 0)
    def _():
        out_ref[...] += share


def gradient_call(moved, side, k_all, step, targets, per_step):
    row_devices, quarter, width = k_all.shape
    return pl.pallas_call(
        functools.partial(gradient_kernel, targets),
        name="gradient",
        grid=(row_devices,),
        in_specs=[
            pl.BlockSpec((1, targets, quarter), lambda i: (i, 0, 0)),
            pl.BlockSpec((side.shape[0], quarter), lambda i: (0, i)),
            pl.BlockSpec((1, quarter, per_step), lambda i: (i, 0, step)),
        ],
        out_specs=pl.BlockSpec((targets, per_step), lambda i: (0, 0)),
        out_shape=jax.ShapeDtypeStruct((targets, per_step), F32),
        cost_estimate=pl.CostEstimate(
            flops=2 * targets * row_devices * quarter * per_step,
            bytes_accessed=2 * row_devices * quarter * per_step,
            transcendentals=0,
        ),
    )(moved, side, k_all)


def scatter_kernel(targets, per_step, off_ref, dest_ref, delta_ref, coef_ref, out_ref, parts_ref):
    group = pl.program_id(0)
    blocks = out_ref.shape[1] // POOL_BLOCK
    length = parts_ref.shape[1]

    @pl.when(group == 0)
    def _():
        for part, value in enumerate(split3(delta_ref[...])):
            parts_ref[part * targets : (part + 1) * targets, :per_step] = value
        parts_ref[:, per_step:] = jnp.zeros((3 * targets, length - per_step), BF16)

    for i in range(blocks):
        columns = slice(i * POOL_BLOCK, (i + 1) * POOL_BLOCK)
        start = off_ref[0, group * blocks + i]
        end = off_ref[0, group * blocks + i + 1]
        base = pl.multiple_of((start // LANES) * LANES, LANES)
        dest = jnp.concatenate(
            [dest_ref[0, 2 * i : 2 * i + 1, :], dest_ref[0, 2 * i + 1 : 2 * i + 2, :]], axis=1
        ) - base
        out_ref[:, columns] = coef_ref[:, columns]
        for first in range(0, POOL_BLOCK + LANES, LANES):

            @pl.when((end - base > first) & (end > start))
            def _(first=first):
                slots = lax.broadcasted_iota(jnp.int32, (LANES, POOL_BLOCK), 0) + first
                pick = jnp.where(slots == dest, 1.0, 0.0).astype(BF16)
                at = pl.ds(pl.multiple_of(base + first, LANES), LANES)
                moved = jnp.dot(parts_ref[:, at], pick, preferred_element_type=F32)
                out_ref[:, columns] += (
                    moved[:targets] + moved[targets : 2 * targets] + moved[2 * targets :]
                )


def scatter_call(off, dest, delta, coefs, step):
    targets, per_step = delta.shape
    pool_dev = coefs.shape[1]
    groups = pool_dev // (8 * LANES)
    length = round_up(per_step, LANES) + POOL_BLOCK + LANES
    return pl.pallas_call(
        functools.partial(scatter_kernel, targets, per_step),
        name="scatter",
        grid_spec=pltpu.PrefetchScalarGridSpec(
            num_scalar_prefetch=1,
            grid=(groups,),
            in_specs=[
                pl.BlockSpec((1, 8, LANES), lambda g, off: (step, g, 0)),
                pl.BlockSpec((targets, per_step), lambda g, off: (0, 0)),
                pl.BlockSpec((targets, 8 * LANES), lambda g, off: (0, g)),
            ],
            out_specs=pl.BlockSpec((targets, 8 * LANES), lambda g, off: (0, g)),
            scratch_shapes=[pltpu.VMEM((3 * targets, length), BF16)],
        ),
        out_shape=jax.ShapeDtypeStruct((targets, pool_dev), F32),
        cost_estimate=pl.CostEstimate(flops=10**9, bytes_accessed=10**6, transcendentals=0),
    )(off[step : step + 1], dest, delta, coefs)


def swap(value, axis, bit):
    count = lax.axis_size(axis)
    return lax.ppermute(value, axis, [(i, i ^ bit) for i in range(count)])


def bits_of(count):
    return [1 << k for k in range(count.bit_length() - 1)]


def local(samples, weights, targets, predictions, centres, coefs, block_index):
    rows_dev, features = samples.shape
    pool_dev = centres.shape[0]
    steps, slice_len = block_index.shape
    target_count = targets.shape[0]
    row_devices, cent_devices = lax.axis_size("rows"), lax.axis_size("cent")
    my_row, my_cent = lax.axis_index("rows"), lax.axis_index("cent")
    quarter = rows_dev // cent_devices
    per_step = slice_len * cent_devices // row_devices
    sharpness = 1.3 / math.sqrt(8.0 * features)
    offset = 2.0 * features * sharpness - 1.5 - 0.5 * math.log(rows_dev * row_devices)

    at = my_cent * quarter
    own_rows = lax.dynamic_slice_in_dim(samples, at, quarter, 0)
    own_weight = lax.dynamic_slice_in_dim(weights, at, quarter, 0)[None, :]
    own_target = lax.dynamic_slice_in_dim(targets, at, quarter, 1)
    own_pred = lax.dynamic_slice_in_dim(predictions, at, quarter, 1)
    weighted = (own_weight * (own_target - own_pred)).astype(BF16)
    side_count = round_up(target_count, 16)
    weight_parts = jnp.concatenate(split3_outside(own_weight), axis=0)
    side_block = jnp.concatenate(
        [
            jnp.pad(weighted, ((0, side_count - target_count), (0, 0))),
            jnp.pad(weight_parts, ((0, side_count - 3), (0, features - 2 * quarter))),
        ],
        axis=1,
    )
    chunks = {0: jnp.concatenate([own_rows, side_block], axis=0)}

    high_count = pool_dev // LANES
    place = block_index - my_row * pool_dev
    inside = (place >= 0) & (place < pool_dev)
    high = jnp.where(inside, place // LANES, -1)
    low = jnp.where(inside, place % LANES, 0)
    high_hot = (high[:, None, :] == jnp.arange(high_count)[None, :, None]).astype(BF16)
    low_hot = (low[:, None, :] == jnp.arange(LANES)[None, :, None]).astype(BF16)
    member = jnp.einsum("shl,sgl->shg", high_hot, low_hot, preferred_element_type=F32).astype(BF16)
    for bit in bits_of(cent_devices):
        member = member + swap(member, "cent", bit)

    for bit in reversed(bits_of(row_devices)):
        for have in sorted(chunks):
            chunks[have | bit] = swap(chunks[have], "rows", bit)

    upper = (jnp.arange(LANES)[:, None] <= jnp.arange(LANES)[None, :]).astype(BF16)
    before = (jnp.arange(high_count)[:, None] > jnp.arange(high_count)[None, :]).astype(BF16)
    running = jnp.einsum("shg,gk->shk", member, upper, preferred_element_type=F32)
    row_count = running[:, :, -1:]
    row_start = jnp.einsum("hi,sik->shk", before, row_count.astype(BF16), preferred_element_type=F32)
    rank = row_start + running - 1.0
    dest = jnp.where(member > 0, rank, -65536.0).astype(jnp.int32)
    group_rows = POOL_BLOCK // LANES
    off = row_start[:, ::group_rows, 0].astype(jnp.int32)
    off = jnp.concatenate([off, jnp.full((steps, 1), per_step, jnp.int32)], axis=1)

    coef_parts = jnp.concatenate(split3_outside(coefs), axis=0)
    side = jnp.pad(coef_parts, ((0, LANES - 3 * target_count), (0, 0))).T
    chosen, _, norm, own_coef = compact(off, dest, centres, side, per_step, target_count)

    state = None
    for have in sorted(chunks, key=lambda c: (bin(c).count("1"), c)):
        slot = (my_row ^ have).astype(jnp.int32)[None]
        k_all, sums, info = block_call(
            slot, chunks[have], chosen, norm, state, per_step, target_count, row_devices, sharpness, offset
        )
        state = (k_all, sums, info)

    squares = lax.all_gather(sums, "cent")
    gathered = squares
    total_change = None
    coef_now = coefs
    weight_row = info[target_count].reshape(row_devices, 1, quarter)
    moved = None
    for step in range(steps):
        if step > 0:
            share = change * weight_row
            if step > 1:
                share = share - last_change * weight_row
            for bit in bits_of(row_devices):
                share = share + swap(share.astype(BF16), "rows", bit).astype(F32)
            moved = share if moved is None else moved + share
            gradient = gradient_call(moved, info, k_all, step, target_count, per_step)
            gathered = lax.all_gather(gradient, "cent")
        last_change = total_change
        delta, change = change_call(
            gathered, squares, own_coef, k_all, step, target_count, total_change
        )
        total_change = change
        coef_now = scatter_call(off, dest, delta, coef_now, step)

    arrived = lax.all_to_all(total_change, "rows", 0, 0)
    own_change = jnp.sum(arrived, axis=0)
    full = lax.all_gather(own_change, "cent")
    full = full.transpose(1, 0, 2).reshape(target_count, rows_dev)
    return (coef_now, predictions + full)


def solution(mesh):
    in_specs = (
        P("rows", None),
        P("rows"),
        P(None, "rows"),
        P(None, "rows"),
        P("rows", None),
        P(None, "rows"),
        P(None, "cent"),
    )
    out_specs = (P(None, "rows"), P(None, "rows"))
    return jax.shard_map(local, mesh=mesh, in_specs=in_specs, out_specs=out_specs, check_vma=False)
```

```python
import functools
import math

import jax
import jax.numpy as jnp
from jax import lax
from jax.experimental import pallas as pl
from jax.experimental.pallas import tpu as pltpu
from jax.sharding import PartitionSpec as P

RIDGE = 1.0
LANES = 128
POOL_BLOCK = 256
WINDOW = 144
KERNEL_VMEM = 16 * 2**20
LOG2E = math.log2(math.e)
NT = (((1,), (1,)), ((), ()))
F32 = jnp.float32
BF16 = jnp.bfloat16


def split3(x):
    first = x.astype(BF16)
    rest = x - first.astype(F32)
    second = rest.astype(BF16)
    third = (rest - second.astype(F32)).astype(BF16)
    return first, second, third


def split3_outside(x):
    first = lax.reduce_precision(x, 8, 7)
    rest = x - first
    second = lax.reduce_precision(rest, 8, 7)
    third = rest - second
    return first.astype(BF16), second.astype(BF16), third.astype(BF16)


def round_up(value, multiple):
    return -(-value // multiple) * multiple


def in_vmem(count):
    return [pl.BlockSpec(memory_space=pltpu.VMEM)] * count


def params():
    return pltpu.CompilerParams(vmem_limit_bytes=KERNEL_VMEM)


def two_rows(ref, step, block):
    row = 2 * block
    return jnp.concatenate([ref[step, pl.ds(row, 1), :], ref[step, pl.ds(row + 1, 1), :]], axis=1)


def compact_kernel(per_step, targets, off_ref, dest_ref, pool_ref, side_ref, out_ref, norm_ref, coef_ref, side_out):
    steps, features = out_ref.shape[0], out_ref.shape[2]
    blocks = pool_ref.shape[0] // POOL_BLOCK
    tile = math.gcd(per_step, 512)

    def place(block, step, window):
        base = pl.multiple_of((off_ref[step, block] // 16) * 16, 16)
        dest = two_rows(dest_ref, step, block) - base
        slots = lax.broadcasted_iota(jnp.int32, (window, POOL_BLOCK), 0)
        pick = jnp.where(slots == dest, 1.0, 0.0).astype(BF16)
        at = pl.ds(pl.multiple_of(block * POOL_BLOCK, POOL_BLOCK), POOL_BLOCK)
        for source, target in ((pool_ref, out_ref), (side_ref, side_out)):
            rows = jnp.dot(pick, source[at, :], preferred_element_type=F32).astype(BF16)
            target[step, pl.ds(base, 16), :] += rows[:16]
            target[step, pl.ds(pl.multiple_of(base + 16, 16), window - 16), :] = rows[16:]

    for step in range(steps):
        out_ref[step, :16, :] = jnp.zeros((16, features), BF16)
        side_out[step, :16, :] = jnp.zeros((16, LANES), BF16)

    narrow = off_ref[0, blocks + 1] <= WINDOW

    @pl.when(narrow)
    def _():
        @pl.loop(0, blocks // 2)
        def _(pair):
            for i in range(2):
                for step in range(steps):
                    place(2 * pair + i, step, WINDOW)

    @pl.when(jnp.logical_not(narrow))
    def _():
        @pl.loop(0, blocks)
        def _(block):
            for step in range(steps):
                place(block, step, POOL_BLOCK + 16)

    ones = jnp.ones((8, features), BF16)
    eye = lax.broadcasted_iota(jnp.int32, (3 * targets, LANES), 0) == lax.broadcasted_iota(
        jnp.int32, (3 * targets, LANES), 1
    )
    eye = jnp.where(eye, 1.0, 0.0).astype(BF16)
    for step in range(steps):
        for first in range(0, per_step, tile):
            rows = out_ref[step, first : first + tile, :].astype(F32)
            square = rows * rows
            high = square.astype(BF16)
            low = (square - high.astype(F32)).astype(BF16)
            norm = lax.dot_general(ones, high, NT, preferred_element_type=F32)
            norm = norm + lax.dot_general(ones, low, NT, preferred_element_type=F32)
            norm_ref[step, :, first : first + tile] = norm
            side = side_out[step, first : first + tile, :]
            parts = lax.dot_general(eye, side, NT, preferred_element_type=F32)
            coef_ref[step, :, first : first + tile] = (
                parts[:targets] + parts[targets : 2 * targets] + parts[2 * targets :]
            )


def compact(off, dest, pool, side, per_step, targets):
    steps = dest.shape[0]
    features = pool.shape[1]
    length = round_up(per_step, 16) + POOL_BLOCK + 16
    return pl.pallas_call(
        functools.partial(compact_kernel, per_step, targets),
        name="compact",
        in_specs=[pl.BlockSpec(memory_space=pltpu.SMEM)] + in_vmem(3),
        out_specs=in_vmem(3),
        out_shape=(
            pltpu.VMEM((steps, length, features), BF16),
            pltpu.VMEM((steps, 8, per_step), F32),
            pltpu.VMEM((steps, targets, per_step), F32),
        ),
        scratch_shapes=[pltpu.VMEM((steps, length, LANES), BF16)],
        compiler_params=params(),
        cost_estimate=pl.CostEstimate(flops=4 * 10**9, bytes_accessed=8 * 10**6, transcendentals=0),
    )(off, dest, pool, side)


def block_kernel(per_step, targets, quarter, scale, offset, slot_ref, rows_ref, chosen_ref, norm_ref, *refs):
    k_ref, sums_ref, side_ref = refs[-3:]
    sums_in = refs[1] if len(refs) > 3 else None
    steps = chosen_ref.shape[0]
    tile = math.gcd(per_step, 512)
    slot = slot_ref[0]

    rows = rows_ref[:quarter, :]
    wide_rows = rows.astype(F32)
    row_norm = jnp.sum(wide_rows * wide_rows, axis=1, keepdims=True) * (scale * LOG2E) - offset * LOG2E
    parts = rows_ref[quarter : quarter + 3, quarter : 2 * quarter].astype(F32)
    weight = jnp.sum(parts, axis=0, keepdims=True)
    weight_column = jnp.transpose(jnp.broadcast_to(weight, (8, quarter)))[:, :1]
    weighted = rows_ref[quarter : quarter + targets, :quarter]
    side_ref[slot, :targets, :] = weighted.astype(F32)
    side_ref[slot, targets:, :] = jnp.broadcast_to(weight, (side_ref.shape[1] - targets, quarter))

    for first in range(0, per_step, tile):
        for step in range(steps):
            dots = lax.dot_general(
                rows, chosen_ref[step, first : first + tile, :], NT, preferred_element_type=F32
            )
            centre = norm_ref[step, :1, first : first + tile] * (scale * LOG2E)
            k_low = jnp.exp2(dots * (2.0 * scale * LOG2E) - row_norm - centre).astype(BF16)
            k_ref[slot, :, step * per_step + first : step * per_step + first + tile] = k_low
            wide = k_low.astype(F32)
            updates = [(targets + step, 1, jnp.sum(weight_column * (wide * wide), axis=0, keepdims=True))]
            if step == 0:
                updates.append((0, targets, jnp.dot(weighted, k_low, preferred_element_type=F32)))
            for row, count, value in updates:
                if sums_in is not None:
                    value = value + sums_in[row : row + count, first : first + tile]
                sums_ref[row : row + count, first : first + tile] = value


def block_call(slot, rows, chosen, norm, state, per_step, targets, row_devices, scale, offset):
    steps, _, features = chosen.shape
    quarter = rows.shape[0] - round_up(targets, 16)
    operands = [slot, rows, chosen, norm]
    aliases = {}
    if state is not None:
        operands += [pltpu.with_memory_space_constraint(x, pltpu.VMEM) for x in state]
        aliases = {4: 0, 5: 1, 6: 2}
    entries = quarter * per_step * steps
    return pl.pallas_call(
        functools.partial(block_kernel, per_step, targets, quarter, scale, offset),
        name="kernel_block",
        in_specs=[pl.BlockSpec(memory_space=pltpu.SMEM)] + in_vmem(len(operands) - 1),
        out_specs=in_vmem(3),
        out_shape=(
            pltpu.VMEM((row_devices, quarter, steps * per_step), BF16),
            pltpu.VMEM((round_up(targets + steps, 8), per_step), F32),
            pltpu.VMEM((row_devices, round_up(targets + 1, 8), quarter), F32),
        ),
        input_output_aliases=aliases,
        compiler_params=params(),
        cost_estimate=pl.CostEstimate(
            flops=2 * entries * features, bytes_accessed=2 * entries, transcendentals=entries
        ),
    )(*operands)


def pass_cost(k_all, per_step, targets):
    entries = k_all.shape[0] * k_all.shape[1] * per_step
    return pl.CostEstimate(flops=2 * targets * entries, bytes_accessed=2 * entries, transcendentals=0)


def change_kernel(targets, step, sums_ref, square_ref, coef_ref, k_ref, side_ref, *refs):
    before_ref = refs[0] if len(refs) == 4 else None
    delta_ref, change_ref, moved_ref = refs[-3:]
    per_step = delta_ref.shape[1]
    total, square = sums_ref[0, :targets, :], square_ref[0, targets + step : targets + step + 1, :]
    for i in range(1, sums_ref.shape[0]):
        total = total + sums_ref[i, :targets, :]
        square = square + square_ref[i, targets + step : targets + step + 1, :]
    delta = (total - RIDGE * coef_ref[step]) / (square + RIDGE)
    delta_ref[...] = delta
    low = delta.astype(BF16)

    def body(i, _):
        k_low = k_ref[i, :, step * per_step : (step + 1) * per_step]
        change = lax.dot_general(low, k_low, NT, preferred_element_type=F32)
        moved_ref[i] = change * side_ref[i, targets : targets + 1, :]
        change_ref[i] = change if before_ref is None else change + before_ref[i]
        return 0

    lax.fori_loop(0, k_ref.shape[0], body, 0, unroll=2)


def change_call(sums, squares, coef, k_all, side, step, targets, before=None):
    row_devices, quarter, _ = k_all.shape
    per_step = sums.shape[2]
    operands = [sums, squares, coef, pltpu.with_memory_space_constraint(k_all, pltpu.VMEM), side]
    if before is not None:
        operands.append(before)
    change = jax.ShapeDtypeStruct((row_devices, targets, quarter), F32)
    return pl.pallas_call(
        functools.partial(change_kernel, targets, step),
        name="change",
        in_specs=in_vmem(len(operands)),
        out_specs=in_vmem(3),
        out_shape=(jax.ShapeDtypeStruct((targets, per_step), F32), change, change),
        compiler_params=params(),
        cost_estimate=pass_cost(k_all, per_step, targets),
    )(*operands)


def gradient_kernel(targets, step, moved_ref, side_ref, k_ref, out_ref):
    per_step = out_ref.shape[1]
    out_ref[...] = jnp.zeros_like(out_ref)

    def body(i, _):
        weighted = (side_ref[i, :targets, :] - moved_ref[i]).astype(BF16)
        k_low = k_ref[i, :, step * per_step : (step + 1) * per_step]
        out_ref[...] += jnp.dot(weighted, k_low, preferred_element_type=F32)
        return 0

    lax.fori_loop(0, k_ref.shape[0], body, 0, unroll=2)


def gradient_call(moved, side, k_all, step, targets, per_step):
    return pl.pallas_call(
        functools.partial(gradient_kernel, targets, step),
        name="gradient",
        in_specs=in_vmem(3),
        out_specs=in_vmem(1)[0],
        out_shape=jax.ShapeDtypeStruct((targets, per_step), F32),
        compiler_params=params(),
        cost_estimate=pass_cost(k_all, per_step, targets),
    )(moved, side, pltpu.with_memory_space_constraint(k_all, pltpu.VMEM))


def scatter_kernel(targets, off_ref, dest_ref, coef_ref, *refs):
    delta_refs, (out_ref, parts_ref) = refs[:-2], refs[-2:]
    steps = len(delta_refs)
    per_step = delta_refs[0].shape[1]
    blocks = out_ref.shape[1] // POOL_BLOCK
    window = POOL_BLOCK + LANES
    for step in range(steps):
        for part, value in enumerate(split3(delta_refs[step][...])):
            parts_ref[step, part * targets : (part + 1) * targets, :per_step] = value
        parts_ref[step, :, per_step:] = jnp.zeros((3 * targets, parts_ref.shape[2] - per_step), BF16)

    @pl.loop(0, blocks // 2)
    def _(pair):
        for i in range(2):
            block = 2 * pair + i
            columns = pl.ds(pl.multiple_of(block * POOL_BLOCK, POOL_BLOCK), POOL_BLOCK)
            value = coef_ref[:, columns]
            for step in range(steps):
                base = pl.multiple_of((off_ref[step, block] // LANES) * LANES, LANES)
                dest = two_rows(dest_ref, step, block) - base
                slots = lax.broadcasted_iota(jnp.int32, (window, POOL_BLOCK), 0)
                pick = jnp.where(slots == dest, 1.0, 0.0).astype(BF16)
                moved = jnp.dot(parts_ref[step, :, pl.ds(base, window)], pick, preferred_element_type=F32)
                value = value + (moved[:targets] + moved[targets : 2 * targets] + moved[2 * targets :])
            out_ref[:, columns] = value


def scatter_call(off, dest, coefs, deltas):
    targets, per_step = deltas[0].shape
    length = round_up(per_step, LANES) + POOL_BLOCK + LANES
    return pl.pallas_call(
        functools.partial(scatter_kernel, targets),
        name="scatter",
        in_specs=[pl.BlockSpec(memory_space=pltpu.SMEM)] + in_vmem(2 + len(deltas)),
        out_specs=in_vmem(1)[0],
        out_shape=jax.ShapeDtypeStruct(coefs.shape, F32),
        scratch_shapes=[pltpu.VMEM((len(deltas), 3 * targets, length), BF16)],
        compiler_params=params(),
        cost_estimate=pl.CostEstimate(flops=10**9, bytes_accessed=10**6, transcendentals=0),
    )(off, dest, coefs, *deltas)


def swap(value, axis, bit):
    count = lax.axis_size(axis)
    return lax.ppermute(value, axis, [(i, i ^ bit) for i in range(count)])


def bits_of(count):
    return [1 << k for k in range(count.bit_length() - 1)]


def local(samples, weights, targets, predictions, centres, coefs, block_index):
    rows_dev, features = samples.shape
    pool_dev = centres.shape[0]
    steps, slice_len = block_index.shape
    target_count = targets.shape[0]
    row_devices, cent_devices = lax.axis_size("rows"), lax.axis_size("cent")
    my_row, my_cent = lax.axis_index("rows"), lax.axis_index("cent")
    quarter = rows_dev // cent_devices
    per_step = slice_len * cent_devices // row_devices
    sharpness = 1.3 / math.sqrt(8.0 * features)
    offset = 2.0 * features * sharpness - 1.5 - 0.5 * math.log(rows_dev * row_devices)

    at = my_cent * quarter
    own_rows = lax.dynamic_slice_in_dim(samples, at, quarter, 0)
    own_weight = lax.dynamic_slice_in_dim(weights, at, quarter, 0)[None, :]
    own_target = lax.dynamic_slice_in_dim(targets, at, quarter, 1)
    own_pred = lax.dynamic_slice_in_dim(predictions, at, quarter, 1)
    weighted = (own_weight * (own_target - own_pred)).astype(BF16)
    side_count = round_up(target_count, 16)
    weight_parts = jnp.concatenate(split3_outside(own_weight), axis=0)
    side_block = jnp.concatenate(
        [
            jnp.pad(weighted, ((0, side_count - target_count), (0, 0))),
            jnp.pad(weight_parts, ((0, side_count - 3), (0, features - 2 * quarter))),
        ],
        axis=1,
    )
    chunks = {0: jnp.concatenate([own_rows, side_block], axis=0)}

    high_count = pool_dev // LANES
    place = block_index - my_row * pool_dev
    inside = (place >= 0) & (place < pool_dev)
    high = jnp.where(inside, place // LANES, -1)
    low = jnp.where(inside, place % LANES, 0)
    high_hot = (high[:, None, :] == jnp.arange(high_count)[None, :, None]).astype(BF16)
    low_hot = (low[:, None, :] == jnp.arange(LANES)[None, :, None]).astype(BF16)
    member = jnp.einsum("shl,sgl->shg", high_hot, low_hot, preferred_element_type=F32).astype(BF16)
    for bit in bits_of(cent_devices):
        member = member + swap(member, "cent", bit)

    for bit in reversed(bits_of(row_devices)):
        for have in sorted(chunks):
            chunks[have | bit] = swap(chunks[have], "rows", bit)

    upper = (jnp.arange(LANES)[:, None] <= jnp.arange(LANES)[None, :]).astype(BF16)
    before = (jnp.arange(high_count)[:, None] > jnp.arange(high_count)[None, :]).astype(BF16)
    running = jnp.einsum("shg,gk->shk", member, upper, preferred_element_type=F32)
    row_count = running[:, :, -1:]
    row_start = jnp.einsum("hi,sik->shk", before, row_count.astype(BF16), preferred_element_type=F32)
    rank = row_start + running - 1.0
    dest = jnp.where(member > 0, rank, -65536.0).astype(jnp.int32)
    group_rows = POOL_BLOCK // LANES
    off = row_start[:, ::group_rows, 0].astype(jnp.int32)
    end = jnp.concatenate([off[:, 1:], jnp.full((steps, 1), per_step, jnp.int32)], axis=1)
    widest = jnp.broadcast_to(jnp.max(end - off // 16 * 16), (steps, 1))
    off = jnp.concatenate([off, end[:, -1:], widest], axis=1)

    coef_parts = jnp.concatenate(split3_outside(coefs), axis=0)
    side = jnp.pad(coef_parts, ((0, LANES - 3 * target_count), (0, 0))).T
    chosen, norm, own_coef = compact(off, dest, centres, side, per_step, target_count)

    state = None
    for have in sorted(chunks, key=lambda c: (bin(c).count("1"), c)):
        slot = (my_row ^ have).astype(jnp.int32)[None]
        k_all, sums, info = block_call(
            slot, chunks[have], chosen, norm, state, per_step, target_count, row_devices, sharpness, offset
        )
        state = (k_all, sums, info)

    squares = lax.all_gather(sums, "cent")
    gathered = squares
    total_change = None
    deltas = []
    for step in range(steps):
        if step > 0:
            for bit in bits_of(row_devices):
                share = share + swap(share.astype(BF16), "rows", bit).astype(F32)
            moved = share if step == 1 else moved + share
            gradient = gradient_call(moved, info, k_all, step, target_count, per_step)
            gathered = lax.all_gather(gradient, "cent")
        delta, total_change, share = change_call(
            gathered, squares, own_coef, k_all, info, step, target_count, total_change
        )
        deltas.append(delta)
    coef_now = scatter_call(off, dest, coefs, deltas)

    arrived = lax.all_to_all(total_change, "rows", 0, 0)
    own_change = jnp.sum(arrived, axis=0)
    full = lax.all_gather(own_change, "cent")
    full = full.transpose(1, 0, 2).reshape(target_count, rows_dev)
    return (coef_now, predictions + full)


def solution(mesh):
    in_specs = (
        P("rows", None),
        P("rows"),
        P(None, "rows"),
        P(None, "rows"),
        P("rows", None),
        P(None, "rows"),
        P(None, "cent"),
    )
    out_specs = (P(None, "rows"), P(None, "rows"))
    return jax.shard_map(local, mesh=mesh, in_specs=in_specs, out_specs=out_specs, check_vma=False)
```

```python
import functools
import math

import jax
import jax.numpy as jnp
from jax import lax
from jax.experimental import pallas as pl
from jax.experimental.pallas import tpu as pltpu
from jax.sharding import PartitionSpec as P

RIDGE = 1.0
LANES = 128
POOL_BLOCK = 256
WINDOW = 144
KERNEL_VMEM = 16 * 2**20
LOG2E = math.log2(math.e)
NT = (((1,), (1,)), ((), ()))
F32 = jnp.float32
BF16 = jnp.bfloat16


def split3(x):
    first = x.astype(BF16)
    rest = x - first.astype(F32)
    second = rest.astype(BF16)
    third = (rest - second.astype(F32)).astype(BF16)
    return first, second, third


def split3_outside(x):
    first = lax.reduce_precision(x, 8, 7)
    rest = x - first
    second = lax.reduce_precision(rest, 8, 7)
    third = rest - second
    return first.astype(BF16), second.astype(BF16), third.astype(BF16)


def round_up(value, multiple):
    return -(-value // multiple) * multiple


def in_vmem(count):
    return [pl.BlockSpec(memory_space=pltpu.VMEM)] * count


def params():
    return pltpu.CompilerParams(vmem_limit_bytes=KERNEL_VMEM)


def two_rows(ref, step, block):
    row = 2 * block
    return jnp.concatenate([ref[step, pl.ds(row, 1), :], ref[step, pl.ds(row + 1, 1), :]], axis=1)


def compact_kernel(per_step, targets, off_ref, dest_ref, pool_hbm, coefs_ref, out_ref, norm_ref, coef_ref, side_out, pool_ref, parts_ref, arrived):
    steps, features = out_ref.shape[0], out_ref.shape[2]
    blocks = pool_ref.shape[0] // POOL_BLOCK
    tile = math.gcd(per_step, 512)

    def fetch(block):
        at = pl.ds(pl.multiple_of(block * POOL_BLOCK, POOL_BLOCK), POOL_BLOCK)
        return pltpu.make_async_copy(pool_hbm.at[at, :], pool_ref.at[at, :], arrived.at[block])

    for block in range(blocks):
        fetch(block).start()
    parts_ref[3 * targets :, :] = jnp.zeros((LANES - 3 * targets, parts_ref.shape[1]), BF16)
    for part, value in enumerate(split3(coefs_ref[...])):
        parts_ref[part * targets : (part + 1) * targets, :] = value

    def place(block, step, window):
        base = pl.multiple_of((off_ref[step, block] // 16) * 16, 16)
        dest = two_rows(dest_ref, step, block) - base
        slots = lax.broadcasted_iota(jnp.int32, (window, POOL_BLOCK), 0)
        pick = jnp.where(slots == dest, 1.0, 0.0).astype(BF16)
        at = pl.ds(pl.multiple_of(block * POOL_BLOCK, POOL_BLOCK), POOL_BLOCK)
        packed = jnp.dot(pick, pool_ref[at, :], preferred_element_type=F32)
        side = lax.dot_general(pick, parts_ref[:, at], NT, preferred_element_type=F32)
        for rows, target in ((packed.astype(BF16), out_ref), (side.astype(BF16), side_out)):
            target[step, pl.ds(base, 16), :] += rows[:16]
            target[step, pl.ds(pl.multiple_of(base + 16, 16), window - 16), :] = rows[16:]

    for step in range(steps):
        out_ref[step, :16, :] = jnp.zeros((16, features), BF16)
        side_out[step, :16, :] = jnp.zeros((16, LANES), BF16)

    widest = 0
    for step in range(steps):
        for block in range(blocks):
            widest = jnp.maximum(widest, off_ref[step, block + 1] - (off_ref[step, block] // 16) * 16)
    narrow = widest <= WINDOW

    @pl.when(narrow)
    def _():
        @pl.loop(0, blocks // 2)
        def _(pair):
            for i in range(2):
                fetch(2 * pair + i).wait()
            for i in range(2):
                for step in range(steps):
                    place(2 * pair + i, step, WINDOW)

    @pl.when(jnp.logical_not(narrow))
    def _():
        @pl.loop(0, blocks)
        def _(block):
            fetch(block).wait()
            for step in range(steps):
                place(block, step, POOL_BLOCK + 16)

    ones = jnp.ones((8, features), BF16)
    eye = lax.broadcasted_iota(jnp.int32, (3 * targets, LANES), 0) == lax.broadcasted_iota(
        jnp.int32, (3 * targets, LANES), 1
    )
    eye = jnp.where(eye, 1.0, 0.0).astype(BF16)
    for step in range(steps):
        for first in range(0, per_step, tile):
            rows = out_ref[step, first : first + tile, :].astype(F32)
            square = rows * rows
            high = square.astype(BF16)
            low = (square - high.astype(F32)).astype(BF16)
            norm = lax.dot_general(ones, high, NT, preferred_element_type=F32)
            norm = norm + lax.dot_general(ones, low, NT, preferred_element_type=F32)
            norm_ref[step, :, first : first + tile] = norm
            side = side_out[step, first : first + tile, :]
            parts = lax.dot_general(eye, side, NT, preferred_element_type=F32)
            coef_ref[step, :, first : first + tile] = (
                parts[:targets] + parts[targets : 2 * targets] + parts[2 * targets :]
            )


def compact(off, dest, pool, coefs, per_step, targets):
    steps = dest.shape[0]
    features = pool.shape[1]
    length = round_up(per_step, 16) + POOL_BLOCK + 16
    return pl.pallas_call(
        functools.partial(compact_kernel, per_step, targets),
        name="compact",
        in_specs=[
            pl.BlockSpec(memory_space=pltpu.SMEM),
            *in_vmem(1),
            pl.BlockSpec(memory_space=pl.ANY),
            *in_vmem(1),
        ],
        out_specs=in_vmem(3),
        out_shape=(
            pltpu.VMEM((steps, length, features), BF16),
            pltpu.VMEM((steps, 8, per_step), F32),
            pltpu.VMEM((steps, targets, per_step), F32),
        ),
        scratch_shapes=[
            pltpu.VMEM((steps, length, LANES), BF16),
            pltpu.VMEM(pool.shape, BF16),
            pltpu.VMEM((LANES, pool.shape[0]), BF16),
            pltpu.SemaphoreType.DMA((pool.shape[0] // POOL_BLOCK,)),
        ],
        compiler_params=params(),
        cost_estimate=pl.CostEstimate(flops=4 * 10**9, bytes_accessed=8 * 10**6, transcendentals=0),
    )(off, dest, pool, coefs)


def block_kernel(per_step, targets, quarter, scale, offset, slot_ref, rows_ref, chosen_ref, norm_ref, *refs):
    k_ref, sums_ref, side_ref = refs[-3:]
    sums_in = refs[1] if len(refs) > 3 else None
    steps = chosen_ref.shape[0]
    tile = math.gcd(per_step, 512)
    slot = slot_ref[0]

    rows = rows_ref[:quarter, :]
    wide_rows = rows.astype(F32)
    row_norm = jnp.sum(wide_rows * wide_rows, axis=1, keepdims=True) * (scale * LOG2E) - offset * LOG2E
    parts = rows_ref[quarter : quarter + 3, quarter : 2 * quarter].astype(F32)
    weight = jnp.sum(parts, axis=0, keepdims=True)
    weight_column = jnp.transpose(jnp.broadcast_to(weight, (8, quarter)))[:, :1]
    weighted = rows_ref[quarter : quarter + targets, :quarter]
    side_ref[slot, :targets, :] = weighted.astype(F32)
    side_ref[slot, targets:, :] = jnp.broadcast_to(weight, (side_ref.shape[1] - targets, quarter))

    for first in range(0, per_step, tile):
        for step in range(steps):
            dots = lax.dot_general(
                rows, chosen_ref[step, first : first + tile, :], NT, preferred_element_type=F32
            )
            centre = norm_ref[step, :1, first : first + tile] * (scale * LOG2E)
            k_low = jnp.exp2(dots * (2.0 * scale * LOG2E) - row_norm - centre).astype(BF16)
            k_ref[slot, :, step * per_step + first : step * per_step + first + tile] = k_low
            wide = k_low.astype(F32)
            updates = [(targets + step, 1, jnp.sum(weight_column * (wide * wide), axis=0, keepdims=True))]
            if step == 0:
                updates.append((0, targets, jnp.dot(weighted, k_low, preferred_element_type=F32)))
            for row, count, value in updates:
                if sums_in is not None:
                    value = value + sums_in[row : row + count, first : first + tile]
                sums_ref[row : row + count, first : first + tile] = value


def block_call(slot, rows, chosen, norm, state, per_step, targets, row_devices, scale, offset):
    steps, _, features = chosen.shape
    quarter = rows.shape[0] - round_up(targets, 16)
    operands = [slot, rows, chosen, norm]
    aliases = {}
    if state is not None:
        operands += [pltpu.with_memory_space_constraint(x, pltpu.VMEM) for x in state]
        aliases = {4: 0, 5: 1, 6: 2}
    entries = quarter * per_step * steps
    return pl.pallas_call(
        functools.partial(block_kernel, per_step, targets, quarter, scale, offset),
        name="kernel_block",
        in_specs=[pl.BlockSpec(memory_space=pltpu.SMEM)] + in_vmem(len(operands) - 1),
        out_specs=in_vmem(3),
        out_shape=(
            pltpu.VMEM((row_devices, quarter, steps * per_step), BF16),
            pltpu.VMEM((round_up(targets + steps, 8), per_step), F32),
            pltpu.VMEM((row_devices, round_up(targets + 1, 8), quarter), F32),
        ),
        input_output_aliases=aliases,
        compiler_params=params(),
        cost_estimate=pl.CostEstimate(
            flops=2 * entries * features, bytes_accessed=2 * entries, transcendentals=entries
        ),
    )(*operands)


def pass_cost(k_all, per_step, targets):
    entries = k_all.shape[0] * k_all.shape[1] * per_step
    return pl.CostEstimate(flops=2 * targets * entries, bytes_accessed=2 * entries, transcendentals=0)


def change_kernel(targets, step, sums_ref, square_ref, coef_ref, k_ref, side_ref, *refs):
    before_ref = refs[0] if len(refs) == 4 else None
    delta_ref, change_ref, moved_ref = refs[-3:]
    per_step = delta_ref.shape[1]
    total, square = sums_ref[0, :targets, :], square_ref[0, targets + step : targets + step + 1, :]
    for i in range(1, sums_ref.shape[0]):
        total = total + sums_ref[i, :targets, :]
        square = square + square_ref[i, targets + step : targets + step + 1, :]
    delta = (total - RIDGE * coef_ref[step]) / (square + RIDGE)
    delta_ref[...] = delta
    low = delta.astype(BF16)

    def body(i, _):
        k_low = k_ref[i, :, step * per_step : (step + 1) * per_step]
        change = lax.dot_general(low, k_low, NT, preferred_element_type=F32)
        moved_ref[i] = change * side_ref[i, targets : targets + 1, :]
        change_ref[i] = change if before_ref is None else change + before_ref[i]
        return 0

    lax.fori_loop(0, k_ref.shape[0], body, 0, unroll=2)


def change_call(sums, squares, coef, k_all, side, step, targets, before=None):
    row_devices, quarter, _ = k_all.shape
    per_step = sums.shape[2]
    operands = [sums, squares, coef, pltpu.with_memory_space_constraint(k_all, pltpu.VMEM), side]
    if before is not None:
        operands.append(before)
    change = jax.ShapeDtypeStruct((row_devices, targets, quarter), F32)
    return pl.pallas_call(
        functools.partial(change_kernel, targets, step),
        name="change",
        in_specs=in_vmem(len(operands)),
        out_specs=in_vmem(3),
        out_shape=(jax.ShapeDtypeStruct((targets, per_step), F32), change, change),
        compiler_params=params(),
        cost_estimate=pass_cost(k_all, per_step, targets),
    )(*operands)


def gradient_kernel(targets, step, moved_ref, side_ref, k_ref, out_ref):
    per_step = out_ref.shape[1]
    out_ref[...] = jnp.zeros_like(out_ref)

    def body(i, _):
        weighted = (side_ref[i, :targets, :] - moved_ref[i]).astype(BF16)
        k_low = k_ref[i, :, step * per_step : (step + 1) * per_step]
        out_ref[...] += jnp.dot(weighted, k_low, preferred_element_type=F32)
        return 0

    lax.fori_loop(0, k_ref.shape[0], body, 0, unroll=2)


def gradient_call(moved, side, k_all, step, targets, per_step):
    return pl.pallas_call(
        functools.partial(gradient_kernel, targets, step),
        name="gradient",
        in_specs=in_vmem(3),
        out_specs=in_vmem(1)[0],
        out_shape=jax.ShapeDtypeStruct((targets, per_step), F32),
        compiler_params=params(),
        cost_estimate=pass_cost(k_all, per_step, targets),
    )(moved, side, pltpu.with_memory_space_constraint(k_all, pltpu.VMEM))


def scatter_kernel(targets, step, off_ref, dest_ref, coef_ref, delta_ref, out_ref, parts_ref):
    per_step = delta_ref.shape[1]
    blocks = out_ref.shape[1] // POOL_BLOCK
    window = POOL_BLOCK + LANES
    for part, value in enumerate(split3(delta_ref[...])):
        parts_ref[part * targets : (part + 1) * targets, :per_step] = value
    parts_ref[:, per_step:] = jnp.zeros((3 * targets, parts_ref.shape[1] - per_step), BF16)

    @pl.loop(0, blocks // 4)
    def _(four):
        for i in range(4):
            block = 4 * four + i
            columns = pl.ds(pl.multiple_of(block * POOL_BLOCK, POOL_BLOCK), POOL_BLOCK)
            base = pl.multiple_of((off_ref[step, block] // LANES) * LANES, LANES)
            dest = two_rows(dest_ref, step, block) - base
            slots = lax.broadcasted_iota(jnp.int32, (window, POOL_BLOCK), 0)
            pick = jnp.where(slots == dest, 1.0, 0.0).astype(BF16)
            moved = jnp.dot(parts_ref[:, pl.ds(base, window)], pick, preferred_element_type=F32)
            moved = moved[:targets] + moved[targets : 2 * targets] + moved[2 * targets :]
            out_ref[:, columns] = coef_ref[:, columns] + moved


def scatter_call(off, dest, coefs, delta, step):
    targets, per_step = delta.shape
    length = round_up(per_step, LANES) + POOL_BLOCK + LANES
    return pl.pallas_call(
        functools.partial(scatter_kernel, targets, step),
        name="scatter",
        in_specs=[pl.BlockSpec(memory_space=pltpu.SMEM)] + in_vmem(3),
        out_specs=in_vmem(1)[0],
        out_shape=jax.ShapeDtypeStruct(coefs.shape, F32),
        scratch_shapes=[pltpu.VMEM((3 * targets, length), BF16)],
        compiler_params=params(),
        cost_estimate=pl.CostEstimate(flops=10**9, bytes_accessed=10**6, transcendentals=0),
    )(off, dest, coefs, delta)


def swap(value, axis, bit):
    count = lax.axis_size(axis)
    return lax.ppermute(value, axis, [(i, i ^ bit) for i in range(count)])


def bits_of(count):
    return [1 << k for k in range(count.bit_length() - 1)]


def local(samples, weights, targets, predictions, centres, coefs, block_index):
    rows_dev, features = samples.shape
    pool_dev = centres.shape[0]
    steps, slice_len = block_index.shape
    target_count = targets.shape[0]
    row_devices, cent_devices = lax.axis_size("rows"), lax.axis_size("cent")
    my_row, my_cent = lax.axis_index("rows"), lax.axis_index("cent")
    quarter = rows_dev // cent_devices
    per_step = slice_len * cent_devices // row_devices
    sharpness = 1.3 / math.sqrt(8.0 * features)
    offset = 2.0 * features * sharpness - 1.5 - 0.5 * math.log(rows_dev * row_devices)

    at = my_cent * quarter
    own_rows = lax.dynamic_slice_in_dim(samples, at, quarter, 0)
    own_weight = lax.dynamic_slice_in_dim(weights, at, quarter, 0)[None, :]
    own_target = lax.dynamic_slice_in_dim(targets, at, quarter, 1)
    own_pred = lax.dynamic_slice_in_dim(predictions, at, quarter, 1)
    weighted = (own_weight * (own_target - own_pred)).astype(BF16)
    side_count = round_up(target_count, 16)
    weight_parts = jnp.concatenate(split3_outside(own_weight), axis=0)
    side_block = jnp.concatenate(
        [
            jnp.pad(weighted, ((0, side_count - target_count), (0, 0))),
            jnp.pad(weight_parts, ((0, side_count - 3), (0, features - 2 * quarter))),
        ],
        axis=1,
    )
    chunks = {0: jnp.concatenate([own_rows, side_block], axis=0)}

    high_count = pool_dev // LANES
    place = block_index - my_row * pool_dev
    inside = (place >= 0) & (place < pool_dev)
    high = jnp.where(inside, place // LANES, -1)
    low = jnp.where(inside, place % LANES, 0)
    high_hot = (high[:, None, :] == jnp.arange(high_count)[None, :, None]).astype(BF16)
    low_hot = (low[:, None, :] == jnp.arange(LANES)[None, :, None]).astype(BF16)
    member = jnp.einsum("shl,sgl->shg", high_hot, low_hot, preferred_element_type=F32).astype(BF16)
    for bit in bits_of(cent_devices):
        member = member + swap(member, "cent", bit)

    for bit in reversed(bits_of(row_devices)):
        for have in sorted(chunks):
            chunks[have | bit] = swap(chunks[have], "rows", bit)

    upper = (jnp.arange(LANES)[:, None] <= jnp.arange(LANES)[None, :]).astype(BF16)
    before = (jnp.arange(high_count)[:, None] > jnp.arange(high_count)[None, :]).astype(BF16)
    running = jnp.einsum("shg,gk->shk", member, upper, preferred_element_type=F32)
    row_count = running[:, :, -1:]
    row_start = jnp.einsum("hi,sik->shk", before, row_count.astype(BF16), preferred_element_type=F32)
    rank = row_start + running - 1.0
    dest = jnp.where(member > 0, rank, -65536.0).astype(jnp.int32)
    group_rows = POOL_BLOCK // LANES
    off = row_start[:, ::group_rows, 0].astype(jnp.int32)
    off = jnp.pad(off, ((0, 0), (0, 1)), constant_values=per_step)

    chosen, norm, own_coef = compact(off, dest, centres, coefs, per_step, target_count)

    state = None
    for have in range(row_devices):
        slot = (my_row ^ have).astype(jnp.int32)[None]
        k_all, sums, info = block_call(
            slot, chunks[have], chosen, norm, state, per_step, target_count, row_devices, sharpness, offset
        )
        state = (k_all, sums, info)

    squares = lax.all_gather(sums, "cent")
    gathered = squares
    total_change = None
    coef_now = coefs
    for step in range(steps):
        if step > 0:
            bits = bits_of(row_devices)
            for first in range(0, len(bits), 2):
                low = share.astype(BF16)
                pair = bits[first : first + 2]
                for bit in pair + ([sum(pair)] if len(pair) > 1 else []):
                    share = share + swap(low, "rows", bit).astype(F32)
            moved = share if step == 1 else moved + share
            gradient = gradient_call(moved, info, k_all, step, target_count, per_step)
            gathered = lax.all_gather(gradient, "cent")
        delta, total_change, share = change_call(
            gathered, squares, own_coef, k_all, info, step, target_count, total_change
        )
        coef_now = scatter_call(off, dest, coef_now, delta, step)

    arrived = lax.all_to_all(total_change, "rows", 0, 0)
    own_change = jnp.sum(arrived, axis=0)
    full = lax.all_gather(own_change, "cent")
    full = full.transpose(1, 0, 2).reshape(target_count, rows_dev)
    return (coef_now, predictions + full)


def solution(mesh):
    in_specs = (
        P("rows", None),
        P("rows"),
        P(None, "rows"),
        P(None, "rows"),
        P("rows", None),
        P(None, "rows"),
        P(None, "cent"),
    )
    out_specs = (P(None, "rows"), P(None, "rows"))
    return jax.shard_map(local, mesh=mesh, in_specs=in_specs, out_specs=out_specs, check_vma=False)
```

```python
import functools
import math

import jax
import jax.numpy as jnp
from jax import lax
from jax.experimental import pallas as pl
from jax.experimental.pallas import tpu as pltpu
from jax.sharding import PartitionSpec as P

RIDGE = 1.0
LANES = 128
POOL_BLOCK = 256
WINDOW = 144
KERNEL_VMEM = 16 * 2**20
LOG2E = math.log2(math.e)
NT = (((1,), (1,)), ((), ()))
F32 = jnp.float32
BF16 = jnp.bfloat16


def split3(x):
    first = x.astype(BF16)
    rest = x - first.astype(F32)
    second = rest.astype(BF16)
    third = (rest - second.astype(F32)).astype(BF16)
    return first, second, third


def split3_outside(x):
    first = lax.reduce_precision(x, 8, 7)
    rest = x - first
    second = lax.reduce_precision(rest, 8, 7)
    third = rest - second
    return first.astype(BF16), second.astype(BF16), third.astype(BF16)


def round_up(value, multiple):
    return -(-value // multiple) * multiple


def in_vmem(count):
    return [pl.BlockSpec(memory_space=pltpu.VMEM)] * count


def in_hbm(x):
    return pltpu.with_memory_space_constraint(x, pltpu.HBM)


def held(x):
    return pltpu.with_memory_space_constraint(x, pltpu.VMEM)


def params():
    return pltpu.CompilerParams(vmem_limit_bytes=KERNEL_VMEM)


def two_rows(ref, step, block):
    row = 2 * block
    return jnp.concatenate([ref[step, pl.ds(row, 1), :], ref[step, pl.ds(row + 1, 1), :]], axis=1)


def compact_kernel(per_step, targets, off_ref, dest_ref, pool_hbm, coefs_hbm, out_ref, norm_ref, coef_ref, side_out, pool_ref, coefs_ref, parts_ref, arrived, coefs_arrived):
    steps, features = out_ref.shape[0], out_ref.shape[2]
    blocks = pool_ref.shape[0] // POOL_BLOCK
    tile = math.gcd(per_step, 512)

    def fetch(block):
        at = pl.ds(pl.multiple_of(block * POOL_BLOCK, POOL_BLOCK), POOL_BLOCK)
        return pltpu.make_async_copy(pool_hbm.at[at, :], pool_ref.at[at, :], arrived.at[block])

    coefs_copy = pltpu.make_async_copy(coefs_hbm, coefs_ref, coefs_arrived)
    coefs_copy.start()
    for block in range(blocks):
        fetch(block).start()
    coefs_copy.wait()
    parts_ref[3 * targets :, :] = jnp.zeros((LANES - 3 * targets, parts_ref.shape[1]), BF16)
    for part, value in enumerate(split3(coefs_ref[...])):
        parts_ref[part * targets : (part + 1) * targets, :] = value

    def place(block, step, window):
        base = pl.multiple_of((off_ref[step, block] // 16) * 16, 16)
        dest = two_rows(dest_ref, step, block) - base
        slots = lax.broadcasted_iota(jnp.int32, (window, POOL_BLOCK), 0)
        pick = jnp.where(slots == dest, 1.0, 0.0).astype(BF16)
        at = pl.ds(pl.multiple_of(block * POOL_BLOCK, POOL_BLOCK), POOL_BLOCK)
        packed = jnp.dot(pick, pool_ref[at, :], preferred_element_type=F32)
        side = lax.dot_general(pick, parts_ref[:, at], NT, preferred_element_type=F32)
        for rows, target in ((packed.astype(BF16), out_ref), (side.astype(BF16), side_out)):
            target[step, pl.ds(base, 16), :] += rows[:16]
            target[step, pl.ds(pl.multiple_of(base + 16, 16), window - 16), :] = rows[16:]

    for step in range(steps):
        out_ref[step, :16, :] = jnp.zeros((16, features), BF16)
        side_out[step, :16, :] = jnp.zeros((16, LANES), BF16)

    widest = 0
    for step in range(steps):
        for block in range(blocks):
            widest = jnp.maximum(widest, off_ref[step, block + 1] - (off_ref[step, block] // 16) * 16)
    narrow = widest <= WINDOW

    @pl.when(narrow)
    def _():
        @pl.loop(0, blocks // 2)
        def _(pair):
            for i in range(2):
                fetch(2 * pair + i).wait()
            for i in range(2):
                for step in range(steps):
                    place(2 * pair + i, step, WINDOW)

    @pl.when(jnp.logical_not(narrow))
    def _():
        @pl.loop(0, blocks)
        def _(block):
            fetch(block).wait()
            for step in range(steps):
                place(block, step, POOL_BLOCK + 16)

    ones = jnp.ones((8, features), BF16)
    eye = lax.broadcasted_iota(jnp.int32, (3 * targets, LANES), 0) == lax.broadcasted_iota(
        jnp.int32, (3 * targets, LANES), 1
    )
    eye = jnp.where(eye, 1.0, 0.0).astype(BF16)
    for step in range(steps):
        for first in range(0, per_step, tile):
            rows = out_ref[step, first : first + tile, :].astype(F32)
            square = rows * rows
            high = square.astype(BF16)
            low = (square - high.astype(F32)).astype(BF16)
            norm = lax.dot_general(ones, high, NT, preferred_element_type=F32)
            norm = norm + lax.dot_general(ones, low, NT, preferred_element_type=F32)
            norm_ref[step, :, first : first + tile] = norm
            side = side_out[step, first : first + tile, :]
            parts = lax.dot_general(eye, side, NT, preferred_element_type=F32)
            coef_ref[step, :, first : first + tile] = (
                parts[:targets] + parts[targets : 2 * targets] + parts[2 * targets :]
            )


def compact(off, dest, pool, coefs, per_step, targets):
    steps = dest.shape[0]
    features = pool.shape[1]
    length = round_up(per_step, 16) + POOL_BLOCK + 16
    return pl.pallas_call(
        functools.partial(compact_kernel, per_step, targets),
        name="compact",
        in_specs=[
            pl.BlockSpec(memory_space=pltpu.SMEM),
            *in_vmem(1),
            pl.BlockSpec(memory_space=pltpu.HBM),
            pl.BlockSpec(memory_space=pltpu.HBM),
        ],
        out_specs=in_vmem(3),
        out_shape=(
            pltpu.VMEM((steps, length, features), BF16),
            pltpu.VMEM((steps, 8, per_step), F32),
            pltpu.VMEM((steps, targets, per_step), F32),
        ),
        scratch_shapes=[
            pltpu.VMEM((steps, length, LANES), BF16),
            pltpu.VMEM(pool.shape, BF16),
            pltpu.VMEM(coefs.shape, F32),
            pltpu.VMEM((LANES, pool.shape[0]), BF16),
            pltpu.SemaphoreType.DMA((pool.shape[0] // POOL_BLOCK,)),
            pltpu.SemaphoreType.DMA,
        ],
        compiler_params=params(),
        cost_estimate=pl.CostEstimate(flops=4 * 10**9, bytes_accessed=8 * 10**6, transcendentals=0),
    )(off, dest, in_hbm(pool), in_hbm(coefs))


def block_kernel(per_step, targets, quarter, scale, offset, slot_ref, rows_ref, chosen_ref, norm_ref, *refs):
    k_ref, sums_ref, side_ref = refs[-3:]
    sums_in = refs[1] if len(refs) > 3 else None
    steps = chosen_ref.shape[0]
    tile = math.gcd(per_step, 512)
    slot = slot_ref[0]

    rows = rows_ref[:quarter, :]
    wide_rows = rows.astype(F32)
    row_norm = jnp.sum(wide_rows * wide_rows, axis=1, keepdims=True) * (scale * LOG2E) - offset * LOG2E
    parts = rows_ref[quarter : quarter + 3, quarter : 2 * quarter].astype(F32)
    weight = jnp.sum(parts, axis=0, keepdims=True)
    weight_column = jnp.transpose(jnp.broadcast_to(weight, (8, quarter)))[:, :1]
    weighted = rows_ref[quarter : quarter + targets, :quarter]
    side_ref[slot, :targets, :] = weighted.astype(F32)
    side_ref[slot, targets:, :] = jnp.broadcast_to(weight, (side_ref.shape[1] - targets, quarter))

    for first in range(0, per_step, tile):
        for step in range(steps):
            dots = lax.dot_general(
                rows, chosen_ref[step, first : first + tile, :], NT, preferred_element_type=F32
            )
            centre = norm_ref[step, :1, first : first + tile] * (scale * LOG2E)
            k_low = jnp.exp2(dots * (2.0 * scale * LOG2E) - row_norm - centre).astype(BF16)
            k_ref[slot, :, step * per_step + first : step * per_step + first + tile] = k_low
            wide = k_low.astype(F32)
            updates = [(targets + step, 1, jnp.sum(weight_column * (wide * wide), axis=0, keepdims=True))]
            if step == 0:
                updates.append((0, targets, jnp.dot(weighted, k_low, preferred_element_type=F32)))
            for row, count, value in updates:
                if sums_in is not None:
                    value = value + sums_in[row : row + count, first : first + tile]
                sums_ref[row : row + count, first : first + tile] = value


def block_call(slot, rows, chosen, norm, state, per_step, targets, row_devices, scale, offset):
    steps, _, features = chosen.shape
    quarter = rows.shape[0] - round_up(targets, 16)
    operands = [slot, rows, held(chosen), held(norm)]
    aliases = {}
    if state is not None:
        operands += [held(x) for x in state]
        aliases = {4: 0, 5: 1, 6: 2}
    entries = quarter * per_step * steps
    return pl.pallas_call(
        functools.partial(block_kernel, per_step, targets, quarter, scale, offset),
        name="kernel_block",
        in_specs=[pl.BlockSpec(memory_space=pltpu.SMEM)] + in_vmem(len(operands) - 1),
        out_specs=in_vmem(3),
        out_shape=(
            pltpu.VMEM((row_devices, quarter, steps * per_step), BF16),
            pltpu.VMEM((round_up(targets + steps, 8), per_step), F32),
            pltpu.VMEM((row_devices, round_up(targets + 1, 8), quarter), F32),
        ),
        input_output_aliases=aliases,
        compiler_params=params(),
        cost_estimate=pl.CostEstimate(
            flops=2 * entries * features, bytes_accessed=2 * entries, transcendentals=entries
        ),
    )(*operands)


def pass_cost(k_all, per_step, targets):
    entries = k_all.shape[0] * k_all.shape[1] * per_step
    return pl.CostEstimate(flops=2 * targets * entries, bytes_accessed=2 * entries, transcendentals=0)


def change_kernel(targets, step, first, last, me_ref, sums_ref, square_ref, coef_ref, k_ref, side_ref, *refs):
    before_ref = None if first else refs[0]
    outs = list(refs if first else refs[1:])
    delta_ref, change_ref = outs[:2]
    per_step = delta_ref.shape[1]
    total, square = sums_ref[0, :targets, :], square_ref[0, targets + step : targets + step + 1, :]
    for i in range(1, sums_ref.shape[0]):
        total = total + sums_ref[i, :targets, :]
        square = square + square_ref[i, targets + step : targets + step + 1, :]
    delta = (total - RIDGE * coef_ref[step]) / (square + RIDGE)
    delta_ref[...] = delta
    low = delta.astype(BF16)

    def body(i, _):
        k_low = k_ref[i, :, step * per_step : (step + 1) * per_step]
        change = lax.dot_general(low, k_low, NT, preferred_element_type=F32)
        relative = i ^ me_ref[0]
        if not last:
            outs[2][i] = change * side_ref[i, targets : targets + 1, :]
        change_ref[relative] = change if first else change + before_ref[relative]
        return 0

    lax.fori_loop(0, k_ref.shape[0], body, 0, unroll=2)


def change_call(me, sums, squares, coef, k_all, side, step, steps, targets, before=None):
    row_devices, quarter, _ = k_all.shape
    per_step = sums.shape[2]
    last = step == steps - 1
    operands = [me, sums, squares, coef, held(k_all), side]
    if before is not None:
        operands.append(before)
    change = jax.ShapeDtypeStruct((row_devices, targets, quarter), F32)
    outs = (jax.ShapeDtypeStruct((targets, per_step), F32), change) + (() if last else (change,))
    return pl.pallas_call(
        functools.partial(change_kernel, targets, step, before is None, last),
        name="change",
        in_specs=[pl.BlockSpec(memory_space=pltpu.SMEM)] + in_vmem(len(operands) - 1),
        out_specs=in_vmem(len(outs)),
        out_shape=outs,
        compiler_params=params(),
        cost_estimate=pass_cost(k_all, per_step, targets),
    )(*operands)


def gradient_kernel(targets, step, moved_ref, side_ref, k_ref, out_ref):
    per_step = out_ref.shape[1]
    out_ref[...] = jnp.zeros_like(out_ref)

    def body(i, _):
        weighted = (side_ref[i, :targets, :] - moved_ref[i]).astype(BF16)
        k_low = k_ref[i, :, step * per_step : (step + 1) * per_step]
        out_ref[...] += jnp.dot(weighted, k_low, preferred_element_type=F32)
        return 0

    lax.fori_loop(0, k_ref.shape[0], body, 0, unroll=2)


def gradient_call(moved, side, k_all, step, targets, per_step):
    return pl.pallas_call(
        functools.partial(gradient_kernel, targets, step),
        name="gradient",
        in_specs=in_vmem(3),
        out_specs=in_vmem(1)[0],
        out_shape=jax.ShapeDtypeStruct((targets, per_step), F32),
        compiler_params=params(),
        cost_estimate=pass_cost(k_all, per_step, targets),
    )(moved, side, held(k_all))


def scatter_kernel(targets, step, off_ref, dest_ref, coef_ref, delta_ref, out_ref, parts_ref):
    per_step = delta_ref.shape[1]
    blocks = out_ref.shape[1] // POOL_BLOCK
    window = POOL_BLOCK + LANES
    for part, value in enumerate(split3(delta_ref[...])):
        parts_ref[part * targets : (part + 1) * targets, :per_step] = value
    parts_ref[:, per_step:] = jnp.zeros((3 * targets, parts_ref.shape[1] - per_step), BF16)

    @pl.loop(0, blocks // 4)
    def _(four):
        for i in range(4):
            block = 4 * four + i
            columns = pl.ds(pl.multiple_of(block * POOL_BLOCK, POOL_BLOCK), POOL_BLOCK)
            base = pl.multiple_of((off_ref[step, block] // LANES) * LANES, LANES)
            dest = two_rows(dest_ref, step, block) - base
            slots = lax.broadcasted_iota(jnp.int32, (window, POOL_BLOCK), 0)
            pick = jnp.where(slots == dest, 1.0, 0.0).astype(BF16)
            moved = jnp.dot(parts_ref[:, pl.ds(base, window)], pick, preferred_element_type=F32)
            moved = moved[:targets] + moved[targets : 2 * targets] + moved[2 * targets :]
            out_ref[:, columns] = coef_ref[:, columns] + moved


def scatter_call(off, dest, coefs, delta, step):
    targets, per_step = delta.shape
    length = round_up(per_step, LANES) + POOL_BLOCK + LANES
    return pl.pallas_call(
        functools.partial(scatter_kernel, targets, step),
        name="scatter",
        in_specs=[pl.BlockSpec(memory_space=pltpu.SMEM)] + in_vmem(3),
        out_specs=in_vmem(1)[0],
        out_shape=jax.ShapeDtypeStruct(coefs.shape, F32),
        scratch_shapes=[pltpu.VMEM((3 * targets, length), BF16)],
        compiler_params=params(),
        cost_estimate=pl.CostEstimate(flops=10**9, bytes_accessed=10**6, transcendentals=0),
    )(off, dest, coefs, delta)


def swap(value, axis, bit):
    count = lax.axis_size(axis)
    return lax.ppermute(value, axis, [(i, i ^ bit) for i in range(count)])


def bits_of(count):
    return [1 << k for k in range(count.bit_length() - 1)]


def local(samples, weights, targets, predictions, centres, coefs, block_index):
    rows_dev, features = samples.shape
    pool_dev = centres.shape[0]
    steps, slice_len = block_index.shape
    target_count = targets.shape[0]
    row_devices, cent_devices = lax.axis_size("rows"), lax.axis_size("cent")
    my_row, my_cent = lax.axis_index("rows"), lax.axis_index("cent")
    quarter = rows_dev // cent_devices
    per_step = slice_len * cent_devices // row_devices
    sharpness = 1.3 / math.sqrt(8.0 * features)
    offset = 2.0 * features * sharpness - 1.5 - 0.5 * math.log(rows_dev * row_devices)

    at = my_cent * quarter
    own_rows = lax.dynamic_slice_in_dim(samples, at, quarter, 0)
    own_weight = lax.dynamic_slice_in_dim(weights, at, quarter, 0)[None, :]
    own_target = lax.dynamic_slice_in_dim(targets, at, quarter, 1)
    own_pred = lax.dynamic_slice_in_dim(predictions, at, quarter, 1)
    weighted = (own_weight * (own_target - own_pred)).astype(BF16)
    side_count = round_up(target_count, 16)
    weight_parts = jnp.concatenate(split3_outside(own_weight), axis=0)
    side_block = jnp.concatenate(
        [
            jnp.pad(weighted, ((0, side_count - target_count), (0, 0))),
            jnp.pad(weight_parts, ((0, side_count - 3), (0, features - 2 * quarter))),
        ],
        axis=1,
    )
    chunks = {0: jnp.concatenate([own_rows, side_block], axis=0)}

    high_count = pool_dev // LANES
    place = block_index - my_row * pool_dev
    inside = (place >= 0) & (place < pool_dev)
    high = jnp.where(inside, place // LANES, -1)
    low = jnp.where(inside, place % LANES, 0)
    high_hot = (high[:, None, :] == jnp.arange(high_count)[None, :, None]).astype(BF16)
    low_hot = (low[:, None, :] == jnp.arange(LANES)[None, :, None]).astype(BF16)
    member = jnp.einsum("shl,sgl->shg", high_hot, low_hot, preferred_element_type=F32).astype(BF16)
    for bit in bits_of(cent_devices):
        member = member + swap(member, "cent", bit)

    for bit in reversed(bits_of(row_devices)):
        for have in sorted(chunks):
            chunks[have | bit] = swap(chunks[have], "rows", bit)

    upper = (jnp.arange(LANES)[:, None] <= jnp.arange(LANES)[None, :]).astype(BF16)
    before = (jnp.arange(high_count)[:, None] > jnp.arange(high_count)[None, :]).astype(BF16)
    running = jnp.einsum("shg,gk->shk", member, upper, preferred_element_type=F32)
    row_count = running[:, :, -1:]
    row_start = jnp.einsum("hi,sik->shk", before, row_count.astype(BF16), preferred_element_type=F32)
    rank = row_start + running - 1.0
    dest = jnp.where(member > 0, rank, -65536.0).astype(jnp.int32)
    group_rows = POOL_BLOCK // LANES
    off = row_start[:, ::group_rows, 0].astype(jnp.int32)
    off = jnp.pad(off, ((0, 0), (0, 1)), constant_values=per_step)

    chosen, norm, own_coef = compact(off, dest, centres, coefs, per_step, target_count)

    state = None
    for have in range(row_devices):
        slot = (my_row ^ have).astype(jnp.int32)[None]
        k_all, sums, info = block_call(
            slot, chunks[have], chosen, norm, state, per_step, target_count, row_devices, sharpness, offset
        )
        state = (k_all, sums, info)

    me = my_row.astype(jnp.int32)[None]
    squares = lax.all_gather(sums, "cent")
    gathered = squares
    total_change = None
    coef_now = coefs
    for step in range(steps):
        if step > 0:
            bits = bits_of(row_devices)
            for first in range(0, len(bits), 2):
                low = share.astype(BF16)
                pair = bits[first : first + 2]
                for bit in pair + ([sum(pair)] if len(pair) > 1 else []):
                    share = share + swap(low, "rows", bit).astype(F32)
            moved = share if step == 1 else moved + share
            gradient = gradient_call(moved, info, k_all, step, target_count, per_step)
            gathered = lax.all_gather(gradient, "cent")
        delta, total_change, *more = change_call(
            me, gathered, squares, own_coef, k_all, info, step, steps, target_count, total_change
        )
        share = more[0] if more else None
        coef_now = scatter_call(off, dest, coef_now, delta, step)

    pieces = total_change
    bits = bits_of(row_devices)
    for first in range(0, len(bits), 2):
        pair = bits[first : first + 2]
        count = 2 ** len(pair)
        pieces = pieces.reshape(pieces.shape[0] // count, count, target_count, quarter)
        kept = pieces[:, 0]
        for k in range(1, count):
            kept = kept + swap(pieces[:, k], "rows", k * pair[0])
        pieces = kept
    own_change = pieces[0]
    full = lax.all_gather(own_change, "cent")
    full = full.transpose(1, 0, 2).reshape(target_count, rows_dev)
    return (coef_now, predictions + full)


def solution(mesh):
    in_specs = (
        P("rows", None),
        P("rows"),
        P(None, "rows"),
        P(None, "rows"),
        P("rows", None),
        P(None, "rows"),
        P(None, "cent"),
    )
    out_specs = (P(None, "rows"), P(None, "rows"))
    return jax.shard_map(local, mesh=mesh, in_specs=in_specs, out_specs=out_specs, check_vma=False)
```

```python
import functools
import math

import jax
import jax.numpy as jnp
from jax import lax
from jax.experimental import pallas as pl
from jax.experimental.pallas import tpu as pltpu
from jax.sharding import PartitionSpec as P

RIDGE = 1.0
LANES = 128
POOL_BLOCK = 256
WINDOW = 144
TILE = 512
GROUPS = [(0, 1), (2, 3), (4, 6), (5,), (7,)]
KERNEL_VMEM = 16 * 2**20
LOG2E = math.log2(math.e)
NT = (((1,), (1,)), ((), ()))
F32 = jnp.float32
BF16 = jnp.bfloat16


def split3(x):
    first = x.astype(BF16)
    rest = x - first.astype(F32)
    second = rest.astype(BF16)
    third = (rest - second.astype(F32)).astype(BF16)
    return first, second, third


def split3_outside(x):
    first = lax.reduce_precision(x, 8, 7)
    rest = x - first
    second = lax.reduce_precision(rest, 8, 7)
    third = rest - second
    return first.astype(BF16), second.astype(BF16), third.astype(BF16)


def round_up(value, multiple):
    return -(-value // multiple) * multiple


def in_vmem(count):
    return [pl.BlockSpec(memory_space=pltpu.VMEM)] * count


def in_hbm(x):
    return pltpu.with_memory_space_constraint(x, pltpu.HBM)


def held(x):
    return pltpu.with_memory_space_constraint(x, pltpu.VMEM)


def params():
    return pltpu.CompilerParams(vmem_limit_bytes=KERNEL_VMEM)


def two_rows(ref, step, block):
    row = 2 * block
    return jnp.concatenate([ref[step, pl.ds(row, 1), :], ref[step, pl.ds(row + 1, 1), :]], axis=1)


def compact_kernel(per_step, targets, off_ref, dest_ref, pool_hbm, coefs_hbm, out_ref, norm_ref, coef_ref, side_out, pool_ref, coefs_ref, parts_ref, arrived, coefs_arrived):
    steps, features = out_ref.shape[0], out_ref.shape[2]
    blocks = pool_ref.shape[0] // POOL_BLOCK
    tile = math.gcd(per_step, 512)

    def fetch(block):
        at = pl.ds(pl.multiple_of(block * POOL_BLOCK, POOL_BLOCK), POOL_BLOCK)
        return pltpu.make_async_copy(pool_hbm.at[at, :], pool_ref.at[at, :], arrived.at[block])

    coefs_copy = pltpu.make_async_copy(coefs_hbm, coefs_ref, coefs_arrived)
    coefs_copy.start()
    for block in range(blocks):
        fetch(block).start()
    coefs_copy.wait()
    parts_ref[3 * targets :, :] = jnp.zeros((LANES - 3 * targets, parts_ref.shape[1]), BF16)
    for part, value in enumerate(split3(coefs_ref[...])):
        parts_ref[part * targets : (part + 1) * targets, :] = value

    def place(block, window):
        bases, picks = [], []
        for step in range(steps):
            bases.append(pl.multiple_of((off_ref[step, block] // 16) * 16, 16))
            dest = two_rows(dest_ref, step, block) - bases[step]
            slots = lax.broadcasted_iota(jnp.int32, (window, POOL_BLOCK), 0)
            picks.append(jnp.where(slots == dest, 1.0, 0.0).astype(BF16))
        pick = jnp.concatenate(picks, axis=0)
        at = pl.ds(pl.multiple_of(block * POOL_BLOCK, POOL_BLOCK), POOL_BLOCK)
        packed = jnp.dot(pick, pool_ref[at, :], preferred_element_type=F32).astype(BF16)
        side = lax.dot_general(pick, parts_ref[:, at], NT, preferred_element_type=F32).astype(BF16)
        for step in range(steps):
            first = step * window
            after = pl.ds(pl.multiple_of(bases[step] + 16, 16), window - 16)
            for rows, target in ((packed, out_ref), (side, side_out)):
                target[step, pl.ds(bases[step], 16), :] += rows[first : first + 16]
                target[step, after, :] = rows[first + 16 : first + window]

    for step in range(steps):
        out_ref[step, :16, :] = jnp.zeros((16, features), BF16)
        side_out[step, :16, :] = jnp.zeros((16, LANES), BF16)

    widest = 0
    for step in range(steps):
        for block in range(blocks):
            widest = jnp.maximum(widest, off_ref[step, block + 1] - (off_ref[step, block] // 16) * 16)
    narrow = widest <= WINDOW

    @pl.when(narrow)
    def _():
        @pl.loop(0, blocks // 2)
        def _(pair):
            for i in range(2):
                fetch(2 * pair + i).wait()
            for i in range(2):
                place(2 * pair + i, WINDOW)

    @pl.when(jnp.logical_not(narrow))
    def _():
        @pl.loop(0, blocks)
        def _(block):
            fetch(block).wait()
            place(block, POOL_BLOCK + 16)

    ones = jnp.ones((8, features), BF16)
    eye = lax.broadcasted_iota(jnp.int32, (3 * targets, LANES), 0) == lax.broadcasted_iota(
        jnp.int32, (3 * targets, LANES), 1
    )
    eye = jnp.where(eye, 1.0, 0.0).astype(BF16)
    for step in range(steps):
        for first in range(0, per_step, tile):
            rows = out_ref[step, first : first + tile, :].astype(F32)
            square = rows * rows
            high = square.astype(BF16)
            low = (square - high.astype(F32)).astype(BF16)
            norm = lax.dot_general(ones, high, NT, preferred_element_type=F32)
            norm = norm + lax.dot_general(ones, low, NT, preferred_element_type=F32)
            norm_ref[step, :, first : first + tile] = norm
            side = side_out[step, first : first + tile, :]
            parts = lax.dot_general(eye, side, NT, preferred_element_type=F32)
            coef_ref[step, :, first : first + tile] = (
                parts[:targets] + parts[targets : 2 * targets] + parts[2 * targets :]
            )


def compact(off, dest, pool, coefs, per_step, targets):
    steps = dest.shape[0]
    features = pool.shape[1]
    length = round_up(per_step, 16) + POOL_BLOCK + 16
    return pl.pallas_call(
        functools.partial(compact_kernel, per_step, targets),
        name="compact",
        in_specs=[
            pl.BlockSpec(memory_space=pltpu.SMEM),
            *in_vmem(1),
            pl.BlockSpec(memory_space=pltpu.HBM),
            pl.BlockSpec(memory_space=pltpu.HBM),
        ],
        out_specs=in_vmem(3),
        out_shape=(
            pltpu.VMEM((steps, length, features), BF16),
            pltpu.VMEM((steps, 8, per_step), F32),
            pltpu.VMEM((steps, targets, per_step), F32),
        ),
        scratch_shapes=[
            pltpu.VMEM((steps, length, LANES), BF16),
            pltpu.VMEM(pool.shape, BF16),
            pltpu.VMEM(coefs.shape, F32),
            pltpu.VMEM((LANES, pool.shape[0]), BF16),
            pltpu.SemaphoreType.DMA((pool.shape[0] // POOL_BLOCK,)),
            pltpu.SemaphoreType.DMA,
        ],
        compiler_params=params(),
        cost_estimate=pl.CostEstimate(flops=4 * 10**9, bytes_accessed=8 * 10**6, transcendentals=0),
    )(off, dest, in_hbm(pool), in_hbm(coefs))


def block_kernel(per_step, targets, quarter, count, scale, offset, slot_ref, chosen_ref, norm_ref, *refs):
    chunk_refs, (k_ref, sums_ref, side_ref) = refs[:count], refs[-3:]
    sums_in = refs[count + 1] if len(refs) > count + 3 else None
    steps = chosen_ref.shape[0]
    tile = math.gcd(per_step, TILE)

    rows = jnp.concatenate([ref[:quarter, :] for ref in chunk_refs], axis=0)
    wide_rows = rows.astype(F32)
    row_norm = jnp.sum(wide_rows * wide_rows, axis=1, keepdims=True) * (scale * LOG2E) - offset * LOG2E
    columns = []
    for i, ref in enumerate(chunk_refs):
        parts = ref[quarter : quarter + 3, quarter : 2 * quarter].astype(F32)
        weight = jnp.sum(parts, axis=0, keepdims=True)
        columns.append(jnp.transpose(jnp.broadcast_to(weight, (8, quarter)))[:, :1])
        side_ref[slot_ref[i], :targets, :] = ref[quarter : quarter + targets, :quarter].astype(F32)
        side_ref[slot_ref[i], targets:, :] = jnp.broadcast_to(weight, (side_ref.shape[1] - targets, quarter))
    weight_column = jnp.concatenate(columns, axis=0)
    weighted = jnp.concatenate([ref[quarter : quarter + targets, :quarter] for ref in chunk_refs], axis=1)

    for first in range(0, per_step, tile):
        for step in range(steps):
            dots = lax.dot_general(
                rows, chosen_ref[step, first : first + tile, :], NT, preferred_element_type=F32
            )
            centre = norm_ref[step, :1, first : first + tile] * (scale * LOG2E)
            k_low = jnp.exp2(dots * (2.0 * scale * LOG2E) - row_norm - centre).astype(BF16)
            at = step * per_step + first
            for i in range(count):
                k_ref[slot_ref[i], :, at : at + tile] = k_low[i * quarter : (i + 1) * quarter]
            wide = k_low.astype(F32)
            updates = [(targets + step, 1, jnp.sum(weight_column * (wide * wide), axis=0, keepdims=True))]
            if step == 0:
                updates.append((0, targets, jnp.dot(weighted, k_low, preferred_element_type=F32)))
            for row, size, value in updates:
                if sums_in is not None:
                    value = value + sums_in[row : row + size, first : first + tile]
                sums_ref[row : row + size, first : first + tile] = value


def block_call(slots, chunks, chosen, norm, state, per_step, targets, row_devices, scale, offset):
    steps, _, features = chosen.shape
    count = len(chunks)
    quarter = chunks[0].shape[0] - round_up(targets, 16)
    operands = [slots, held(chosen), held(norm), *chunks]
    aliases = {}
    if state is not None:
        aliases = {len(operands) + i: i for i in range(3)}
        operands += [held(x) for x in state]
    entries = count * quarter * per_step * steps
    return pl.pallas_call(
        functools.partial(block_kernel, per_step, targets, quarter, count, scale, offset),
        name="kernel_block",
        in_specs=[pl.BlockSpec(memory_space=pltpu.SMEM)] + in_vmem(len(operands) - 1),
        out_specs=in_vmem(3),
        out_shape=(
            pltpu.VMEM((row_devices, quarter, steps * per_step), BF16),
            pltpu.VMEM((round_up(targets + steps, 8), per_step), F32),
            pltpu.VMEM((row_devices, round_up(targets + 1, 8), quarter), F32),
        ),
        input_output_aliases=aliases,
        compiler_params=params(),
        cost_estimate=pl.CostEstimate(
            flops=2 * entries * features, bytes_accessed=2 * entries, transcendentals=entries
        ),
    )(*operands)


def pass_cost(k_all, per_step, targets):
    entries = k_all.shape[0] * k_all.shape[1] * per_step
    return pl.CostEstimate(flops=2 * targets * entries, bytes_accessed=2 * entries, transcendentals=0)


def change_kernel(targets, step, first, last, me_ref, sums_ref, square_ref, coef_ref, k_ref, side_ref, *refs):
    before_ref = None if first else refs[0]
    outs = list(refs if first else refs[1:])
    delta_ref, change_ref = outs[:2]
    per_step = delta_ref.shape[1]
    total, square = sums_ref[0, :targets, :], square_ref[0, targets + step : targets + step + 1, :]
    for i in range(1, sums_ref.shape[0]):
        total = total + sums_ref[i, :targets, :]
        square = square + square_ref[i, targets + step : targets + step + 1, :]
    delta = (total - RIDGE * coef_ref[step]) / (square + RIDGE)
    delta_ref[...] = delta
    low = delta.astype(BF16)

    def body(i, _):
        k_low = k_ref[i, :, step * per_step : (step + 1) * per_step]
        change = lax.dot_general(low, k_low, NT, preferred_element_type=F32)
        relative = i ^ me_ref[0]
        if not last:
            outs[2][i] = change * side_ref[i, targets : targets + 1, :]
        change_ref[relative] = change if first else change + before_ref[relative]
        return 0

    lax.fori_loop(0, k_ref.shape[0], body, 0, unroll=2)


def change_call(me, sums, squares, coef, k_all, side, step, steps, targets, before=None):
    row_devices, quarter, _ = k_all.shape
    per_step = sums.shape[2]
    last = step == steps - 1
    operands = [me, sums, squares, coef, held(k_all), side]
    if before is not None:
        operands.append(before)
    change = jax.ShapeDtypeStruct((row_devices, targets, quarter), F32)
    outs = (jax.ShapeDtypeStruct((targets, per_step), F32), change) + (() if last else (change,))
    return pl.pallas_call(
        functools.partial(change_kernel, targets, step, before is None, last),
        name="change",
        in_specs=[pl.BlockSpec(memory_space=pltpu.SMEM)] + in_vmem(len(operands) - 1),
        out_specs=in_vmem(len(outs)),
        out_shape=outs,
        compiler_params=params(),
        cost_estimate=pass_cost(k_all, per_step, targets),
    )(*operands)


def gradient_kernel(targets, step, moved_ref, side_ref, k_ref, out_ref):
    per_step = out_ref.shape[1]
    out_ref[...] = jnp.zeros_like(out_ref)

    def body(i, _):
        weighted = (side_ref[i, :targets, :] - moved_ref[i]).astype(BF16)
        k_low = k_ref[i, :, step * per_step : (step + 1) * per_step]
        out_ref[...] += jnp.dot(weighted, k_low, preferred_element_type=F32)
        return 0

    lax.fori_loop(0, k_ref.shape[0], body, 0, unroll=2)


def gradient_call(moved, side, k_all, step, targets, per_step):
    return pl.pallas_call(
        functools.partial(gradient_kernel, targets, step),
        name="gradient",
        in_specs=in_vmem(3),
        out_specs=in_vmem(1)[0],
        out_shape=jax.ShapeDtypeStruct((targets, per_step), F32),
        compiler_params=params(),
        cost_estimate=pass_cost(k_all, per_step, targets),
    )(moved, side, held(k_all))


def scatter_kernel(targets, step, off_ref, dest_ref, coef_ref, delta_ref, out_ref, parts_ref):
    per_step = delta_ref.shape[1]
    blocks = out_ref.shape[1] // POOL_BLOCK
    window = POOL_BLOCK + LANES
    for part, value in enumerate(split3(delta_ref[...])):
        parts_ref[part * targets : (part + 1) * targets, :per_step] = value
    parts_ref[:, per_step:] = jnp.zeros((3 * targets, parts_ref.shape[1] - per_step), BF16)

    @pl.loop(0, blocks // 4)
    def _(four):
        for i in range(4):
            block = 4 * four + i
            columns = pl.ds(pl.multiple_of(block * POOL_BLOCK, POOL_BLOCK), POOL_BLOCK)
            base = pl.multiple_of((off_ref[step, block] // LANES) * LANES, LANES)
            dest = two_rows(dest_ref, step, block) - base
            slots = lax.broadcasted_iota(jnp.int32, (window, POOL_BLOCK), 0)
            pick = jnp.where(slots == dest, 1.0, 0.0).astype(BF16)
            moved = jnp.dot(parts_ref[:, pl.ds(base, window)], pick, preferred_element_type=F32)
            moved = moved[:targets] + moved[targets : 2 * targets] + moved[2 * targets :]
            out_ref[:, columns] = coef_ref[:, columns] + moved


def scatter_call(off, dest, coefs, delta, step):
    targets, per_step = delta.shape
    length = round_up(per_step, LANES) + POOL_BLOCK + LANES
    return pl.pallas_call(
        functools.partial(scatter_kernel, targets, step),
        name="scatter",
        in_specs=[pl.BlockSpec(memory_space=pltpu.SMEM)] + in_vmem(3),
        out_specs=in_vmem(1)[0],
        out_shape=jax.ShapeDtypeStruct(coefs.shape, F32),
        scratch_shapes=[pltpu.VMEM((3 * targets, length), BF16)],
        compiler_params=params(),
        cost_estimate=pl.CostEstimate(flops=10**9, bytes_accessed=10**6, transcendentals=0),
    )(off, dest, coefs, delta)


def swap(value, axis, bit):
    count = lax.axis_size(axis)
    return lax.ppermute(value, axis, [(i, i ^ bit) for i in range(count)])


def bits_of(count):
    return [1 << k for k in range(count.bit_length() - 1)]


def groups_of(row_devices):
    if row_devices == 8:
        return GROUPS
    return [(have,) for have in range(row_devices)]


def local(samples, weights, targets, predictions, centres, coefs, block_index):
    rows_dev, features = samples.shape
    pool_dev = centres.shape[0]
    steps, slice_len = block_index.shape
    target_count = targets.shape[0]
    row_devices, cent_devices = lax.axis_size("rows"), lax.axis_size("cent")
    my_row, my_cent = lax.axis_index("rows"), lax.axis_index("cent")
    quarter = rows_dev // cent_devices
    per_step = slice_len * cent_devices // row_devices
    sharpness = 1.3 / math.sqrt(8.0 * features)
    offset = 2.0 * features * sharpness - 1.5 - 0.5 * math.log(rows_dev * row_devices)

    at = my_cent * quarter
    own_rows = lax.dynamic_slice_in_dim(samples, at, quarter, 0)
    own_weight = lax.dynamic_slice_in_dim(weights, at, quarter, 0)[None, :]
    own_target = lax.dynamic_slice_in_dim(targets, at, quarter, 1)
    own_pred = lax.dynamic_slice_in_dim(predictions, at, quarter, 1)
    weighted = (own_weight * (own_target - own_pred)).astype(BF16)
    side_count = round_up(target_count, 16)
    weight_parts = jnp.concatenate(split3_outside(own_weight), axis=0)
    side_block = jnp.concatenate(
        [
            jnp.pad(weighted, ((0, side_count - target_count), (0, 0))),
            jnp.pad(weight_parts, ((0, side_count - 3), (0, features - 2 * quarter))),
        ],
        axis=1,
    )
    chunks = {0: jnp.concatenate([own_rows, side_block], axis=0)}

    high_count = pool_dev // LANES
    place = block_index - my_row * pool_dev
    inside = (place >= 0) & (place < pool_dev)
    high = jnp.where(inside, place // LANES, -1)
    low = jnp.where(inside, place % LANES, 0)
    high_hot = (high[:, None, :] == jnp.arange(high_count)[None, :, None]).astype(BF16)
    low_hot = (low[:, None, :] == jnp.arange(LANES)[None, :, None]).astype(BF16)
    member = jnp.einsum("shl,sgl->shg", high_hot, low_hot, preferred_element_type=F32).astype(BF16)
    for bit in bits_of(cent_devices):
        member = member + swap(member, "cent", bit)

    for bit in reversed(bits_of(row_devices)):
        for have in sorted(chunks):
            source = chunks[have]
            if bit == 1 and have == row_devices // 2:
                source = lax.optimization_barrier(source + lax.optimization_barrier(jnp.zeros((), BF16)))
            chunks[have | bit] = swap(source, "rows", bit)

    upper = (jnp.arange(LANES)[:, None] <= jnp.arange(LANES)[None, :]).astype(BF16)
    before = (jnp.arange(high_count)[:, None] > jnp.arange(high_count)[None, :]).astype(BF16)
    running = jnp.einsum("shg,gk->shk", member, upper, preferred_element_type=F32)
    row_count = running[:, :, -1:]
    row_start = jnp.einsum("hi,sik->shk", before, row_count.astype(BF16), preferred_element_type=F32)
    rank = row_start + running - 1.0
    dest = jnp.where(member > 0, rank, -65536.0).astype(jnp.int32)
    group_rows = POOL_BLOCK // LANES
    off = row_start[:, ::group_rows, 0].astype(jnp.int32)
    off = jnp.pad(off, ((0, 0), (0, 1)), constant_values=per_step)

    chosen, norm, own_coef = compact(off, dest, centres, coefs, per_step, target_count)

    state = None
    for group in groups_of(row_devices):
        slots = my_row.astype(jnp.int32) ^ jnp.array(group, jnp.int32)
        k_all, sums, info = block_call(
            slots, [chunks[have] for have in group], chosen, norm, state,
            per_step, target_count, row_devices, sharpness, offset,
        )
        state = (k_all, sums, info)

    me = my_row.astype(jnp.int32)[None]
    squares = lax.all_gather(sums, "cent")
    gathered = squares
    total_change = None
    coef_now = coefs
    for step in range(steps):
        if step > 0:
            bits = bits_of(row_devices)
            for first in range(0, len(bits), 2):
                low = share.astype(BF16)
                pair = bits[first : first + 2]
                for bit in pair + ([sum(pair)] if len(pair) > 1 else []):
                    share = share + swap(low, "rows", bit).astype(F32)
            moved = share if step == 1 else moved + share
            gradient = gradient_call(moved, info, k_all, step, target_count, per_step)
            gathered = lax.all_gather(gradient, "cent")
        delta, total_change, *more = change_call(
            me, gathered, squares, own_coef, k_all, info, step, steps, target_count, total_change
        )
        share = more[0] if more else None
        coef_now = scatter_call(off, dest, coef_now, delta, step)

    pieces = total_change
    bits = bits_of(row_devices)
    for first in range(0, len(bits), 2):
        pair = bits[first : first + 2]
        count = 2 ** len(pair)
        pieces = pieces.reshape(pieces.shape[0] // count, count, target_count, quarter)
        kept = pieces[:, 0]
        for k in range(1, count):
            kept = kept + swap(pieces[:, k], "rows", k * pair[0])
        pieces = kept
    own_change = pieces[0]
    full = lax.all_gather(own_change, "cent")
    full = full.transpose(1, 0, 2).reshape(target_count, rows_dev)
    return (coef_now, predictions + full)


def solution(mesh):
    in_specs = (
        P("rows", None),
        P("rows"),
        P(None, "rows"),
        P(None, "rows"),
        P("rows", None),
        P(None, "rows"),
        P(None, "cent"),
    )
    out_specs = (P(None, "rows"), P(None, "rows"))
    return jax.shard_map(local, mesh=mesh, in_specs=in_specs, out_specs=out_specs, check_vma=False)
```

```python
import functools
import math

import jax
import jax.numpy as jnp
from jax import lax
from jax.experimental import pallas as pl
from jax.experimental.pallas import tpu as pltpu
from jax.sharding import PartitionSpec as P

RIDGE = 1.0
LANES = 128
POOL_BLOCK = 256
WINDOW = 144
TILE = 512
FIRST_GROUPS = [(0, 1), (2, 3), (4,), (6,), (5,), (7,)]
LATER_GROUPS = [(0, 1), (2, 3), (4, 6), (5, 7)]
KERNEL_VMEM = 16 * 2**20
LOG2E = math.log2(math.e)
NT = (((1,), (1,)), ((), ()))
F32 = jnp.float32
BF16 = jnp.bfloat16


def split3(x):
    first = x.astype(BF16)
    rest = x - first.astype(F32)
    second = rest.astype(BF16)
    third = (rest - second.astype(F32)).astype(BF16)
    return first, second, third


def split3_outside(x):
    first = lax.reduce_precision(x, 8, 7)
    rest = x - first
    second = lax.reduce_precision(rest, 8, 7)
    third = rest - second
    return first.astype(BF16), second.astype(BF16), third.astype(BF16)


def round_up(value, multiple):
    return -(-value // multiple) * multiple


def in_vmem(count):
    return [pl.BlockSpec(memory_space=pltpu.VMEM)] * count


def in_hbm(x):
    return pltpu.with_memory_space_constraint(x, pltpu.HBM)


def held(x):
    return pltpu.with_memory_space_constraint(x, pltpu.VMEM)


def params():
    return pltpu.CompilerParams(vmem_limit_bytes=KERNEL_VMEM)


def two_rows(ref, step, block):
    row = 2 * block
    return jnp.concatenate([ref[step, pl.ds(row, 1), :], ref[step, pl.ds(row + 1, 1), :]], axis=1)


def compact_kernel(step, per_step, targets, off_ref, dest_ref, pool_hbm, coefs_hbm, out_ref, norm_ref, coef_ref, side_out, pool_ref, coefs_ref, parts_ref, arrived, coefs_arrived):
    features = out_ref.shape[1]
    blocks = pool_ref.shape[0] // POOL_BLOCK
    tile = math.gcd(per_step, 512)

    def fetch(block):
        at = pl.ds(pl.multiple_of(block * POOL_BLOCK, POOL_BLOCK), POOL_BLOCK)
        return pltpu.make_async_copy(pool_hbm.at[at, :], pool_ref.at[at, :], arrived.at[block])

    coefs_copy = pltpu.make_async_copy(coefs_hbm, coefs_ref, coefs_arrived)
    coefs_copy.start()
    for block in range(blocks):
        fetch(block).start()
    widest = 0
    for block in range(blocks):
        widest = jnp.maximum(widest, off_ref[step, block + 1] - (off_ref[step, block] // 16) * 16)
    narrow = widest <= WINDOW
    out_ref[:16, :] = jnp.zeros((16, features), BF16)
    side_out[:16, :] = jnp.zeros((16, LANES), BF16)
    coefs_copy.wait()
    parts_ref[3 * targets :, :] = jnp.zeros((LANES - 3 * targets, parts_ref.shape[1]), BF16)
    for part, value in enumerate(split3(coefs_ref[...])):
        parts_ref[part * targets : (part + 1) * targets, :] = value

    def place(block, window):
        base = pl.multiple_of((off_ref[step, block] // 16) * 16, 16)
        dest = two_rows(dest_ref, step, block) - base
        slots = lax.broadcasted_iota(jnp.int32, (window, POOL_BLOCK), 0)
        pick = jnp.where(slots == dest, 1.0, 0.0).astype(BF16)
        at = pl.ds(pl.multiple_of(block * POOL_BLOCK, POOL_BLOCK), POOL_BLOCK)
        after = pl.ds(pl.multiple_of(base + 16, 16), window - 16)
        packed = jnp.dot(pick, pool_ref[at, :], preferred_element_type=F32).astype(BF16)
        side = lax.dot_general(pick, parts_ref[:, at], NT, preferred_element_type=F32).astype(BF16)
        for rows, target in ((packed, out_ref), (side, side_out)):
            target[pl.ds(base, 16), :] += rows[:16]
            target[after, :] = rows[16:]

    @pl.when(narrow)
    def _():
        @pl.loop(0, blocks // 4)
        def _(four):
            for i in range(4):
                fetch(4 * four + i).wait()
            for i in range(4):
                place(4 * four + i, WINDOW)

    @pl.when(jnp.logical_not(narrow))
    def _():
        @pl.loop(0, blocks)
        def _(block):
            fetch(block).wait()
            place(block, POOL_BLOCK + 16)

    ones = jnp.ones((8, features), BF16)
    eye = lax.broadcasted_iota(jnp.int32, (3 * targets, LANES), 0) == lax.broadcasted_iota(
        jnp.int32, (3 * targets, LANES), 1
    )
    eye = jnp.where(eye, 1.0, 0.0).astype(BF16)
    for first in range(0, per_step, tile):
        rows = out_ref[first : first + tile, :].astype(F32)
        square = rows * rows
        high = square.astype(BF16)
        low = (square - high.astype(F32)).astype(BF16)
        norm = lax.dot_general(ones, high, NT, preferred_element_type=F32)
        norm_ref[:, first : first + tile] = norm + lax.dot_general(ones, low, NT, preferred_element_type=F32)
        parts = lax.dot_general(eye, side_out[first : first + tile, :], NT, preferred_element_type=F32)
        coef_ref[:, first : first + tile] = (
            parts[:targets] + parts[targets : 2 * targets] + parts[2 * targets :]
        )


def compact(step, off, dest, pool, coefs, per_step, targets):
    features = pool.shape[1]
    length = round_up(per_step, 16) + POOL_BLOCK + 16
    return pl.pallas_call(
        functools.partial(compact_kernel, step, per_step, targets),
        name="compact",
        in_specs=[
            pl.BlockSpec(memory_space=pltpu.SMEM),
            *in_vmem(1),
            pl.BlockSpec(memory_space=pltpu.HBM),
            pl.BlockSpec(memory_space=pltpu.HBM),
        ],
        out_specs=in_vmem(3),
        out_shape=(
            pltpu.VMEM((length, features), BF16),
            pltpu.VMEM((8, per_step), F32),
            pltpu.VMEM((targets, per_step), F32),
        ),
        scratch_shapes=[
            pltpu.VMEM((length, LANES), BF16),
            pltpu.VMEM(pool.shape, BF16),
            pltpu.VMEM(coefs.shape, F32),
            pltpu.VMEM((LANES, pool.shape[0]), BF16),
            pltpu.SemaphoreType.DMA((pool.shape[0] // POOL_BLOCK,)),
            pltpu.SemaphoreType.DMA,
        ],
        compiler_params=params(),
        cost_estimate=pl.CostEstimate(flops=2 * 10**9, bytes_accessed=6 * 10**6, transcendentals=0),
    )(off, dest, in_hbm(pool), in_hbm(coefs))


def block_kernel(first_step, targets, quarter, count, scale, offset, slot_ref, chosen_ref, norm_ref, *refs):
    chunk_refs = refs[:count]
    outs = refs[count:]
    outs_count = 3 if first_step else 2
    sums_in = outs[1] if len(outs) > outs_count else None
    outs = outs[-outs_count:]
    k_ref, sums_ref = outs[:2]
    per_step = sums_ref.shape[1]
    square_row = targets if first_step else 0
    tile = math.gcd(per_step, TILE)

    rows = jnp.concatenate([ref[:quarter, :] for ref in chunk_refs], axis=0)
    wide_rows = rows.astype(F32)
    row_norm = jnp.sum(wide_rows * wide_rows, axis=1, keepdims=True) * (scale * LOG2E) - offset * LOG2E
    columns = []
    for i, ref in enumerate(chunk_refs):
        parts = ref[quarter : quarter + 3, quarter : 2 * quarter].astype(F32)
        weight = jnp.sum(parts, axis=0, keepdims=True)
        columns.append(jnp.transpose(jnp.broadcast_to(weight, (8, quarter)))[:, :1])
        if first_step:
            side_ref = outs[2]
            side_ref[slot_ref[i], :targets, :] = ref[quarter : quarter + targets, :quarter].astype(F32)
            side_ref[slot_ref[i], targets:, :] = jnp.broadcast_to(
                weight, (side_ref.shape[1] - targets, quarter)
            )
    weight_column = jnp.concatenate(columns, axis=0)
    weighted = jnp.concatenate([ref[quarter : quarter + targets, :quarter] for ref in chunk_refs], axis=1)

    for first in range(0, per_step, tile):
        dots = lax.dot_general(rows, chosen_ref[first : first + tile, :], NT, preferred_element_type=F32)
        centre = norm_ref[:1, first : first + tile] * (scale * LOG2E)
        k_low = jnp.exp2(dots * (2.0 * scale * LOG2E) - row_norm - centre).astype(BF16)
        for i in range(count):
            k_ref[slot_ref[i], :, first : first + tile] = k_low[i * quarter : (i + 1) * quarter]
        wide = k_low.astype(F32)
        updates = [(square_row, 1, jnp.sum(weight_column * (wide * wide), axis=0, keepdims=True))]
        if first_step:
            updates.append((0, targets, jnp.dot(weighted, k_low, preferred_element_type=F32)))
        for row, size, value in updates:
            if sums_in is not None:
                value = value + sums_in[row : row + size, first : first + tile]
            sums_ref[row : row + size, first : first + tile] = value


def block_call(first_step, slots, chunks, chosen, norm, state, targets, row_devices, scale, offset):
    features = chosen.shape[1]
    per_step = norm.shape[1]
    count = len(chunks)
    quarter = chunks[0].shape[0] - round_up(targets, 16)
    operands = [slots, held(chosen), held(norm), *chunks]
    outs = [
        pltpu.VMEM((row_devices, quarter, per_step), BF16),
        pltpu.VMEM((round_up(targets + 1, 8) if first_step else 8, per_step), F32),
    ]
    if first_step:
        outs.append(pltpu.VMEM((row_devices, round_up(targets + 1, 8), quarter), F32))
    aliases = {}
    if state is not None:
        aliases = {len(operands) + i: i for i in range(len(outs))}
        operands += [held(x) for x in state]
    entries = count * quarter * per_step
    return pl.pallas_call(
        functools.partial(block_kernel, first_step, targets, quarter, count, scale, offset),
        name="kernel_block",
        in_specs=[pl.BlockSpec(memory_space=pltpu.SMEM)] + in_vmem(len(operands) - 1),
        out_specs=in_vmem(len(outs)),
        out_shape=tuple(outs),
        input_output_aliases=aliases,
        compiler_params=params(),
        cost_estimate=pl.CostEstimate(
            flops=2 * entries * features, bytes_accessed=2 * entries, transcendentals=entries
        ),
    )(*operands)


def pass_cost(k_step, targets):
    entries = math.prod(k_step.shape)
    return pl.CostEstimate(flops=2 * targets * entries, bytes_accessed=2 * entries, transcendentals=0)


def change_kernel(targets, first, last, me_ref, sums_ref, coef_ref, k_ref, side_ref, *refs):
    before_ref = None if first else refs[0]
    outs = list(refs if first else refs[1:])
    delta_ref, change_ref = outs[:2]
    total = sums_ref[0]
    for i in range(1, sums_ref.shape[0]):
        total = total + sums_ref[i]
    delta = (total[:targets] - RIDGE * coef_ref[...]) / (total[targets : targets + 1] + RIDGE)
    delta_ref[...] = delta
    low = delta.astype(BF16)

    def body(i, _):
        change = lax.dot_general(low, k_ref[i], NT, preferred_element_type=F32)
        relative = i ^ me_ref[0]
        if not last:
            outs[2][i] = change * side_ref[i, targets : targets + 1, :]
        change_ref[relative] = change if first else change + before_ref[relative]
        return 0

    lax.fori_loop(0, k_ref.shape[0], body, 0, unroll=2)


def change_call(me, sums, coef, k_step, side, last, targets, before=None):
    row_devices, quarter, per_step = k_step.shape
    operands = [me, sums, coef, held(k_step), side]
    if before is not None:
        operands.append(before)
    change = jax.ShapeDtypeStruct((row_devices, targets, quarter), F32)
    outs = (jax.ShapeDtypeStruct((targets, per_step), F32), change) + (() if last else (change,))
    return pl.pallas_call(
        functools.partial(change_kernel, targets, before is None, last),
        name="change",
        in_specs=[pl.BlockSpec(memory_space=pltpu.SMEM)] + in_vmem(len(operands) - 1),
        out_specs=in_vmem(len(outs)),
        out_shape=outs,
        compiler_params=params(),
        cost_estimate=pass_cost(k_step, targets),
    )(*operands)


def gradient_kernel(targets, moved_ref, side_ref, k_ref, square_ref, out_ref):
    out_ref[:targets, :] = jnp.zeros((targets, out_ref.shape[1]), F32)
    out_ref[targets : targets + 1, :] = square_ref[:1, :]

    def body(i, _):
        weighted = (side_ref[i, :targets, :] - moved_ref[i]).astype(BF16)
        out_ref[:targets, :] += jnp.dot(weighted, k_ref[i], preferred_element_type=F32)
        return 0

    lax.fori_loop(0, k_ref.shape[0], body, 0, unroll=2)


def gradient_call(moved, side, k_step, squares, targets):
    return pl.pallas_call(
        functools.partial(gradient_kernel, targets),
        name="gradient",
        in_specs=in_vmem(4),
        out_specs=in_vmem(1)[0],
        out_shape=jax.ShapeDtypeStruct((round_up(targets + 1, 8), k_step.shape[2]), F32),
        compiler_params=params(),
        cost_estimate=pass_cost(k_step, targets),
    )(moved, side, held(k_step), squares)


def scatter_kernel(targets, step, off_ref, dest_ref, coef_ref, delta_ref, out_ref, parts_ref):
    per_step = delta_ref.shape[1]
    blocks = out_ref.shape[1] // POOL_BLOCK
    window = POOL_BLOCK + LANES
    for part, value in enumerate(split3(delta_ref[...])):
        parts_ref[part * targets : (part + 1) * targets, :per_step] = value
    parts_ref[:, per_step:] = jnp.zeros((3 * targets, parts_ref.shape[1] - per_step), BF16)

    @pl.loop(0, blocks // 4)
    def _(four):
        for i in range(4):
            block = 4 * four + i
            columns = pl.ds(pl.multiple_of(block * POOL_BLOCK, POOL_BLOCK), POOL_BLOCK)
            base = pl.multiple_of((off_ref[step, block] // LANES) * LANES, LANES)
            dest = two_rows(dest_ref, step, block) - base
            slots = lax.broadcasted_iota(jnp.int32, (window, POOL_BLOCK), 0)
            pick = jnp.where(slots == dest, 1.0, 0.0).astype(BF16)
            moved = jnp.dot(parts_ref[:, pl.ds(base, window)], pick, preferred_element_type=F32)
            moved = moved[:targets] + moved[targets : 2 * targets] + moved[2 * targets :]
            out_ref[:, columns] = coef_ref[:, columns] + moved


def scatter_call(off, dest, coefs, delta, step):
    targets, per_step = delta.shape
    length = round_up(per_step, LANES) + POOL_BLOCK + LANES
    return pl.pallas_call(
        functools.partial(scatter_kernel, targets, step),
        name="scatter",
        in_specs=[pl.BlockSpec(memory_space=pltpu.SMEM)] + in_vmem(3),
        out_specs=in_vmem(1)[0],
        out_shape=jax.ShapeDtypeStruct(coefs.shape, F32),
        scratch_shapes=[pltpu.VMEM((3 * targets, length), BF16)],
        compiler_params=params(),
        cost_estimate=pl.CostEstimate(flops=10**9, bytes_accessed=10**6, transcendentals=0),
    )(off, dest, coefs, delta)


def swap(value, axis, bit):
    count = lax.axis_size(axis)
    return lax.ppermute(value, axis, [(i, i ^ bit) for i in range(count)])


def bits_of(count):
    return [1 << k for k in range(count.bit_length() - 1)]


def groups_of(row_devices, step):
    if row_devices == 8:
        return FIRST_GROUPS if step == 0 else LATER_GROUPS
    return [(have,) for have in range(row_devices)]


def local(samples, weights, targets, predictions, centres, coefs, block_index):
    rows_dev, features = samples.shape
    pool_dev = centres.shape[0]
    steps, slice_len = block_index.shape
    target_count = targets.shape[0]
    row_devices, cent_devices = lax.axis_size("rows"), lax.axis_size("cent")
    my_row, my_cent = lax.axis_index("rows"), lax.axis_index("cent")
    quarter = rows_dev // cent_devices
    per_step = slice_len * cent_devices // row_devices
    sharpness = 1.3 / math.sqrt(8.0 * features)
    offset = 2.0 * features * sharpness - 1.5 - 0.5 * math.log(rows_dev * row_devices)

    at = my_cent * quarter
    own_rows = lax.dynamic_slice_in_dim(samples, at, quarter, 0)
    own_weight = lax.dynamic_slice_in_dim(weights, at, quarter, 0)[None, :]
    own_target = lax.dynamic_slice_in_dim(targets, at, quarter, 1)
    own_pred = lax.dynamic_slice_in_dim(predictions, at, quarter, 1)
    weighted = (own_weight * (own_target - own_pred)).astype(BF16)
    side_count = round_up(target_count, 16)
    weight_parts = jnp.concatenate(split3_outside(own_weight), axis=0)
    side_block = jnp.concatenate(
        [
            jnp.pad(weighted, ((0, side_count - target_count), (0, 0))),
            jnp.pad(weight_parts, ((0, side_count - 3), (0, features - 2 * quarter))),
        ],
        axis=1,
    )
    chunks = {0: jnp.concatenate([own_rows, side_block], axis=0)}

    high_count = pool_dev // LANES
    place = block_index - my_row * pool_dev
    inside = (place >= 0) & (place < pool_dev)
    high = jnp.where(inside, place // LANES, -1)
    low = jnp.where(inside, place % LANES, 0)
    high_hot = (high[:, None, :] == jnp.arange(high_count)[None, :, None]).astype(BF16)
    low_hot = (low[:, None, :] == jnp.arange(LANES)[None, :, None]).astype(BF16)
    member = jnp.einsum("shl,sgl->shg", high_hot, low_hot, preferred_element_type=F32).astype(BF16)
    for bit in bits_of(cent_devices):
        member = member + swap(member, "cent", bit)

    for bit in reversed(bits_of(row_devices)):
        for have in sorted(chunks):
            source = chunks[have]
            if bit == 1 and have == row_devices // 2:
                source = lax.optimization_barrier(source + lax.optimization_barrier(jnp.zeros((), BF16)))
            chunks[have | bit] = swap(source, "rows", bit)

    upper = (jnp.arange(LANES)[:, None] <= jnp.arange(LANES)[None, :]).astype(BF16)
    before = (jnp.arange(high_count)[:, None] > jnp.arange(high_count)[None, :]).astype(BF16)
    running = jnp.einsum("shg,gk->shk", member, upper, preferred_element_type=F32)
    row_count = running[:, :, -1:]
    row_start = jnp.einsum("hi,sik->shk", before, row_count.astype(BF16), preferred_element_type=F32)
    rank = row_start + running - 1.0
    dest = jnp.where(member > 0, rank, -65536.0).astype(jnp.int32)
    group_rows = POOL_BLOCK // LANES
    off = row_start[:, ::group_rows, 0].astype(jnp.int32)
    off = jnp.pad(off, ((0, 0), (0, 1)), constant_values=per_step)

    blocks = []
    own_coefs = []
    for step in range(steps):
        chosen, norm, own_coef = compact(step, off, dest, centres, coefs, per_step, target_count)
        own_coefs.append(own_coef)
        state = None
        for group in groups_of(row_devices, step):
            slots = my_row.astype(jnp.int32) ^ jnp.array(group, jnp.int32)
            state = block_call(
                step == 0, slots, [chunks[have] for have in group], chosen, norm, state,
                target_count, row_devices, sharpness, offset,
            )
        blocks.append(state)

    me = my_row.astype(jnp.int32)[None]
    info = blocks[0][2]
    sums = blocks[0][1]
    total_change = None
    deltas = []
    for step in range(steps):
        if step > 0:
            bits = bits_of(row_devices)
            for first in range(0, len(bits), 2):
                low = share.astype(BF16)
                pair = bits[first : first + 2]
                for bit in pair + ([sum(pair)] if len(pair) > 1 else []):
                    share = share + swap(low, "rows", bit).astype(F32)
            moved = share if step == 1 else moved + share
            sums = gradient_call(moved, info, blocks[step][0], blocks[step][1], target_count)
        delta, total_change, *more = change_call(
            me, lax.all_gather(sums, "cent"), own_coefs[step], blocks[step][0], info,
            step == steps - 1, target_count, total_change,
        )
        share = more[0] if more else None
        deltas.append(delta)
    coef_now = coefs
    for step in reversed(range(steps)):
        coef_now = scatter_call(off, dest, coef_now, deltas[step], step)

    pieces = total_change
    bits = bits_of(row_devices)
    for first in range(0, len(bits), 2):
        pair = bits[first : first + 2]
        count = 2 ** len(pair)
        pieces = pieces.reshape(pieces.shape[0] // count, count, target_count, quarter)
        kept = pieces[:, 0]
        for k in range(1, count):
            kept = kept + swap(pieces[:, k], "rows", k * pair[0])
        pieces = kept
    own_change = pieces[0]
    full = lax.all_gather(own_change, "cent")
    full = full.transpose(1, 0, 2).reshape(target_count, rows_dev)
    return (coef_now, predictions + full)


def solution(mesh):
    in_specs = (
        P("rows", None),
        P("rows"),
        P(None, "rows"),
        P(None, "rows"),
        P("rows", None),
        P(None, "rows"),
        P(None, "cent"),
    )
    out_specs = (P(None, "rows"), P(None, "rows"))
    return jax.shard_map(local, mesh=mesh, in_specs=in_specs, out_specs=out_specs, check_vma=False)
```

```python
import functools
import math

import jax
import jax.numpy as jnp
from jax import lax
from jax.experimental import pallas as pl
from jax.experimental.pallas import tpu as pltpu
from jax.sharding import PartitionSpec as P

RIDGE = 1.0
LANES = 128
POOL_BLOCK = 256
WINDOW = 144
TILE = 512
FIRST_GROUPS = [(0, 1), (2, 3), (4,), (6,), (5,), (7,)]
LATER_GROUPS = [(0, 1), (2, 3), (4, 6), (5, 7)]
KERNEL_VMEM = 16 * 2**20
LOG2E = math.log2(math.e)
NT = (((1,), (1,)), ((), ()))
F32 = jnp.float32
BF16 = jnp.bfloat16


def split3(x):
    first = x.astype(BF16)
    rest = x - first.astype(F32)
    second = rest.astype(BF16)
    third = (rest - second.astype(F32)).astype(BF16)
    return first, second, third


def split3_outside(x):
    first = lax.reduce_precision(x, 8, 7)
    rest = x - first
    second = lax.reduce_precision(rest, 8, 7)
    third = rest - second
    return first.astype(BF16), second.astype(BF16), third.astype(BF16)


def round_up(value, multiple):
    return -(-value // multiple) * multiple


def in_vmem(count):
    return [pl.BlockSpec(memory_space=pltpu.VMEM)] * count


def in_hbm(x):
    return pltpu.with_memory_space_constraint(x, pltpu.HBM)


def held(x):
    return pltpu.with_memory_space_constraint(x, pltpu.VMEM)


def params():
    return pltpu.CompilerParams(vmem_limit_bytes=KERNEL_VMEM)


def two_rows(ref, step, block):
    row = 2 * block
    return jnp.concatenate([ref[step, pl.ds(row, 1), :], ref[step, pl.ds(row + 1, 1), :]], axis=1)


def compact_kernel(step, per_step, targets, off_ref, dest_ref, pool_hbm, coefs_hbm, out_ref, norm_ref, coef_ref, side_out, pool_ref, coefs_ref, parts_ref, arrived, coefs_arrived):
    features = out_ref.shape[1]
    blocks = pool_ref.shape[0] // POOL_BLOCK
    tile = math.gcd(per_step, 512)

    def fetch(block):
        at = pl.ds(pl.multiple_of(block * POOL_BLOCK, POOL_BLOCK), POOL_BLOCK)
        return pltpu.make_async_copy(pool_hbm.at[at, :], pool_ref.at[at, :], arrived.at[block])

    coefs_copy = pltpu.make_async_copy(coefs_hbm, coefs_ref, coefs_arrived)
    coefs_copy.start()
    for block in range(blocks):
        fetch(block).start()
    widest = 0
    for block in range(blocks):
        widest = jnp.maximum(widest, off_ref[step, block + 1] - (off_ref[step, block] // 16) * 16)
    narrow = widest <= WINDOW
    out_ref[:16, :] = jnp.zeros((16, features), BF16)
    side_out[:16, :] = jnp.zeros((16, LANES), BF16)
    coefs_copy.wait()
    parts_ref[3 * targets :, :] = jnp.zeros((LANES - 3 * targets, parts_ref.shape[1]), BF16)
    for part, value in enumerate(split3(coefs_ref[...])):
        parts_ref[part * targets : (part + 1) * targets, :] = value

    def place(block, window):
        base = pl.multiple_of((off_ref[step, block] // 16) * 16, 16)
        dest = two_rows(dest_ref, step, block) - base
        slots = lax.broadcasted_iota(jnp.int32, (window, POOL_BLOCK), 0)
        pick = jnp.where(slots == dest, 1.0, 0.0).astype(BF16)
        at = pl.ds(pl.multiple_of(block * POOL_BLOCK, POOL_BLOCK), POOL_BLOCK)
        after = pl.ds(pl.multiple_of(base + 16, 16), window - 16)
        packed = jnp.dot(pick, pool_ref[at, :], preferred_element_type=F32).astype(BF16)
        side = lax.dot_general(pick, parts_ref[:, at], NT, preferred_element_type=F32).astype(BF16)
        for rows, target in ((packed, out_ref), (side, side_out)):
            target[pl.ds(base, 16), :] += rows[:16]
            target[after, :] = rows[16:]

    @pl.when(narrow)
    def _():
        @pl.loop(0, blocks // 4)
        def _(four):
            for i in range(4):
                fetch(4 * four + i).wait()
            for i in range(4):
                place(4 * four + i, WINDOW)

    @pl.when(jnp.logical_not(narrow))
    def _():
        @pl.loop(0, blocks)
        def _(block):
            fetch(block).wait()
            place(block, POOL_BLOCK + 16)

    ones = jnp.ones((8, features), BF16)
    eye = lax.broadcasted_iota(jnp.int32, (3 * targets, LANES), 0) == lax.broadcasted_iota(
        jnp.int32, (3 * targets, LANES), 1
    )
    eye = jnp.where(eye, 1.0, 0.0).astype(BF16)
    for first in range(0, per_step, tile):
        rows = out_ref[first : first + tile, :].astype(F32)
        square = rows * rows
        high = square.astype(BF16)
        low = (square - high.astype(F32)).astype(BF16)
        norm = lax.dot_general(ones, high, NT, preferred_element_type=F32)
        norm_ref[:, first : first + tile] = norm + lax.dot_general(ones, low, NT, preferred_element_type=F32)
        parts = lax.dot_general(eye, side_out[first : first + tile, :], NT, preferred_element_type=F32)
        coef_ref[:, first : first + tile] = (
            parts[:targets] + parts[targets : 2 * targets] + parts[2 * targets :]
        )


def compact(step, off, dest, pool, coefs, per_step, targets):
    features = pool.shape[1]
    length = round_up(per_step, 16) + POOL_BLOCK + 16
    return pl.pallas_call(
        functools.partial(compact_kernel, step, per_step, targets),
        name="compact",
        in_specs=[
            pl.BlockSpec(memory_space=pltpu.SMEM),
            *in_vmem(1),
            pl.BlockSpec(memory_space=pltpu.HBM),
            pl.BlockSpec(memory_space=pltpu.HBM),
        ],
        out_specs=in_vmem(3),
        out_shape=(
            pltpu.VMEM((length, features), BF16),
            pltpu.VMEM((8, per_step), F32),
            pltpu.VMEM((targets, per_step), F32),
        ),
        scratch_shapes=[
            pltpu.VMEM((length, LANES), BF16),
            pltpu.VMEM(pool.shape, BF16),
            pltpu.VMEM(coefs.shape, F32),
            pltpu.VMEM((LANES, pool.shape[0]), BF16),
            pltpu.SemaphoreType.DMA((pool.shape[0] // POOL_BLOCK,)),
            pltpu.SemaphoreType.DMA,
        ],
        compiler_params=params(),
        cost_estimate=pl.CostEstimate(flops=2 * 10**9, bytes_accessed=6 * 10**6, transcendentals=0),
    )(off, dest, in_hbm(pool), in_hbm(coefs))


def block_kernel(first_step, targets, quarter, group, scale, offset, me_ref, chosen_ref, norm_ref, *refs):
    count = len(group)
    chunk_refs = refs[:count]
    outs = refs[count:]
    slots = [me_ref[0] ^ have for have in group]
    outs_count = 3 if first_step else 2
    sums_in = outs[1] if len(outs) > outs_count else None
    outs = outs[-outs_count:]
    k_ref, sums_ref = outs[:2]
    per_step = sums_ref.shape[1]
    square_row = targets if first_step else 0
    tile = math.gcd(per_step, TILE)

    rows = jnp.concatenate([ref[:quarter, :] for ref in chunk_refs], axis=0)
    wide_rows = rows.astype(F32)
    row_norm = jnp.sum(wide_rows * wide_rows, axis=1, keepdims=True) * (scale * LOG2E) - offset * LOG2E
    columns = []
    for i, ref in enumerate(chunk_refs):
        parts = ref[quarter : quarter + 3, quarter : 2 * quarter].astype(F32)
        weight = jnp.sum(parts, axis=0, keepdims=True)
        columns.append(jnp.transpose(jnp.broadcast_to(weight, (8, quarter)))[:, :1])
        if first_step:
            side_ref = outs[2]
            side_ref[slots[i], :targets, :] = ref[quarter : quarter + targets, :quarter].astype(F32)
            side_ref[slots[i], targets:, :] = jnp.broadcast_to(
                weight, (side_ref.shape[1] - targets, quarter)
            )
    weight_column = jnp.concatenate(columns, axis=0)
    weighted = jnp.concatenate([ref[quarter : quarter + targets, :quarter] for ref in chunk_refs], axis=1)

    for first in range(0, per_step, tile):
        dots = lax.dot_general(rows, chosen_ref[first : first + tile, :], NT, preferred_element_type=F32)
        centre = norm_ref[:1, first : first + tile] * (scale * LOG2E)
        k_low = jnp.exp2(dots * (2.0 * scale * LOG2E) - row_norm - centre).astype(BF16)
        for i in range(count):
            k_ref[slots[i], :, first : first + tile] = k_low[i * quarter : (i + 1) * quarter]
        wide = k_low.astype(F32)
        updates = [(square_row, 1, jnp.sum(weight_column * (wide * wide), axis=0, keepdims=True))]
        if first_step:
            updates.append((0, targets, jnp.dot(weighted, k_low, preferred_element_type=F32)))
        for row, size, value in updates:
            if sums_in is not None:
                value = value + sums_in[row : row + size, first : first + tile]
            sums_ref[row : row + size, first : first + tile] = value


def block_call(first_step, me, group, chunks, chosen, norm, state, targets, row_devices, scale, offset):
    features = chosen.shape[1]
    per_step = norm.shape[1]
    count = len(chunks)
    quarter = chunks[0].shape[0] - round_up(targets, 16)
    operands = [me, held(chosen), held(norm), *chunks]
    outs = [
        pltpu.VMEM((row_devices, quarter, per_step), BF16),
        pltpu.VMEM((round_up(targets + 1, 8) if first_step else 8, per_step), F32),
    ]
    if first_step:
        outs.append(pltpu.VMEM((row_devices, round_up(targets + 1, 8), quarter), F32))
    aliases = {}
    if state is not None:
        aliases = {len(operands) + i: i for i in range(len(outs))}
        operands += [held(x) for x in state]
    entries = count * quarter * per_step
    return pl.pallas_call(
        functools.partial(block_kernel, first_step, targets, quarter, group, scale, offset),
        name="kernel_block",
        in_specs=[pl.BlockSpec(memory_space=pltpu.SMEM)] + in_vmem(len(operands) - 1),
        out_specs=in_vmem(len(outs)),
        out_shape=tuple(outs),
        input_output_aliases=aliases,
        compiler_params=params(),
        cost_estimate=pl.CostEstimate(
            flops=2 * entries * features, bytes_accessed=2 * entries, transcendentals=entries
        ),
    )(*operands)


def pass_cost(k_step, targets):
    entries = math.prod(k_step.shape)
    return pl.CostEstimate(flops=2 * targets * entries, bytes_accessed=2 * entries, transcendentals=0)


def change_kernel(targets, first, last, me_ref, sums_ref, coef_ref, k_ref, side_ref, *refs):
    before_ref = None if first else refs[0]
    outs = list(refs if first else refs[1:])
    delta_ref, change_ref = outs[:2]
    total = sums_ref[0]
    for i in range(1, sums_ref.shape[0]):
        total = total + sums_ref[i]
    delta = (total[:targets] - RIDGE * coef_ref[...]) / (total[targets : targets + 1] + RIDGE)
    delta_ref[...] = delta
    low = delta.astype(BF16)

    def body(i, _):
        change = lax.dot_general(low, k_ref[i], NT, preferred_element_type=F32)
        relative = i ^ me_ref[0]
        if not last:
            outs[2][i] = change * side_ref[i, targets : targets + 1, :]
        change_ref[relative] = change if first else change + before_ref[relative]
        return 0

    lax.fori_loop(0, k_ref.shape[0], body, 0, unroll=2)


def change_call(me, sums, coef, k_step, side, last, targets, before=None):
    row_devices, quarter, per_step = k_step.shape
    operands = [me, sums, coef, held(k_step), side]
    if before is not None:
        operands.append(before)
    change = jax.ShapeDtypeStruct((row_devices, targets, quarter), F32)
    outs = (jax.ShapeDtypeStruct((targets, per_step), F32), change) + (() if last else (change,))
    return pl.pallas_call(
        functools.partial(change_kernel, targets, before is None, last),
        name="change",
        in_specs=[pl.BlockSpec(memory_space=pltpu.SMEM)] + in_vmem(len(operands) - 1),
        out_specs=in_vmem(len(outs)),
        out_shape=outs,
        compiler_params=params(),
        cost_estimate=pass_cost(k_step, targets),
    )(*operands)


def gradient_kernel(targets, moved_ref, side_ref, k_ref, square_ref, out_ref):
    out_ref[:targets, :] = jnp.zeros((targets, out_ref.shape[1]), F32)
    out_ref[targets : targets + 1, :] = square_ref[:1, :]

    def body(i, _):
        weighted = (side_ref[i, :targets, :] - moved_ref[i]).astype(BF16)
        out_ref[:targets, :] += jnp.dot(weighted, k_ref[i], preferred_element_type=F32)
        return 0

    lax.fori_loop(0, k_ref.shape[0], body, 0, unroll=2)


def gradient_call(moved, side, k_step, squares, targets):
    return pl.pallas_call(
        functools.partial(gradient_kernel, targets),
        name="gradient",
        in_specs=in_vmem(4),
        out_specs=in_vmem(1)[0],
        out_shape=jax.ShapeDtypeStruct((round_up(targets + 1, 8), k_step.shape[2]), F32),
        compiler_params=params(),
        cost_estimate=pass_cost(k_step, targets),
    )(moved, side, held(k_step), squares)


def scatter_kernel(targets, step, off_ref, dest_ref, coef_ref, delta_ref, out_ref, parts_ref):
    per_step = delta_ref.shape[1]
    blocks = out_ref.shape[1] // POOL_BLOCK
    window = POOL_BLOCK + LANES
    for part, value in enumerate(split3(delta_ref[...])):
        parts_ref[part * targets : (part + 1) * targets, :per_step] = value
    parts_ref[:, per_step:] = jnp.zeros((3 * targets, parts_ref.shape[1] - per_step), BF16)

    @pl.loop(0, blocks // 4)
    def _(four):
        for i in range(4):
            block = 4 * four + i
            columns = pl.ds(pl.multiple_of(block * POOL_BLOCK, POOL_BLOCK), POOL_BLOCK)
            base = pl.multiple_of((off_ref[step, block] // LANES) * LANES, LANES)
            dest = two_rows(dest_ref, step, block) - base
            slots = lax.broadcasted_iota(jnp.int32, (window, POOL_BLOCK), 0)
            pick = jnp.where(slots == dest, 1.0, 0.0).astype(BF16)
            moved = jnp.dot(parts_ref[:, pl.ds(base, window)], pick, preferred_element_type=F32)
            moved = moved[:targets] + moved[targets : 2 * targets] + moved[2 * targets :]
            out_ref[:, columns] = coef_ref[:, columns] + moved


def scatter_call(off, dest, coefs, delta, step):
    targets, per_step = delta.shape
    length = round_up(per_step, LANES) + POOL_BLOCK + LANES
    return pl.pallas_call(
        functools.partial(scatter_kernel, targets, step),
        name="scatter",
        in_specs=[pl.BlockSpec(memory_space=pltpu.SMEM)] + in_vmem(3),
        out_specs=in_vmem(1)[0],
        out_shape=jax.ShapeDtypeStruct(coefs.shape, F32),
        scratch_shapes=[pltpu.VMEM((3 * targets, length), BF16)],
        compiler_params=params(),
        cost_estimate=pl.CostEstimate(flops=10**9, bytes_accessed=10**6, transcendentals=0),
    )(off, dest, coefs, delta)


def swap(value, axis, bit):
    count = lax.axis_size(axis)
    return lax.ppermute(value, axis, [(i, i ^ bit) for i in range(count)])


def own_buffer(value):
    return lax.optimization_barrier(value + lax.optimization_barrier(jnp.zeros((), value.dtype)))


def swap_both(value, row_bit, cent_bit):
    rows, cents = lax.axis_size("rows"), lax.axis_size("cent")
    pairs = [
        (r * cents + c, (r ^ row_bit) * cents + (c ^ cent_bit)) for r in range(rows) for c in range(cents)
    ]
    return lax.ppermute(value, ("rows", "cent"), pairs)


def in_order(mine, other, my_cent, bit):
    high = (my_cent & bit) > 0
    at = mine.ndim - 2
    return jnp.stack([jnp.where(high, other, mine), jnp.where(high, mine, other)], axis=at)


def bits_of(count):
    return [1 << k for k in range(count.bit_length() - 1)]


def groups_of(row_devices, step):
    if row_devices == 8:
        return FIRST_GROUPS if step == 0 else LATER_GROUPS
    return [(have,) for have in range(row_devices)]


def local(samples, weights, targets, predictions, centres, coefs, block_index):
    rows_dev, features = samples.shape
    pool_dev = centres.shape[0]
    steps, slice_len = block_index.shape
    target_count = targets.shape[0]
    row_devices, cent_devices = lax.axis_size("rows"), lax.axis_size("cent")
    my_row, my_cent = lax.axis_index("rows"), lax.axis_index("cent")
    quarter = rows_dev // cent_devices
    per_step = slice_len * cent_devices // row_devices
    sharpness = 1.3 / math.sqrt(8.0 * features)
    offset = 2.0 * features * sharpness - 1.5 - 0.5 * math.log(rows_dev * row_devices)

    at = my_cent * quarter
    own_rows = lax.dynamic_slice_in_dim(samples, at, quarter, 0)
    own_weight = lax.dynamic_slice_in_dim(weights, at, quarter, 0)[None, :]
    own_target = lax.dynamic_slice_in_dim(targets, at, quarter, 1)
    own_pred = lax.dynamic_slice_in_dim(predictions, at, quarter, 1)
    weighted = (own_weight * (own_target - own_pred)).astype(BF16)
    side_count = round_up(target_count, 16)
    weight_parts = jnp.concatenate(split3_outside(own_weight), axis=0)
    side_block = jnp.concatenate(
        [
            jnp.pad(weighted, ((0, side_count - target_count), (0, 0))),
            jnp.pad(weight_parts, ((0, side_count - 3), (0, features - 2 * quarter))),
        ],
        axis=1,
    )
    chunks = {0: jnp.concatenate([own_rows, side_block], axis=0)}

    high_count = pool_dev // LANES
    place = block_index - my_row * pool_dev
    inside = (place >= 0) & (place < pool_dev)
    high = jnp.where(inside, place // LANES, -1)
    low = jnp.where(inside, place % LANES, 0)
    high_hot = (high[:, None, :] == jnp.arange(high_count)[None, :, None]).astype(BF16)
    low_hot = (low[:, None, :] == jnp.arange(LANES)[None, :, None]).astype(BF16)
    member = jnp.einsum("shl,sgl->shg", high_hot, low_hot, preferred_element_type=F32).astype(BF16)
    for bit in bits_of(cent_devices):
        member = member + swap(member, "cent", bit)

    for bit in reversed(bits_of(row_devices)):
        for have in sorted(chunks):
            source = chunks[have]
            if bit == 1 and have == row_devices // 2:
                source = own_buffer(source)
            chunks[have | bit] = swap(source, "rows", bit)

    upper = (jnp.arange(LANES)[:, None] <= jnp.arange(LANES)[None, :]).astype(BF16)
    before = (jnp.arange(high_count)[:, None] > jnp.arange(high_count)[None, :]).astype(BF16)
    running = jnp.einsum("shg,gk->shk", member, upper, preferred_element_type=F32)
    row_count = running[:, :, -1:]
    row_start = jnp.einsum("hi,sik->shk", before, row_count.astype(BF16), preferred_element_type=F32)
    rank = row_start + running - 1.0
    dest = jnp.where(member > 0, rank, -65536.0).astype(jnp.int32)
    group_rows = POOL_BLOCK // LANES
    off = row_start[:, ::group_rows, 0].astype(jnp.int32)
    off = jnp.pad(off, ((0, 0), (0, 1)), constant_values=per_step)

    me = my_row.astype(jnp.int32)[None]
    blocks = []
    own_coefs = []
    for step in range(steps):
        chosen, norm, own_coef = compact(step, off, dest, centres, coefs, per_step, target_count)
        own_coefs.append(own_coef)
        state = None
        for group in groups_of(row_devices, step):
            state = block_call(
                step == 0, me, group, [chunks[have] for have in group], chosen, norm, state,
                target_count, row_devices, sharpness, offset,
            )
        blocks.append(state)

    info = blocks[0][2]
    sums = blocks[0][1]
    total_change = None
    deltas = []
    for step in range(steps):
        if step > 0:
            bits = bits_of(row_devices)
            for first in range(0, len(bits), 2):
                low = share.astype(BF16)
                pair = bits[first : first + 2]
                for bit in pair + ([sum(pair)] if len(pair) > 1 else []):
                    share = share + swap(low, "rows", bit).astype(F32)
            moved = share if step == 1 else moved + share
            sums = gradient_call(moved, info, blocks[step][0], blocks[step][1], target_count)
        delta, total_change, *more = change_call(
            me, lax.all_gather(sums, "cent"), own_coefs[step], blocks[step][0], info,
            step == steps - 1, target_count, total_change,
        )
        share = more[0] if more else None
        deltas.append(delta)
    coef_now = coefs
    for step in reversed(range(steps)):
        coef_now = scatter_call(off, dest, coef_now, deltas[step], step)

    pieces = total_change
    bits = bits_of(row_devices)
    for first in range(0, len(bits) - 1, 2):
        pair = bits[: len(bits) - 1][first : first + 2]
        count = 2 ** len(pair)
        pieces = pieces.reshape(pieces.shape[0] // count, count, target_count, quarter)
        kept = pieces[:, 0]
        for k in range(1, count):
            kept = kept + swap(pieces[:, k], "rows", k * pair[0])
        pieces = kept
    far, *near = reversed(bits_of(cent_devices))
    mine = pieces[0] + swap(pieces[1], "rows", bits[-1])
    other = swap(pieces[0], "cent", far)
    other = other + swap_both(own_buffer(pieces[1]), bits[-1], far)
    full = in_order(mine, other, my_cent, far)
    for bit in near:
        other = swap(full, "cent", bit)
        full = in_order(full, other, my_cent, bit)
    full = full.reshape(cent_devices, target_count, quarter)
    full = full.transpose(1, 0, 2).reshape(target_count, rows_dev)
    return (coef_now, predictions + full)


def solution(mesh):
    in_specs = (
        P("rows", None),
        P("rows"),
        P(None, "rows"),
        P(None, "rows"),
        P("rows", None),
        P(None, "rows"),
        P(None, "cent"),
    )
    out_specs = (P(None, "rows"), P(None, "rows"))
    return jax.shard_map(local, mesh=mesh, in_specs=in_specs, out_specs=out_specs, check_vma=False)
```

```python
import functools
import math

import jax
import jax.numpy as jnp
from jax import lax
from jax.experimental import pallas as pl
from jax.experimental.pallas import tpu as pltpu
from jax.sharding import PartitionSpec as P

RIDGE = 1.0
LANES = 128
POOL_BLOCK = 256
WINDOW = 144
TILE = 512
FIRST_GROUPS = [(0, 1), (2, 4), (5, 6), (3, 7)]
LATER_GROUPS = [(0, 1), (2, 4), (5, 6), (3, 7)]
KERNEL_VMEM = 16 * 2**20
LOG2E = math.log2(math.e)
NT = (((1,), (1,)), ((), ()))
F32 = jnp.float32
BF16 = jnp.bfloat16


def split3(x):
    first = x.astype(BF16)
    rest = x - first.astype(F32)
    second = rest.astype(BF16)
    third = (rest - second.astype(F32)).astype(BF16)
    return first, second, third


def split3_outside(x):
    first = lax.reduce_precision(x, 8, 7)
    rest = x - first
    second = lax.reduce_precision(rest, 8, 7)
    third = rest - second
    return first.astype(BF16), second.astype(BF16), third.astype(BF16)


def round_up(value, multiple):
    return -(-value // multiple) * multiple


def in_vmem(count):
    return [pl.BlockSpec(memory_space=pltpu.VMEM)] * count


def in_hbm(x):
    return pltpu.with_memory_space_constraint(x, pltpu.HBM)


def held(x):
    return pltpu.with_memory_space_constraint(x, pltpu.VMEM)


def params():
    return pltpu.CompilerParams(vmem_limit_bytes=KERNEL_VMEM)


def two_rows(ref, step, block):
    row = 2 * block
    return jnp.concatenate([ref[step, pl.ds(row, 1), :], ref[step, pl.ds(row + 1, 1), :]], axis=1)


def compact_kernel(step, per_step, targets, off_ref, dest_ref, *refs):
    loads = step == 0
    if loads:
        pool_hbm, coefs_hbm, out_ref, norm_ref, coef_ref, pool_ref, parts_ref, side_out, coefs_ref, arrived, coefs_arrived = refs
    else:
        pool_ref, parts_ref, out_ref, norm_ref, coef_ref, side_out = refs
    features = out_ref.shape[1]
    blocks = pool_ref.shape[0] // POOL_BLOCK
    tile = math.gcd(per_step, 512)

    def fetch(block):
        at = pl.ds(pl.multiple_of(block * POOL_BLOCK, POOL_BLOCK), POOL_BLOCK)
        return pltpu.make_async_copy(pool_hbm.at[at, :], pool_ref.at[at, :], arrived.at[block])

    if loads:
        coefs_copy = pltpu.make_async_copy(coefs_hbm, coefs_ref, coefs_arrived)
        coefs_copy.start()
        for block in range(blocks):
            fetch(block).start()
    widest = 0
    for block in range(blocks):
        widest = jnp.maximum(widest, off_ref[step, block + 1] - (off_ref[step, block] // 16) * 16)
    narrow = widest <= WINDOW
    out_ref[:16, :] = jnp.zeros((16, features), BF16)
    side_out[:16, :] = jnp.zeros((16, LANES), BF16)
    if loads:
        coefs_copy.wait()
        parts_ref[3 * targets :, :] = jnp.zeros((LANES - 3 * targets, parts_ref.shape[1]), BF16)
        for part, value in enumerate(split3(coefs_ref[...])):
            parts_ref[part * targets : (part + 1) * targets, :] = value

    def place(block, window):
        base = pl.multiple_of((off_ref[step, block] // 16) * 16, 16)
        dest = two_rows(dest_ref, step, block) - base
        slots = lax.broadcasted_iota(jnp.int32, (window, POOL_BLOCK), 0)
        pick = jnp.where(slots == dest, 1.0, 0.0).astype(BF16)
        at = pl.ds(pl.multiple_of(block * POOL_BLOCK, POOL_BLOCK), POOL_BLOCK)
        after = pl.ds(pl.multiple_of(base + 16, 16), window - 16)
        packed = jnp.dot(pick, pool_ref[at, :], preferred_element_type=F32).astype(BF16)
        side = lax.dot_general(pick, parts_ref[:, at], NT, preferred_element_type=F32).astype(BF16)
        for rows, target in ((packed, out_ref), (side, side_out)):
            target[pl.ds(base, 16), :] += rows[:16]
            target[after, :] = rows[16:]

    @pl.when(narrow)
    def _():
        @pl.loop(0, blocks // 4)
        def _(four):
            if loads:
                for i in range(4):
                    fetch(4 * four + i).wait()
            for i in range(4):
                place(4 * four + i, WINDOW)

    @pl.when(jnp.logical_not(narrow))
    def _():
        @pl.loop(0, blocks)
        def _(block):
            if loads:
                fetch(block).wait()
            place(block, POOL_BLOCK + 16)

    ones = jnp.ones((8, features), BF16)
    eye = lax.broadcasted_iota(jnp.int32, (3 * targets, LANES), 0) == lax.broadcasted_iota(
        jnp.int32, (3 * targets, LANES), 1
    )
    eye = jnp.where(eye, 1.0, 0.0).astype(BF16)
    for first in range(0, per_step, tile):
        rows = out_ref[first : first + tile, :].astype(F32)
        square = rows * rows
        high = square.astype(BF16)
        low = (square - high.astype(F32)).astype(BF16)
        norm = lax.dot_general(ones, high, NT, preferred_element_type=F32)
        norm_ref[:, first : first + tile] = norm + lax.dot_general(ones, low, NT, preferred_element_type=F32)
        parts = lax.dot_general(eye, side_out[first : first + tile, :], NT, preferred_element_type=F32)
        coef_ref[:, first : first + tile] = (
            parts[:targets] + parts[targets : 2 * targets] + parts[2 * targets :]
        )


def compact(step, off, dest, pool, coefs, per_step, targets):
    features = pool.shape[1]
    length = round_up(per_step, 16) + POOL_BLOCK + 16
    loads = step == 0
    outs = [
        pltpu.VMEM((length, features), BF16),
        pltpu.VMEM((8, per_step), F32),
        pltpu.VMEM((targets, per_step), F32),
    ]
    scratch = [pltpu.VMEM((length, LANES), BF16)]
    sources = in_vmem(2)
    operands = [held(pool), held(coefs)]
    if loads:
        outs += [pltpu.VMEM(pool.shape, BF16), pltpu.VMEM((LANES, pool.shape[0]), BF16)]
        scratch += [
            pltpu.VMEM(coefs.shape, F32),
            pltpu.SemaphoreType.DMA((pool.shape[0] // POOL_BLOCK,)),
            pltpu.SemaphoreType.DMA,
        ]
        sources = [pl.BlockSpec(memory_space=pltpu.HBM)] * 2
        operands = [in_hbm(pool), in_hbm(coefs)]
    return pl.pallas_call(
        functools.partial(compact_kernel, step, per_step, targets),
        name="compact",
        in_specs=[pl.BlockSpec(memory_space=pltpu.SMEM), *in_vmem(1), *sources],
        out_specs=in_vmem(len(outs)),
        out_shape=tuple(outs),
        scratch_shapes=scratch,
        compiler_params=params(),
        cost_estimate=pl.CostEstimate(flops=2 * 10**9, bytes_accessed=6 * 10**6, transcendentals=0),
    )(off, dest, *operands)


def block_kernel(first_step, targets, quarter, group, scale, offset, me_ref, chosen_ref, norm_ref, *refs):
    count = len(group)
    chunk_refs = refs[:count]
    outs = refs[count:]
    slots = [me_ref[0] ^ have for have in group]
    outs_count = 3 if first_step else 2
    sums_in = outs[1] if len(outs) > outs_count else None
    outs = outs[-outs_count:]
    k_ref, sums_ref = outs[:2]
    per_step = sums_ref.shape[1]
    square_row = targets if first_step else 0
    tile = math.gcd(per_step, TILE)

    rows = jnp.concatenate([ref[:quarter, :] for ref in chunk_refs], axis=0)
    wide_rows = rows.astype(F32)
    row_norm = jnp.sum(wide_rows * wide_rows, axis=1, keepdims=True) * (scale * LOG2E) - offset * LOG2E
    columns = []
    for i, ref in enumerate(chunk_refs):
        parts = ref[quarter : quarter + 3, quarter : 2 * quarter].astype(F32)
        weight = jnp.sum(parts, axis=0, keepdims=True)
        columns.append(jnp.transpose(jnp.broadcast_to(weight, (8, quarter)))[:, :1])
        if first_step:
            side_ref = outs[2]
            side_ref[slots[i], :targets, :] = ref[quarter : quarter + targets, :quarter].astype(F32)
            side_ref[slots[i], targets:, :] = jnp.broadcast_to(
                weight, (side_ref.shape[1] - targets, quarter)
            )
    weight_column = jnp.concatenate(columns, axis=0)
    weighted = jnp.concatenate([ref[quarter : quarter + targets, :quarter] for ref in chunk_refs], axis=1)

    for first in range(0, per_step, tile):
        dots = lax.dot_general(rows, chosen_ref[first : first + tile, :], NT, preferred_element_type=F32)
        centre = norm_ref[:1, first : first + tile] * (scale * LOG2E)
        k_low = jnp.exp2(dots * (2.0 * scale * LOG2E) - row_norm - centre).astype(BF16)
        for i in range(count):
            k_ref[slots[i], :, first : first + tile] = k_low[i * quarter : (i + 1) * quarter]
        wide = k_low.astype(F32)
        updates = [(square_row, 1, jnp.sum(weight_column * (wide * wide), axis=0, keepdims=True))]
        if first_step:
            updates.append((0, targets, jnp.dot(weighted, k_low, preferred_element_type=F32)))
        for row, size, value in updates:
            if sums_in is not None:
                value = value + sums_in[row : row + size, first : first + tile]
            sums_ref[row : row + size, first : first + tile] = value


def block_call(first_step, me, group, chunks, chosen, norm, state, targets, row_devices, scale, offset):
    features = chosen.shape[1]
    per_step = norm.shape[1]
    count = len(chunks)
    quarter = chunks[0].shape[0] - round_up(targets, 16)
    operands = [me, held(chosen), held(norm), *chunks]
    outs = [
        pltpu.VMEM((row_devices, quarter, per_step), BF16),
        pltpu.VMEM((round_up(targets + 1, 8) if first_step else 8, per_step), F32),
    ]
    if first_step:
        outs.append(pltpu.VMEM((row_devices, round_up(targets + 1, 8), quarter), F32))
    aliases = {}
    if state is not None:
        aliases = {len(operands) + i: i for i in range(len(outs))}
        operands += [held(x) for x in state]
    entries = count * quarter * per_step
    return pl.pallas_call(
        functools.partial(block_kernel, first_step, targets, quarter, group, scale, offset),
        name="kernel_block",
        in_specs=[pl.BlockSpec(memory_space=pltpu.SMEM)] + in_vmem(len(operands) - 1),
        out_specs=in_vmem(len(outs)),
        out_shape=tuple(outs),
        input_output_aliases=aliases,
        compiler_params=params(),
        cost_estimate=pl.CostEstimate(
            flops=2 * entries * features, bytes_accessed=2 * entries, transcendentals=entries
        ),
    )(*operands)


def pass_cost(k_step, targets):
    entries = math.prod(k_step.shape)
    return pl.CostEstimate(flops=2 * targets * entries, bytes_accessed=2 * entries, transcendentals=0)


def change_kernel(targets, first, last, me_ref, sums_ref, coef_ref, k_ref, side_ref, *refs):
    before_ref = None if first else refs[0]
    outs = list(refs if first else refs[1:])
    delta_ref, change_ref = outs[:2]
    total = sums_ref[0]
    for i in range(1, sums_ref.shape[0]):
        total = total + sums_ref[i]
    delta = (total[:targets] - RIDGE * coef_ref[...]) / (total[targets : targets + 1] + RIDGE)
    delta_ref[...] = delta
    low = delta.astype(BF16)

    def body(i, _):
        change = lax.dot_general(low, k_ref[i], NT, preferred_element_type=F32)
        relative = i ^ me_ref[0]
        if not last:
            outs[2][i] = change * side_ref[i, targets : targets + 1, :]
        change_ref[relative] = change if first else change + before_ref[relative]
        return 0

    lax.fori_loop(0, k_ref.shape[0], body, 0, unroll=2)


def change_call(me, sums, coef, k_step, side, last, targets, before=None):
    row_devices, quarter, per_step = k_step.shape
    operands = [me, sums, coef, held(k_step), side]
    if before is not None:
        operands.append(before)
    change = jax.ShapeDtypeStruct((row_devices, targets, quarter), F32)
    outs = (jax.ShapeDtypeStruct((targets, per_step), F32), change) + (() if last else (change,))
    return pl.pallas_call(
        functools.partial(change_kernel, targets, before is None, last),
        name="change",
        in_specs=[pl.BlockSpec(memory_space=pltpu.SMEM)] + in_vmem(len(operands) - 1),
        out_specs=in_vmem(len(outs)),
        out_shape=outs,
        compiler_params=params(),
        cost_estimate=pass_cost(k_step, targets),
    )(*operands)


def gradient_kernel(targets, moved_ref, side_ref, k_ref, square_ref, out_ref):
    out_ref[:targets, :] = jnp.zeros((targets, out_ref.shape[1]), F32)
    out_ref[targets : targets + 1, :] = square_ref[:1, :]

    def body(i, _):
        weighted = (side_ref[i, :targets, :] - moved_ref[i]).astype(BF16)
        out_ref[:targets, :] += jnp.dot(weighted, k_ref[i], preferred_element_type=F32)
        return 0

    lax.fori_loop(0, k_ref.shape[0], body, 0, unroll=2)


def gradient_call(moved, side, k_step, squares, targets):
    return pl.pallas_call(
        functools.partial(gradient_kernel, targets),
        name="gradient",
        in_specs=in_vmem(4),
        out_specs=in_vmem(1)[0],
        out_shape=jax.ShapeDtypeStruct((round_up(targets + 1, 8), k_step.shape[2]), F32),
        compiler_params=params(),
        cost_estimate=pass_cost(k_step, targets),
    )(moved, side, held(k_step), squares)


def scatter_kernel(targets, step, off_ref, dest_ref, coef_ref, delta_ref, out_ref, parts_ref):
    per_step = delta_ref.shape[1]
    blocks = out_ref.shape[1] // POOL_BLOCK
    window = POOL_BLOCK + LANES
    for part, value in enumerate(split3(delta_ref[...])):
        parts_ref[part * targets : (part + 1) * targets, :per_step] = value
    parts_ref[:, per_step:] = jnp.zeros((3 * targets, parts_ref.shape[1] - per_step), BF16)

    @pl.loop(0, blocks // 4)
    def _(four):
        for i in range(4):
            block = 4 * four + i
            columns = pl.ds(pl.multiple_of(block * POOL_BLOCK, POOL_BLOCK), POOL_BLOCK)
            base = pl.multiple_of((off_ref[step, block] // LANES) * LANES, LANES)
            dest = two_rows(dest_ref, step, block) - base
            slots = lax.broadcasted_iota(jnp.int32, (window, POOL_BLOCK), 0)
            pick = jnp.where(slots == dest, 1.0, 0.0).astype(BF16)
            moved = jnp.dot(parts_ref[:, pl.ds(base, window)], pick, preferred_element_type=F32)
            moved = moved[:targets] + moved[targets : 2 * targets] + moved[2 * targets :]
            out_ref[:, columns] = coef_ref[:, columns] + moved


def scatter_call(off, dest, coefs, delta, step):
    targets, per_step = delta.shape
    length = round_up(per_step, LANES) + POOL_BLOCK + LANES
    return pl.pallas_call(
        functools.partial(scatter_kernel, targets, step),
        name="scatter",
        in_specs=[pl.BlockSpec(memory_space=pltpu.SMEM)] + in_vmem(3),
        out_specs=in_vmem(1)[0],
        out_shape=jax.ShapeDtypeStruct(coefs.shape, F32),
        scratch_shapes=[pltpu.VMEM((3 * targets, length), BF16)],
        compiler_params=params(),
        cost_estimate=pl.CostEstimate(flops=10**9, bytes_accessed=10**6, transcendentals=0),
    )(off, dest, coefs, delta)


def swap(value, axis, bit):
    count = lax.axis_size(axis)
    return lax.ppermute(value, axis, [(i, i ^ bit) for i in range(count)])


def own_buffer(value):
    return lax.optimization_barrier(value + lax.optimization_barrier(jnp.zeros((), value.dtype)))


def bits_of(count):
    return [1 << k for k in range(count.bit_length() - 1)]


def last_hop(chunk, row_devices):
    return 2 if (chunk, row_devices) == (3, 8) else chunk & -chunk


def groups_of(row_devices, step):
    if row_devices == 8:
        return FIRST_GROUPS if step == 0 else LATER_GROUPS
    return [(have,) for have in range(row_devices)]


def local(samples, weights, targets, predictions, centres, coefs, block_index):
    rows_dev, features = samples.shape
    pool_dev = centres.shape[0]
    steps, slice_len = block_index.shape
    target_count = targets.shape[0]
    row_devices, cent_devices = lax.axis_size("rows"), lax.axis_size("cent")
    my_row, my_cent = lax.axis_index("rows"), lax.axis_index("cent")
    quarter = rows_dev // cent_devices
    per_step = slice_len * cent_devices // row_devices
    sharpness = 1.3 / math.sqrt(8.0 * features)
    offset = 2.0 * features * sharpness - 1.5 - 0.5 * math.log(rows_dev * row_devices)

    at = my_cent * quarter
    own_rows = lax.dynamic_slice_in_dim(samples, at, quarter, 0)
    own_weight = lax.dynamic_slice_in_dim(weights, at, quarter, 0)[None, :]
    own_target = lax.dynamic_slice_in_dim(targets, at, quarter, 1)
    own_pred = lax.dynamic_slice_in_dim(predictions, at, quarter, 1)
    weighted = (own_weight * (own_target - own_pred)).astype(BF16)
    side_count = round_up(target_count, 16)
    weight_parts = jnp.concatenate(split3_outside(own_weight), axis=0)
    side_block = jnp.concatenate(
        [
            jnp.pad(weighted, ((0, side_count - target_count), (0, 0))),
            jnp.pad(weight_parts, ((0, side_count - 3), (0, features - 2 * quarter))),
        ],
        axis=1,
    )
    chunks = {0: jnp.concatenate([own_rows, side_block], axis=0)}

    high_count = pool_dev // LANES
    place = block_index - my_row * pool_dev
    inside = (place >= 0) & (place < pool_dev)
    high = jnp.where(inside, place // LANES, -1)
    low = jnp.where(inside, place % LANES, 0)
    high_hot = (high[:, None, :] == jnp.arange(high_count)[None, :, None]).astype(BF16)
    low_hot = (low[:, None, :] == jnp.arange(LANES)[None, :, None]).astype(BF16)
    member = jnp.einsum("shl,sgl->shg", high_hot, low_hot, preferred_element_type=F32).astype(BF16)
    for bit in bits_of(cent_devices):
        member = member + swap(member, "cent", bit)

    for chunk in sorted(range(1, row_devices), key=lambda chunk: (bin(chunk).count("1"), chunk)):
        bit = last_hop(chunk, row_devices)
        source = chunks[chunk ^ bit]
        if bit == 1 and chunk ^ bit == row_devices // 2:
            source = own_buffer(source)
        chunks[chunk] = swap(source, "rows", bit)

    upper = (jnp.arange(LANES)[:, None] <= jnp.arange(LANES)[None, :]).astype(BF16)
    before = (jnp.arange(high_count)[:, None] > jnp.arange(high_count)[None, :]).astype(BF16)
    running = jnp.einsum("shg,gk->shk", member, upper, preferred_element_type=F32)
    row_count = running[:, :, -1:]
    row_start = jnp.einsum("hi,sik->shk", before, row_count.astype(BF16), preferred_element_type=F32)
    rank = row_start + running - 1.0
    dest = jnp.where(member > 0, rank, -65536.0).astype(jnp.int32)
    group_rows = POOL_BLOCK // LANES
    off = row_start[:, ::group_rows, 0].astype(jnp.int32)
    off = jnp.pad(off, ((0, 0), (0, 1)), constant_values=per_step)

    me = my_row.astype(jnp.int32)[None]
    blocks = []
    own_coefs = []
    shard = []
    for step in range(steps):
        chosen, norm, own_coef, *more = compact(
            step, off, dest, *((centres, coefs) if step == 0 else shard), per_step, target_count
        )
        shard = more or shard
        own_coefs.append(own_coef)
        state = None
        for group in groups_of(row_devices, step):
            state = block_call(
                step == 0, me, group, [chunks[have] for have in group], chosen, norm, state,
                target_count, row_devices, sharpness, offset,
            )
        blocks.append(state)

    info = blocks[0][2]
    sums = blocks[0][1]
    total_change = None
    deltas = []
    for step in range(steps):
        if step > 0:
            bits = bits_of(row_devices)
            for first in range(0, len(bits), 2):
                low = share.astype(BF16)
                pair = bits[first : first + 2]
                for bit in pair + ([sum(pair)] if len(pair) > 1 else []):
                    share = share + swap(low, "rows", bit).astype(F32)
            moved = share if step == 1 else moved + share
            sums = gradient_call(moved, info, blocks[step][0], blocks[step][1], target_count)
        delta, total_change, *more = change_call(
            me, lax.all_gather(sums, "cent"), own_coefs[step], blocks[step][0], info,
            step == steps - 1, target_count, total_change,
        )
        share = more[0] if more else None
        deltas.append(delta)
    coef_now = coefs
    for step in reversed(range(steps)):
        coef_now = scatter_call(off, dest, coef_now, deltas[step], step)

    pieces = total_change
    bits = bits_of(row_devices)
    for first in range(0, len(bits), 2):
        pair = bits[first : first + 2]
        count = 2 ** len(pair)
        pieces = pieces.reshape(pieces.shape[0] // count, count, target_count, quarter)
        kept = pieces[:, 0]
        for k in range(1, count):
            kept = kept + swap(pieces[:, k], "rows", k * pair[0])
        pieces = kept
    own_change = pieces[0]
    full = lax.all_gather(own_change, "cent")
    full = full.transpose(1, 0, 2).reshape(target_count, rows_dev)
    return (coef_now, predictions + full)


def solution(mesh):
    in_specs = (
        P("rows", None),
        P("rows"),
        P(None, "rows"),
        P(None, "rows"),
        P("rows", None),
        P(None, "rows"),
        P(None, "cent"),
    )
    out_specs = (P(None, "rows"), P(None, "rows"))
    return jax.shard_map(local, mesh=mesh, in_specs=in_specs, out_specs=out_specs, check_vma=False)
```

```python
import functools
import math

import jax
import jax.numpy as jnp
from jax import lax
from jax.experimental import pallas as pl
from jax.experimental.pallas import tpu as pltpu
from jax.sharding import PartitionSpec as P

RIDGE = 1.0
LANES = 128
POOL_BLOCK = 256
WINDOW = 144
TILE = 512
FIRST_GROUPS = [(0, 1), (2, 4), (5, 6), (3, 7)]
LATER_GROUPS = [(0, 1), (2, 4), (5, 6), (3, 7)]
KERNEL_VMEM = 16 * 2**20
LOG2E = math.log2(math.e)
NT = (((1,), (1,)), ((), ()))
F32 = jnp.float32
BF16 = jnp.bfloat16


def split3(x):
    first = x.astype(BF16)
    rest = x - first.astype(F32)
    second = rest.astype(BF16)
    third = (rest - second.astype(F32)).astype(BF16)
    return first, second, third


def split3_outside(x):
    first = lax.reduce_precision(x, 8, 7)
    rest = x - first
    second = lax.reduce_precision(rest, 8, 7)
    third = rest - second
    return first.astype(BF16), second.astype(BF16), third.astype(BF16)


def round_up(value, multiple):
    return -(-value // multiple) * multiple


def in_vmem(count):
    return [pl.BlockSpec(memory_space=pltpu.VMEM)] * count


def in_hbm(x):
    return pltpu.with_memory_space_constraint(x, pltpu.HBM)


def held(x):
    return pltpu.with_memory_space_constraint(x, pltpu.VMEM)


def params():
    return pltpu.CompilerParams(vmem_limit_bytes=KERNEL_VMEM)


def two_rows(ref, step, block):
    row = 2 * block
    return jnp.concatenate([ref[step, pl.ds(row, 1), :], ref[step, pl.ds(row + 1, 1), :]], axis=1)


def compact_kernel(step, per_step, targets, off_ref, dest_ref, *refs):
    loads = step == 0
    if loads:
        pool_hbm, coefs_hbm, out_ref, norm_ref, coef_ref, pool_ref, parts_ref, side_out, coefs_ref, arrived, coefs_arrived = refs
    else:
        pool_ref, parts_ref, out_ref, norm_ref, coef_ref, side_out = refs
    features = out_ref.shape[1]
    blocks = pool_ref.shape[0] // POOL_BLOCK
    tile = math.gcd(per_step, 512)

    def fetch(block):
        at = pl.ds(pl.multiple_of(block * POOL_BLOCK, POOL_BLOCK), POOL_BLOCK)
        return pltpu.make_async_copy(pool_hbm.at[at, :], pool_ref.at[at, :], arrived.at[block])

    if loads:
        coefs_copy = pltpu.make_async_copy(coefs_hbm, coefs_ref, coefs_arrived)
        coefs_copy.start()
        for block in range(8):
            fetch(block).start()
    widest = 0
    for block in range(blocks):
        widest = jnp.maximum(widest, off_ref[step, block + 1] - (off_ref[step, block] // 16) * 16)
    narrow = widest <= WINDOW
    out_ref[:16, :] = jnp.zeros((16, features), BF16)
    side_out[:16, :] = jnp.zeros((16, LANES), BF16)
    if loads:
        coefs_copy.wait()
        parts_ref[3 * targets :, :] = jnp.zeros((LANES - 3 * targets, parts_ref.shape[1]), BF16)
        for part, value in enumerate(split3(coefs_ref[...])):
            parts_ref[part * targets : (part + 1) * targets, :] = value

    def place(block, window):
        base = pl.multiple_of((off_ref[step, block] // 16) * 16, 16)
        dest = two_rows(dest_ref, step, block) - base
        slots = lax.broadcasted_iota(jnp.int32, (window, POOL_BLOCK), 0)
        pick = jnp.where(slots == dest, 1.0, 0.0).astype(BF16)
        at = pl.ds(pl.multiple_of(block * POOL_BLOCK, POOL_BLOCK), POOL_BLOCK)
        after = pl.ds(pl.multiple_of(base + 16, 16), window - 16)
        packed = jnp.dot(pick, pool_ref[at, :], preferred_element_type=F32).astype(BF16)
        side = lax.dot_general(pick, parts_ref[:, at], NT, preferred_element_type=F32).astype(BF16)
        for rows, target in ((packed, out_ref), (side, side_out)):
            target[pl.ds(base, 16), :] += rows[:16]
            target[after, :] = rows[16:]

    @pl.when(narrow)
    def _():
        @pl.loop(0, blocks // 4)
        def _(four):
            if loads:

                @pl.when(four + 2 < blocks // 4)
                def _():
                    for i in range(4):
                        fetch(4 * four + 8 + i).start()

                for i in range(4):
                    fetch(4 * four + i).wait()
            for i in range(4):
                place(4 * four + i, WINDOW)

    @pl.when(jnp.logical_not(narrow))
    def _():
        if loads:
            for block in range(8, blocks):
                fetch(block).start()

        @pl.loop(0, blocks)
        def _(block):
            if loads:
                fetch(block).wait()
            place(block, POOL_BLOCK + 16)

    ones = jnp.ones((8, features), BF16)
    eye = lax.broadcasted_iota(jnp.int32, (3 * targets, LANES), 0) == lax.broadcasted_iota(
        jnp.int32, (3 * targets, LANES), 1
    )
    eye = jnp.where(eye, 1.0, 0.0).astype(BF16)
    for first in range(0, per_step, tile):
        rows = out_ref[first : first + tile, :].astype(F32)
        square = rows * rows
        high = square.astype(BF16)
        low = (square - high.astype(F32)).astype(BF16)
        norm = lax.dot_general(ones, high, NT, preferred_element_type=F32)
        norm_ref[:, first : first + tile] = norm + lax.dot_general(ones, low, NT, preferred_element_type=F32)
        parts = lax.dot_general(eye, side_out[first : first + tile, :], NT, preferred_element_type=F32)
        coef_ref[:, first : first + tile] = (
            parts[:targets] + parts[targets : 2 * targets] + parts[2 * targets :]
        )


def compact(step, off, dest, pool, coefs, per_step, targets):
    features = pool.shape[1]
    length = round_up(per_step, 16) + POOL_BLOCK + 16
    loads = step == 0
    outs = [
        pltpu.VMEM((length, features), BF16),
        pltpu.VMEM((8, per_step), F32),
        pltpu.VMEM((targets, per_step), F32),
    ]
    scratch = [pltpu.VMEM((length, LANES), BF16)]
    sources = in_vmem(2)
    operands = [held(pool), held(coefs)]
    if loads:
        outs += [pltpu.VMEM(pool.shape, BF16), pltpu.VMEM((LANES, pool.shape[0]), BF16)]
        scratch += [
            pltpu.VMEM(coefs.shape, F32),
            pltpu.SemaphoreType.DMA((pool.shape[0] // POOL_BLOCK,)),
            pltpu.SemaphoreType.DMA,
        ]
        sources = [pl.BlockSpec(memory_space=pltpu.HBM)] * 2
        operands = [in_hbm(pool), in_hbm(coefs)]
    return pl.pallas_call(
        functools.partial(compact_kernel, step, per_step, targets),
        name="compact",
        in_specs=[pl.BlockSpec(memory_space=pltpu.SMEM), *in_vmem(1), *sources],
        out_specs=in_vmem(len(outs)),
        out_shape=tuple(outs),
        scratch_shapes=scratch,
        compiler_params=params(),
        cost_estimate=pl.CostEstimate(flops=2 * 10**9, bytes_accessed=6 * 10**6, transcendentals=0),
    )(off, dest, *operands)


def block_kernel(first_step, targets, quarter, group, scale, offset, me_ref, chosen_ref, norm_ref, *refs):
    count = len(group)
    chunk_refs = refs[:count]
    outs = refs[count:]
    slots = [me_ref[0] ^ have for have in group]
    outs_count = 3 if first_step else 2
    sums_in = outs[1] if len(outs) > outs_count else None
    outs = outs[-outs_count:]
    k_ref, sums_ref = outs[:2]
    per_step = sums_ref.shape[1]
    square_row = targets if first_step else 0
    tile = math.gcd(per_step, TILE)

    rows = jnp.concatenate([ref[:quarter, :] for ref in chunk_refs], axis=0)
    wide_rows = rows.astype(F32)
    row_norm = jnp.sum(wide_rows * wide_rows, axis=1, keepdims=True) * (scale * LOG2E) - offset * LOG2E
    columns = []
    for i, ref in enumerate(chunk_refs):
        parts = ref[quarter : quarter + 3, quarter : 2 * quarter].astype(F32)
        weight = jnp.sum(parts, axis=0, keepdims=True)
        columns.append(jnp.transpose(jnp.broadcast_to(weight, (8, quarter)))[:, :1])
        if first_step:
            side_ref = outs[2]
            side_ref[slots[i], :targets, :] = ref[quarter : quarter + targets, :quarter].astype(F32)
            side_ref[slots[i], targets:, :] = jnp.broadcast_to(
                weight, (side_ref.shape[1] - targets, quarter)
            )
    weight_column = jnp.concatenate(columns, axis=0)
    weighted = jnp.concatenate([ref[quarter : quarter + targets, :quarter] for ref in chunk_refs], axis=1)

    for first in range(0, per_step, tile):
        dots = lax.dot_general(rows, chosen_ref[first : first + tile, :], NT, preferred_element_type=F32)
        centre = norm_ref[:1, first : first + tile] * (scale * LOG2E)
        k_low = jnp.exp2(dots * (2.0 * scale * LOG2E) - row_norm - centre).astype(BF16)
        for i in range(count):
            k_ref[slots[i], :, first : first + tile] = k_low[i * quarter : (i + 1) * quarter]
        wide = k_low.astype(F32)
        updates = [(square_row, 1, jnp.sum(weight_column * (wide * wide), axis=0, keepdims=True))]
        if first_step:
            updates.append((0, targets, jnp.dot(weighted, k_low, preferred_element_type=F32)))
        for row, size, value in updates:
            if sums_in is not None:
                value = value + sums_in[row : row + size, first : first + tile]
            sums_ref[row : row + size, first : first + tile] = value


def block_call(first_step, me, group, chunks, chosen, norm, state, targets, row_devices, scale, offset):
    features = chosen.shape[1]
    per_step = norm.shape[1]
    count = len(chunks)
    quarter = chunks[0].shape[0] - round_up(targets, 16)
    operands = [me, held(chosen), held(norm), *chunks]
    outs = [
        pltpu.VMEM((row_devices, quarter, per_step), BF16),
        pltpu.VMEM((round_up(targets + 1, 8) if first_step else 8, per_step), F32),
    ]
    if first_step:
        outs.append(pltpu.VMEM((row_devices, round_up(targets + 1, 8), quarter), F32))
    aliases = {}
    if state is not None:
        aliases = {len(operands) + i: i for i in range(len(outs))}
        operands += [held(x) for x in state]
    entries = count * quarter * per_step
    return pl.pallas_call(
        functools.partial(block_kernel, first_step, targets, quarter, group, scale, offset),
        name="kernel_block",
        in_specs=[pl.BlockSpec(memory_space=pltpu.SMEM)] + in_vmem(len(operands) - 1),
        out_specs=in_vmem(len(outs)),
        out_shape=tuple(outs),
        input_output_aliases=aliases,
        compiler_params=params(),
        cost_estimate=pl.CostEstimate(
            flops=2 * entries * features, bytes_accessed=2 * entries, transcendentals=entries
        ),
    )(*operands)


def pass_cost(k_step, targets):
    entries = math.prod(k_step.shape)
    return pl.CostEstimate(flops=2 * targets * entries, bytes_accessed=2 * entries, transcendentals=0)


def change_kernel(targets, first, last, me_ref, sums_ref, coef_ref, k_ref, side_ref, *refs):
    before_ref = None if first else refs[0]
    outs = list(refs if first else refs[1:])
    delta_ref, change_ref = outs[:2]
    total = sums_ref[0]
    for i in range(1, sums_ref.shape[0]):
        total = total + sums_ref[i]
    delta = (total[:targets] - RIDGE * coef_ref[...]) / (total[targets : targets + 1] + RIDGE)
    delta_ref[...] = delta
    low = delta.astype(BF16)

    def body(i, _):
        change = lax.dot_general(low, k_ref[i], NT, preferred_element_type=F32)
        relative = i ^ me_ref[0]
        if not last:
            outs[2][i] = change * side_ref[i, targets : targets + 1, :]
        change_ref[relative] = change if first else change + before_ref[relative]
        return 0

    lax.fori_loop(0, k_ref.shape[0], body, 0, unroll=2)


def change_call(me, sums, coef, k_step, side, last, targets, before=None):
    row_devices, quarter, per_step = k_step.shape
    operands = [me, sums, coef, held(k_step), side]
    if before is not None:
        operands.append(before)
    change = jax.ShapeDtypeStruct((row_devices, targets, quarter), F32)
    outs = (jax.ShapeDtypeStruct((targets, per_step), F32), change) + (() if last else (change,))
    return pl.pallas_call(
        functools.partial(change_kernel, targets, before is None, last),
        name="change",
        in_specs=[pl.BlockSpec(memory_space=pltpu.SMEM)] + in_vmem(len(operands) - 1),
        out_specs=in_vmem(len(outs)),
        out_shape=outs,
        compiler_params=params(),
        cost_estimate=pass_cost(k_step, targets),
    )(*operands)


def gradient_kernel(targets, moved_ref, side_ref, k_ref, square_ref, out_ref):
    out_ref[:targets, :] = jnp.zeros((targets, out_ref.shape[1]), F32)
    out_ref[targets : targets + 1, :] = square_ref[:1, :]

    def body(i, _):
        weighted = (side_ref[i, :targets, :] - moved_ref[i]).astype(BF16)
        out_ref[:targets, :] += jnp.dot(weighted, k_ref[i], preferred_element_type=F32)
        return 0

    lax.fori_loop(0, k_ref.shape[0], body, 0, unroll=2)


def gradient_call(moved, side, k_step, squares, targets):
    return pl.pallas_call(
        functools.partial(gradient_kernel, targets),
        name="gradient",
        in_specs=in_vmem(4),
        out_specs=in_vmem(1)[0],
        out_shape=jax.ShapeDtypeStruct((round_up(targets + 1, 8), k_step.shape[2]), F32),
        compiler_params=params(),
        cost_estimate=pass_cost(k_step, targets),
    )(moved, side, held(k_step), squares)


def scatter_kernel(targets, step, off_ref, dest_ref, coef_ref, delta_ref, out_ref, parts_ref):
    per_step = delta_ref.shape[1]
    blocks = out_ref.shape[1] // POOL_BLOCK
    window = POOL_BLOCK + LANES
    for part, value in enumerate(split3(delta_ref[...])):
        parts_ref[part * targets : (part + 1) * targets, :per_step] = value
    parts_ref[:, per_step:] = jnp.zeros((3 * targets, parts_ref.shape[1] - per_step), BF16)

    @pl.loop(0, blocks // 4)
    def _(four):
        for i in range(4):
            block = 4 * four + i
            columns = pl.ds(pl.multiple_of(block * POOL_BLOCK, POOL_BLOCK), POOL_BLOCK)
            base = pl.multiple_of((off_ref[step, block] // LANES) * LANES, LANES)
            dest = two_rows(dest_ref, step, block) - base
            slots = lax.broadcasted_iota(jnp.int32, (window, POOL_BLOCK), 0)
            pick = jnp.where(slots == dest, 1.0, 0.0).astype(BF16)
            moved = jnp.dot(parts_ref[:, pl.ds(base, window)], pick, preferred_element_type=F32)
            moved = moved[:targets] + moved[targets : 2 * targets] + moved[2 * targets :]
            out_ref[:, columns] = coef_ref[:, columns] + moved


def scatter_call(off, dest, coefs, delta, step):
    targets, per_step = delta.shape
    length = round_up(per_step, LANES) + POOL_BLOCK + LANES
    return pl.pallas_call(
        functools.partial(scatter_kernel, targets, step),
        name="scatter",
        in_specs=[pl.BlockSpec(memory_space=pltpu.SMEM)] + in_vmem(3),
        out_specs=in_vmem(1)[0],
        out_shape=jax.ShapeDtypeStruct(coefs.shape, F32),
        scratch_shapes=[pltpu.VMEM((3 * targets, length), BF16)],
        compiler_params=params(),
        cost_estimate=pl.CostEstimate(flops=10**9, bytes_accessed=10**6, transcendentals=0),
    )(off, dest, coefs, delta)


def swap(value, axis, bit):
    count = lax.axis_size(axis)
    return lax.ppermute(value, axis, [(i, i ^ bit) for i in range(count)])


def own_buffer(value):
    return lax.optimization_barrier(value + lax.optimization_barrier(jnp.zeros((), value.dtype)))


def bits_of(count):
    return [1 << k for k in range(count.bit_length() - 1)]


def last_hop(chunk, row_devices):
    return 2 if (chunk, row_devices) == (3, 8) else chunk & -chunk


def groups_of(row_devices, step):
    if row_devices == 8:
        return FIRST_GROUPS if step == 0 else LATER_GROUPS
    return [(have,) for have in range(row_devices)]


def local(samples, weights, targets, predictions, centres, coefs, block_index):
    rows_dev, features = samples.shape
    pool_dev = centres.shape[0]
    steps, slice_len = block_index.shape
    target_count = targets.shape[0]
    row_devices, cent_devices = lax.axis_size("rows"), lax.axis_size("cent")
    my_row, my_cent = lax.axis_index("rows"), lax.axis_index("cent")
    quarter = rows_dev // cent_devices
    per_step = slice_len * cent_devices // row_devices
    sharpness = 1.3 / math.sqrt(8.0 * features)
    offset = 2.0 * features * sharpness - 1.5 - 0.5 * math.log(rows_dev * row_devices)

    at = my_cent * quarter
    own_rows = lax.dynamic_slice_in_dim(samples, at, quarter, 0)
    own_weight = lax.dynamic_slice_in_dim(weights, at, quarter, 0)[None, :]
    own_target = lax.dynamic_slice_in_dim(targets, at, quarter, 1)
    own_pred = lax.dynamic_slice_in_dim(predictions, at, quarter, 1)
    weighted = (own_weight * (own_target - own_pred)).astype(BF16)
    side_count = round_up(target_count, 16)
    weight_parts = jnp.concatenate(split3_outside(own_weight), axis=0)
    side_block = jnp.concatenate(
        [
            jnp.pad(weighted, ((0, side_count - target_count), (0, 0))),
            jnp.pad(weight_parts, ((0, side_count - 3), (0, features - 2 * quarter))),
        ],
        axis=1,
    )
    chunks = {0: jnp.concatenate([own_rows, side_block], axis=0)}

    high_count = pool_dev // LANES
    place = block_index - my_row * pool_dev
    inside = (place >= 0) & (place < pool_dev)
    high = jnp.where(inside, place // LANES, -1)
    low = jnp.where(inside, place % LANES, 0)
    high_hot = (high[:, None, :] == jnp.arange(high_count)[None, :, None]).astype(BF16)
    low_hot = (low[:, None, :] == jnp.arange(LANES)[None, :, None]).astype(BF16)
    member = jnp.einsum("shl,sgl->shg", high_hot, low_hot, preferred_element_type=F32).astype(BF16)
    for bit in bits_of(cent_devices):
        member = member + swap(member, "cent", bit)

    for chunk in sorted(range(1, row_devices), key=lambda chunk: (bin(chunk).count("1"), chunk)):
        bit = last_hop(chunk, row_devices)
        source = chunks[chunk ^ bit]
        if bit == 1 and chunk ^ bit == row_devices // 2:
            source = own_buffer(source)
        chunks[chunk] = swap(source, "rows", bit)

    upper = (jnp.arange(LANES)[:, None] <= jnp.arange(LANES)[None, :]).astype(BF16)
    before = (jnp.arange(high_count)[:, None] > jnp.arange(high_count)[None, :]).astype(BF16)
    running = jnp.einsum("shg,gk->shk", member, upper, preferred_element_type=F32)
    row_count = running[:, :, -1:]
    row_start = jnp.einsum("hi,sik->shk", before, row_count.astype(BF16), preferred_element_type=F32)
    rank = row_start + running - 1.0
    dest = jnp.where(member > 0, rank, -65536.0).astype(jnp.int32)
    group_rows = POOL_BLOCK // LANES
    off = row_start[:, ::group_rows, 0].astype(jnp.int32)
    off = jnp.pad(off, ((0, 0), (0, 1)), constant_values=per_step)

    me = my_row.astype(jnp.int32)[None]
    blocks = []
    own_coefs = []
    shard = []
    for step in range(steps):
        chosen, norm, own_coef, *more = compact(
            step, off, dest, *((centres, coefs) if step == 0 else shard), per_step, target_count
        )
        shard = more or shard
        own_coefs.append(own_coef)
        state = None
        for group in groups_of(row_devices, step):
            state = block_call(
                step == 0, me, group, [chunks[have] for have in group], chosen, norm, state,
                target_count, row_devices, sharpness, offset,
            )
        blocks.append(state)

    info = blocks[0][2]
    sums = blocks[0][1]
    total_change = None
    deltas = []
    for step in range(steps):
        if step > 0:
            bits = bits_of(row_devices)
            for first in range(0, len(bits), 2):
                low = share.astype(BF16)
                pair = bits[first : first + 2]
                for bit in pair + ([sum(pair)] if len(pair) > 1 else []):
                    share = share + swap(low, "rows", bit).astype(F32)
            moved = share if step == 1 else moved + share
            sums = gradient_call(moved, info, blocks[step][0], blocks[step][1], target_count)
        delta, total_change, *more = change_call(
            me, lax.all_gather(sums, "cent"), own_coefs[step], blocks[step][0], info,
            step == steps - 1, target_count, total_change,
        )
        share = more[0] if more else None
        deltas.append(delta)
    coef_now = coefs
    for step in reversed(range(steps)):
        coef_now = scatter_call(off, dest, coef_now, deltas[step], step)

    pieces = total_change
    bits = bits_of(row_devices)
    for first in range(0, len(bits), 2):
        pair = bits[first : first + 2]
        count = 2 ** len(pair)
        pieces = pieces.reshape(pieces.shape[0] // count, count, target_count, quarter)
        kept = pieces[:, 0]
        for k in range(1, count):
            kept = kept + swap(pieces[:, k], "rows", k * pair[0])
        pieces = kept
    own_change = pieces[0]
    full = lax.all_gather(own_change, "cent")
    full = full.transpose(1, 0, 2).reshape(target_count, rows_dev)
    return (coef_now, predictions + full)


def solution(mesh):
    in_specs = (
        P("rows", None),
        P("rows"),
        P(None, "rows"),
        P(None, "rows"),
        P("rows", None),
        P(None, "rows"),
        P(None, "cent"),
    )
    out_specs = (P(None, "rows"), P(None, "rows"))
    return jax.shard_map(local, mesh=mesh, in_specs=in_specs, out_specs=out_specs, check_vma=False)
```

```python
import functools
import math

import jax
import jax.numpy as jnp
from jax import lax
from jax.experimental import pallas as pl
from jax.experimental.pallas import tpu as pltpu
from jax.sharding import PartitionSpec as P

RIDGE = 1.0
LANES = 128
POOL_BLOCK = 256
WINDOW = 144
TILE = 512
FIRST_GROUPS = [(0, 1), (2, 4), (5, 6), (3, 7)]
LATER_GROUPS = [(0, 1), (2, 4), (5, 6), (3, 7)]
KERNEL_VMEM = 16 * 2**20
LOG2E = math.log2(math.e)
NT = (((1,), (1,)), ((), ()))
F32 = jnp.float32
BF16 = jnp.bfloat16


def split3(x):
    first = x.astype(BF16)
    rest = x - first.astype(F32)
    second = rest.astype(BF16)
    third = (rest - second.astype(F32)).astype(BF16)
    return first, second, third


def split3_outside(x):
    first = lax.reduce_precision(x, 8, 7)
    rest = x - first
    second = lax.reduce_precision(rest, 8, 7)
    third = rest - second
    return first.astype(BF16), second.astype(BF16), third.astype(BF16)


def round_up(value, multiple):
    return -(-value // multiple) * multiple


def in_vmem(count):
    return [pl.BlockSpec(memory_space=pltpu.VMEM)] * count


def in_hbm(x):
    return pltpu.with_memory_space_constraint(x, pltpu.HBM)


def held(x):
    return pltpu.with_memory_space_constraint(x, pltpu.VMEM)


def params():
    return pltpu.CompilerParams(vmem_limit_bytes=KERNEL_VMEM)


def two_rows(ref, step, block):
    row = 2 * block
    return jnp.concatenate([ref[step, pl.ds(row, 1), :], ref[step, pl.ds(row + 1, 1), :]], axis=1)


def pool_copy(source, target, half, block, done):
    at = pl.ds(pl.multiple_of(block * POOL_BLOCK, POOL_BLOCK), POOL_BLOCK)
    start = half * target.shape[0] + block * POOL_BLOCK
    start = pl.multiple_of(start, POOL_BLOCK)
    return pltpu.make_async_copy(source.at[pl.ds(start, POOL_BLOCK), :], target.at[at, :], done.at[block])


def load_kernel(targets, pool_hbm, coefs_hbm, pool_ref, parts_ref, coefs_ref, arrived, coefs_arrived):
    copies = [pool_copy(pool_hbm, pool_ref, 0, block, arrived) for block in range(arrived.shape[0])]
    coefs_copy = pltpu.make_async_copy(coefs_hbm, coefs_ref, coefs_arrived)
    coefs_copy.start()
    for copy in copies:
        copy.start()
    coefs_copy.wait()
    parts_ref[3 * targets :, :] = jnp.zeros((LANES - 3 * targets, parts_ref.shape[1]), BF16)
    for part, value in enumerate(split3(coefs_ref[...])):
        parts_ref[part * targets : (part + 1) * targets, :] = value
    for copy in copies:
        copy.wait()


def load_call(pool, coefs):
    return pl.pallas_call(
        functools.partial(load_kernel, coefs.shape[0]),
        name="load",
        in_specs=[pl.BlockSpec(memory_space=pltpu.HBM)] * 2,
        out_specs=in_vmem(2),
        out_shape=(
            pltpu.VMEM((pool.shape[0] // 2, pool.shape[1]), BF16),
            pltpu.VMEM((LANES, pool.shape[0]), BF16),
        ),
        scratch_shapes=[
            pltpu.VMEM(coefs.shape, F32),
            pltpu.SemaphoreType.DMA((pool.shape[0] // POOL_BLOCK // 2,)),
            pltpu.SemaphoreType.DMA,
        ],
        compiler_params=params(),
        cost_estimate=pl.CostEstimate(flops=10**6, bytes_accessed=3 * 10**6, transcendentals=0),
    )(in_hbm(pool), in_hbm(coefs))


def compact_kernel(step, per_step, targets, off_ref, dest_ref, *refs):
    loads = step == 0
    if loads:
        first_ref, parts_ref, pool_hbm, out_ref, norm_ref, coef_ref, second_ref, side_out, arrived = refs
    else:
        first_ref, second_ref, parts_ref, out_ref, norm_ref, coef_ref, side_out = refs
    features = out_ref.shape[1]
    half = first_ref.shape[0] // POOL_BLOCK
    blocks = 2 * half
    tile = math.gcd(per_step, 512)

    if loads:
        for block in range(half):
            pool_copy(pool_hbm, second_ref, 1, block, arrived).start()
    widest = 0
    for block in range(blocks):
        widest = jnp.maximum(widest, off_ref[step, block + 1] - (off_ref[step, block] // 16) * 16)
    narrow = widest <= WINDOW
    out_ref[:16, :] = jnp.zeros((16, features), BF16)
    side_out[:16, :] = jnp.zeros((16, LANES), BF16)

    def place(pool_ref, part, index, window):
        block = part * half + index
        base = pl.multiple_of((off_ref[step, block] // 16) * 16, 16)
        dest = two_rows(dest_ref, step, block) - base
        slots = lax.broadcasted_iota(jnp.int32, (window, POOL_BLOCK), 0)
        pick = jnp.where(slots == dest, 1.0, 0.0).astype(BF16)
        at = pl.ds(pl.multiple_of(block * POOL_BLOCK, POOL_BLOCK), POOL_BLOCK)
        inner = pl.ds(pl.multiple_of(index * POOL_BLOCK, POOL_BLOCK), POOL_BLOCK)
        after = pl.ds(pl.multiple_of(base + 16, 16), window - 16)
        packed = jnp.dot(pick, pool_ref[inner, :], preferred_element_type=F32).astype(BF16)
        side = lax.dot_general(pick, parts_ref[:, at], NT, preferred_element_type=F32).astype(BF16)
        for rows, target in ((packed, out_ref), (side, side_out)):
            target[pl.ds(base, 16), :] += rows[:16]
            target[after, :] = rows[16:]

    def walk(window, width):
        for part, pool_ref in enumerate((first_ref, second_ref)):

            @pl.loop(0, half // width)
            def _(group, part=part, pool_ref=pool_ref):
                if loads and part == 1:
                    for i in range(width):
                        pool_copy(pool_hbm, second_ref, 1, width * group + i, arrived).wait()
                for i in range(width):
                    place(pool_ref, part, width * group + i, window)

    @pl.when(narrow)
    def _():
        walk(WINDOW, 4)

    @pl.when(jnp.logical_not(narrow))
    def _():
        walk(POOL_BLOCK + 16, 1)

    ones = jnp.ones((8, features), BF16)
    eye = lax.broadcasted_iota(jnp.int32, (3 * targets, LANES), 0) == lax.broadcasted_iota(
        jnp.int32, (3 * targets, LANES), 1
    )
    eye = jnp.where(eye, 1.0, 0.0).astype(BF16)
    for first in range(0, per_step, tile):
        rows = out_ref[first : first + tile, :].astype(F32)
        square = rows * rows
        high = square.astype(BF16)
        low = (square - high.astype(F32)).astype(BF16)
        norm = lax.dot_general(ones, high, NT, preferred_element_type=F32)
        norm_ref[:, first : first + tile] = norm + lax.dot_general(ones, low, NT, preferred_element_type=F32)
        parts = lax.dot_general(eye, side_out[first : first + tile, :], NT, preferred_element_type=F32)
        coef_ref[:, first : first + tile] = (
            parts[:targets] + parts[targets : 2 * targets] + parts[2 * targets :]
        )


def compact(step, off, dest, pool, parts, pool_hbm, per_step, targets):
    features = pool_hbm.shape[1]
    length = round_up(per_step, 16) + POOL_BLOCK + 16
    outs = [
        pltpu.VMEM((length, features), BF16),
        pltpu.VMEM((8, per_step), F32),
        pltpu.VMEM((targets, per_step), F32),
    ]
    scratch = [pltpu.VMEM((length, LANES), BF16)]
    operands = [off, dest, *[held(half) for half in pool], held(parts)]
    specs = [pl.BlockSpec(memory_space=pltpu.SMEM), *in_vmem(len(operands) - 1)]
    if step == 0:
        half = pool[0].shape
        outs.append(pltpu.VMEM(half, BF16))
        scratch.append(pltpu.SemaphoreType.DMA((half[0] // POOL_BLOCK,)))
        specs.append(pl.BlockSpec(memory_space=pltpu.HBM))
        operands.append(in_hbm(pool_hbm))
    return pl.pallas_call(
        functools.partial(compact_kernel, step, per_step, targets),
        name="compact",
        in_specs=specs,
        out_specs=in_vmem(len(outs)),
        out_shape=tuple(outs),
        scratch_shapes=scratch,
        compiler_params=params(),
        cost_estimate=pl.CostEstimate(flops=2 * 10**9, bytes_accessed=6 * 10**6, transcendentals=0),
    )(*operands)


def block_kernel(first_step, targets, quarter, group, scale, offset, me_ref, chosen_ref, norm_ref, *refs):
    count = len(group)
    chunk_refs = refs[:count]
    outs = refs[count:]
    slots = [me_ref[0] ^ have for have in group]
    outs_count = 3 if first_step else 2
    sums_in = outs[1] if len(outs) > outs_count else None
    outs = outs[-outs_count:]
    k_ref, sums_ref = outs[:2]
    per_step = sums_ref.shape[1]
    square_row = targets if first_step else 0
    tile = math.gcd(per_step, TILE)

    rows = jnp.concatenate([ref[:quarter, :] for ref in chunk_refs], axis=0)
    wide_rows = rows.astype(F32)
    row_norm = jnp.sum(wide_rows * wide_rows, axis=1, keepdims=True) * (scale * LOG2E) - offset * LOG2E
    columns = []
    for i, ref in enumerate(chunk_refs):
        parts = ref[quarter : quarter + 3, quarter : 2 * quarter].astype(F32)
        weight = jnp.sum(parts, axis=0, keepdims=True)
        columns.append(jnp.transpose(jnp.broadcast_to(weight, (8, quarter)))[:, :1])
        if first_step:
            side_ref = outs[2]
            side_ref[slots[i], :targets, :] = ref[quarter : quarter + targets, :quarter].astype(F32)
            side_ref[slots[i], targets:, :] = jnp.broadcast_to(
                weight, (side_ref.shape[1] - targets, quarter)
            )
    weight_column = jnp.concatenate(columns, axis=0)
    weighted = jnp.concatenate([ref[quarter : quarter + targets, :quarter] for ref in chunk_refs], axis=1)

    for first in range(0, per_step, tile):
        dots = lax.dot_general(rows, chosen_ref[first : first + tile, :], NT, preferred_element_type=F32)
        centre = norm_ref[:1, first : first + tile] * (scale * LOG2E)
        k_low = jnp.exp2(dots * (2.0 * scale * LOG2E) - row_norm - centre).astype(BF16)
        for i in range(count):
            k_ref[slots[i], :, first : first + tile] = k_low[i * quarter : (i + 1) * quarter]
        wide = k_low.astype(F32)
        updates = [(square_row, 1, jnp.sum(weight_column * (wide * wide), axis=0, keepdims=True))]
        if first_step:
            updates.append((0, targets, jnp.dot(weighted, k_low, preferred_element_type=F32)))
        for row, size, value in updates:
            if sums_in is not None:
                value = value + sums_in[row : row + size, first : first + tile]
            sums_ref[row : row + size, first : first + tile] = value


def block_call(first_step, me, group, chunks, chosen, norm, state, targets, row_devices, scale, offset):
    features = chosen.shape[1]
    per_step = norm.shape[1]
    count = len(chunks)
    quarter = chunks[0].shape[0] - round_up(targets, 16)
    operands = [me, held(chosen), held(norm), *chunks]
    outs = [
        pltpu.VMEM((row_devices, quarter, per_step), BF16),
        pltpu.VMEM((round_up(targets + 1, 8) if first_step else 8, per_step), F32),
    ]
    if first_step:
        outs.append(pltpu.VMEM((row_devices, round_up(targets + 1, 8), quarter), F32))
    aliases = {}
    if state is not None:
        aliases = {len(operands) + i: i for i in range(len(outs))}
        operands += [held(x) for x in state]
    entries = count * quarter * per_step
    return pl.pallas_call(
        functools.partial(block_kernel, first_step, targets, quarter, group, scale, offset),
        name="kernel_block",
        in_specs=[pl.BlockSpec(memory_space=pltpu.SMEM)] + in_vmem(len(operands) - 1),
        out_specs=in_vmem(len(outs)),
        out_shape=tuple(outs),
        input_output_aliases=aliases,
        compiler_params=params(),
        cost_estimate=pl.CostEstimate(
            flops=2 * entries * features, bytes_accessed=2 * entries, transcendentals=entries
        ),
    )(*operands)


def pass_cost(k_step, targets):
    entries = math.prod(k_step.shape)
    return pl.CostEstimate(flops=2 * targets * entries, bytes_accessed=2 * entries, transcendentals=0)


def change_kernel(targets, first, last, me_ref, sums_ref, coef_ref, k_ref, side_ref, *refs):
    before_ref = None if first else refs[0]
    outs = list(refs if first else refs[1:])
    delta_ref, change_ref = outs[:2]
    total = sums_ref[0]
    for i in range(1, sums_ref.shape[0]):
        total = total + sums_ref[i]
    delta = (total[:targets] - RIDGE * coef_ref[...]) / (total[targets : targets + 1] + RIDGE)
    delta_ref[...] = delta
    low = delta.astype(BF16)

    def body(i, _):
        change = lax.dot_general(low, k_ref[i], NT, preferred_element_type=F32)
        relative = i ^ me_ref[0]
        if not last:
            outs[2][i] = change * side_ref[i, targets : targets + 1, :]
        change_ref[relative] = change if first else change + before_ref[relative]
        return 0

    lax.fori_loop(0, k_ref.shape[0], body, 0, unroll=2)


def change_call(me, sums, coef, k_step, side, last, targets, before=None):
    row_devices, quarter, per_step = k_step.shape
    operands = [me, sums, coef, held(k_step), side]
    if before is not None:
        operands.append(before)
    change = jax.ShapeDtypeStruct((row_devices, targets, quarter), F32)
    outs = (jax.ShapeDtypeStruct((targets, per_step), F32), change) + (() if last else (change,))
    return pl.pallas_call(
        functools.partial(change_kernel, targets, before is None, last),
        name="change",
        in_specs=[pl.BlockSpec(memory_space=pltpu.SMEM)] + in_vmem(len(operands) - 1),
        out_specs=in_vmem(len(outs)),
        out_shape=outs,
        compiler_params=params(),
        cost_estimate=pass_cost(k_step, targets),
    )(*operands)


def gradient_kernel(targets, moved_ref, side_ref, k_ref, square_ref, out_ref):
    out_ref[:targets, :] = jnp.zeros((targets, out_ref.shape[1]), F32)
    out_ref[targets : targets + 1, :] = square_ref[:1, :]

    def body(i, _):
        weighted = (side_ref[i, :targets, :] - moved_ref[i]).astype(BF16)
        out_ref[:targets, :] += jnp.dot(weighted, k_ref[i], preferred_element_type=F32)
        return 0

    lax.fori_loop(0, k_ref.shape[0], body, 0, unroll=2)


def gradient_call(moved, side, k_step, squares, targets):
    return pl.pallas_call(
        functools.partial(gradient_kernel, targets),
        name="gradient",
        in_specs=in_vmem(4),
        out_specs=in_vmem(1)[0],
        out_shape=jax.ShapeDtypeStruct((round_up(targets + 1, 8), k_step.shape[2]), F32),
        compiler_params=params(),
        cost_estimate=pass_cost(k_step, targets),
    )(moved, side, held(k_step), squares)


def scatter_kernel(targets, step, off_ref, dest_ref, coef_ref, delta_ref, out_ref, parts_ref):
    per_step = delta_ref.shape[1]
    blocks = out_ref.shape[1] // POOL_BLOCK
    window = POOL_BLOCK + LANES
    for part, value in enumerate(split3(delta_ref[...])):
        parts_ref[part * targets : (part + 1) * targets, :per_step] = value
    parts_ref[:, per_step:] = jnp.zeros((3 * targets, parts_ref.shape[1] - per_step), BF16)

    @pl.loop(0, blocks // 4)
    def _(four):
        for i in range(4):
            block = 4 * four + i
            columns = pl.ds(pl.multiple_of(block * POOL_BLOCK, POOL_BLOCK), POOL_BLOCK)
            base = pl.multiple_of((off_ref[step, block] // LANES) * LANES, LANES)
            dest = two_rows(dest_ref, step, block) - base
            slots = lax.broadcasted_iota(jnp.int32, (window, POOL_BLOCK), 0)
            pick = jnp.where(slots == dest, 1.0, 0.0).astype(BF16)
            moved = jnp.dot(parts_ref[:, pl.ds(base, window)], pick, preferred_element_type=F32)
            moved = moved[:targets] + moved[targets : 2 * targets] + moved[2 * targets :]
            out_ref[:, columns] = coef_ref[:, columns] + moved


def scatter_call(off, dest, coefs, delta, step):
    targets, per_step = delta.shape
    length = round_up(per_step, LANES) + POOL_BLOCK + LANES
    return pl.pallas_call(
        functools.partial(scatter_kernel, targets, step),
        name="scatter",
        in_specs=[pl.BlockSpec(memory_space=pltpu.SMEM)] + in_vmem(3),
        out_specs=in_vmem(1)[0],
        out_shape=jax.ShapeDtypeStruct(coefs.shape, F32),
        scratch_shapes=[pltpu.VMEM((3 * targets, length), BF16)],
        compiler_params=params(),
        cost_estimate=pl.CostEstimate(flops=10**9, bytes_accessed=10**6, transcendentals=0),
    )(off, dest, coefs, delta)


def swap(value, axis, bit):
    count = lax.axis_size(axis)
    return lax.ppermute(value, axis, [(i, i ^ bit) for i in range(count)])


def own_buffer(value):
    return lax.optimization_barrier(value + lax.optimization_barrier(jnp.zeros((), value.dtype)))


def bits_of(count):
    return [1 << k for k in range(count.bit_length() - 1)]


def last_hop(chunk, row_devices):
    return 2 if (chunk, row_devices) == (3, 8) else chunk & -chunk


def groups_of(row_devices, step):
    if row_devices == 8:
        return FIRST_GROUPS if step == 0 else LATER_GROUPS
    return [(have,) for have in range(row_devices)]


def local(samples, weights, targets, predictions, centres, coefs, block_index):
    rows_dev, features = samples.shape
    pool_dev = centres.shape[0]
    steps, slice_len = block_index.shape
    target_count = targets.shape[0]
    row_devices, cent_devices = lax.axis_size("rows"), lax.axis_size("cent")
    my_row, my_cent = lax.axis_index("rows"), lax.axis_index("cent")
    quarter = rows_dev // cent_devices
    per_step = slice_len * cent_devices // row_devices
    sharpness = 1.3 / math.sqrt(8.0 * features)
    offset = 2.0 * features * sharpness - 1.5 - 0.5 * math.log(rows_dev * row_devices)

    at = my_cent * quarter
    own_rows = lax.dynamic_slice_in_dim(samples, at, quarter, 0)
    own_weight = lax.dynamic_slice_in_dim(weights, at, quarter, 0)[None, :]
    own_target = lax.dynamic_slice_in_dim(targets, at, quarter, 1)
    own_pred = lax.dynamic_slice_in_dim(predictions, at, quarter, 1)
    weighted = (own_weight * (own_target - own_pred)).astype(BF16)
    side_count = round_up(target_count, 16)
    weight_parts = jnp.concatenate(split3_outside(own_weight), axis=0)
    side_block = jnp.concatenate(
        [
            jnp.pad(weighted, ((0, side_count - target_count), (0, 0))),
            jnp.pad(weight_parts, ((0, side_count - 3), (0, features - 2 * quarter))),
        ],
        axis=1,
    )
    chunks = {0: jnp.concatenate([own_rows, side_block], axis=0)}

    high_count = pool_dev // LANES
    place = block_index - my_row * pool_dev
    inside = (place >= 0) & (place < pool_dev)
    high = jnp.where(inside, place // LANES, -1)
    low = jnp.where(inside, place % LANES, 0)
    high_hot = (high[:, None, :] == jnp.arange(high_count)[None, :, None]).astype(BF16)
    low_hot = (low[:, None, :] == jnp.arange(LANES)[None, :, None]).astype(BF16)
    member = jnp.einsum("shl,sgl->shg", high_hot, low_hot, preferred_element_type=F32).astype(BF16)
    for bit in bits_of(cent_devices):
        member = member + swap(member, "cent", bit)

    for chunk in sorted(range(1, row_devices), key=lambda chunk: (bin(chunk).count("1"), chunk)):
        bit = last_hop(chunk, row_devices)
        source = chunks[chunk ^ bit]
        if bit == 1 and chunk ^ bit == row_devices // 2:
            source = own_buffer(source)
        chunks[chunk] = swap(source, "rows", bit)

    upper = (jnp.arange(LANES)[:, None] <= jnp.arange(LANES)[None, :]).astype(BF16)
    before = (jnp.arange(high_count)[:, None] > jnp.arange(high_count)[None, :]).astype(BF16)
    running = jnp.einsum("shg,gk->shk", member, upper, preferred_element_type=F32)
    row_count = running[:, :, -1:]
    row_start = jnp.einsum("hi,sik->shk", before, row_count.astype(BF16), preferred_element_type=F32)
    rank = row_start + running - 1.0
    dest = jnp.where(member > 0, rank, -65536.0).astype(jnp.int32)
    limits = jnp.arange(pool_dev // POOL_BLOCK + 1) * (POOL_BLOCK // LANES)
    earlier = (limits[:, None] > jnp.arange(high_count)[None, :]).astype(BF16)
    off = jnp.einsum("bi,sik->sb", earlier, row_count.astype(BF16), preferred_element_type=F32)
    off = off.astype(jnp.int32)

    me = my_row.astype(jnp.int32)[None]
    blocks = []
    own_coefs = []
    first_half, parts = load_call(centres, coefs)
    pool = [first_half]
    for step in range(steps):
        chosen, norm, own_coef, *more = compact(
            step, off, dest, pool, parts, centres, per_step, target_count
        )
        pool += more
        own_coefs.append(own_coef)
        state = None
        for group in groups_of(row_devices, step):
            state = block_call(
                step == 0, me, group, [chunks[have] for have in group], chosen, norm, state,
                target_count, row_devices, sharpness, offset,
            )
        blocks.append(state)

    info = blocks[0][2]
    sums = blocks[0][1]
    total_change = None
    deltas = []
    for step in range(steps):
        if step > 0:
            bits = bits_of(row_devices)
            for first in range(0, len(bits), 2):
                low = share.astype(BF16)
                pair = bits[first : first + 2]
                for bit in pair + ([sum(pair)] if len(pair) > 1 else []):
                    share = share + swap(low, "rows", bit).astype(F32)
            moved = share if step == 1 else moved + share
            sums = gradient_call(moved, info, blocks[step][0], blocks[step][1], target_count)
        delta, total_change, *more = change_call(
            me, lax.all_gather(sums, "cent"), own_coefs[step], blocks[step][0], info,
            step == steps - 1, target_count, total_change,
        )
        share = more[0] if more else None
        deltas.append(delta)
    coef_now = coefs
    for step in reversed(range(steps)):
        coef_now = scatter_call(off, dest, coef_now, deltas[step], step)

    pieces = total_change
    bits = bits_of(row_devices)
    for first in range(0, len(bits), 2):
        pair = bits[first : first + 2]
        count = 2 ** len(pair)
        pieces = pieces.reshape(pieces.shape[0] // count, count, target_count, quarter)
        kept = pieces[:, 0]
        for k in range(1, count):
            kept = kept + swap(pieces[:, k], "rows", k * pair[0])
        pieces = kept
    own_change = pieces[0]
    full = lax.all_gather(own_change, "cent")
    full = full.transpose(1, 0, 2).reshape(target_count, rows_dev)
    return (coef_now, predictions + full)


def solution(mesh):
    in_specs = (
        P("rows", None),
        P("rows"),
        P(None, "rows"),
        P(None, "rows"),
        P("rows", None),
        P(None, "rows"),
        P(None, "cent"),
    )
    out_specs = (P(None, "rows"), P(None, "rows"))
    return jax.shard_map(local, mesh=mesh, in_specs=in_specs, out_specs=out_specs, check_vma=False)
```

```python
import functools
import math

import jax
import jax.numpy as jnp
from jax import lax
from jax.experimental import pallas as pl
from jax.experimental.pallas import tpu as pltpu
from jax.sharding import PartitionSpec as P

RIDGE = 1.0
LANES = 128
POOL_BLOCK = 256
WINDOW = 144
TILE = 512
FIRST_GROUPS = [(0, 1), (2, 4), (5, 6), (3, 7)]
LATER_GROUPS = [(0, 1), (2, 4), (5, 6), (3, 7)]
KERNEL_VMEM = 16 * 2**20
LOG2E = math.log2(math.e)
NT = (((1,), (1,)), ((), ()))
F32 = jnp.float32
BF16 = jnp.bfloat16


def split3(x):
    first = x.astype(BF16)
    rest = x - first.astype(F32)
    second = rest.astype(BF16)
    third = (rest - second.astype(F32)).astype(BF16)
    return first, second, third


def split3_outside(x):
    first = lax.reduce_precision(x, 8, 7)
    rest = x - first
    second = lax.reduce_precision(rest, 8, 7)
    third = rest - second
    return first.astype(BF16), second.astype(BF16), third.astype(BF16)


def round_up(value, multiple):
    return -(-value // multiple) * multiple


def in_vmem(count):
    return [pl.BlockSpec(memory_space=pltpu.VMEM)] * count


def in_hbm(x):
    return pltpu.with_memory_space_constraint(x, pltpu.HBM)


def held(x):
    return pltpu.with_memory_space_constraint(x, pltpu.VMEM)


def params():
    return pltpu.CompilerParams(vmem_limit_bytes=KERNEL_VMEM)


def two_rows(ref, step, block):
    row = 2 * block
    return jnp.concatenate([ref[step, pl.ds(row, 1), :], ref[step, pl.ds(row + 1, 1), :]], axis=1)


def pool_copy(source, target, half, block, done):
    at = pl.ds(pl.multiple_of(block * POOL_BLOCK, POOL_BLOCK), POOL_BLOCK)
    start = half * target.shape[0] + block * POOL_BLOCK
    start = pl.multiple_of(start, POOL_BLOCK)
    return pltpu.make_async_copy(source.at[pl.ds(start, POOL_BLOCK), :], target.at[at, :], done.at[block])


def load_kernel(targets, pool_hbm, coefs_hbm, pool_ref, parts_ref, coefs_ref, arrived, coefs_arrived):
    copies = [pool_copy(pool_hbm, pool_ref, 0, block, arrived) for block in range(arrived.shape[0])]
    coefs_copy = pltpu.make_async_copy(coefs_hbm, coefs_ref, coefs_arrived)
    coefs_copy.start()
    for copy in copies:
        copy.start()
    coefs_copy.wait()
    parts_ref[3 * targets :, :] = jnp.zeros((LANES - 3 * targets, parts_ref.shape[1]), BF16)
    for part, value in enumerate(split3(coefs_ref[...])):
        parts_ref[part * targets : (part + 1) * targets, :] = value
    for copy in copies:
        copy.wait()


def load_call(pool, coefs):
    return pl.pallas_call(
        functools.partial(load_kernel, coefs.shape[0]),
        name="load",
        in_specs=[pl.BlockSpec(memory_space=pltpu.HBM)] * 2,
        out_specs=in_vmem(2),
        out_shape=(
            pltpu.VMEM((pool.shape[0] // 2, pool.shape[1]), BF16),
            pltpu.VMEM((LANES, pool.shape[0]), BF16),
        ),
        scratch_shapes=[
            pltpu.VMEM(coefs.shape, F32),
            pltpu.SemaphoreType.DMA((pool.shape[0] // POOL_BLOCK // 2,)),
            pltpu.SemaphoreType.DMA,
        ],
        compiler_params=params(),
        cost_estimate=pl.CostEstimate(flops=10**6, bytes_accessed=3 * 10**6, transcendentals=0),
    )(in_hbm(pool), in_hbm(coefs))


def compact_kernel(step, per_step, targets, off_ref, dest_ref, *refs):
    loads = step == 0
    if loads:
        first_ref, parts_ref, pool_hbm, out_ref, norm_ref, coef_ref, second_ref, side_out, arrived = refs
    else:
        first_ref, second_ref, parts_ref, out_ref, norm_ref, coef_ref, side_out = refs
    features = out_ref.shape[1]
    half = first_ref.shape[0] // POOL_BLOCK
    blocks = 2 * half
    tile = math.gcd(per_step, 512)

    if loads:
        for block in range(half):
            pool_copy(pool_hbm, second_ref, 1, block, arrived).start()
    widest = 0
    for block in range(blocks):
        widest = jnp.maximum(widest, off_ref[step, block + 1] - (off_ref[step, block] // 16) * 16)
    narrow = widest <= WINDOW
    out_ref[:16, :] = jnp.zeros((16, features), BF16)
    side_out[:16, :] = jnp.zeros((16, LANES), BF16)

    def place(pool_ref, part, index, window):
        block = part * half + index
        base = pl.multiple_of((off_ref[step, block] // 16) * 16, 16)
        dest = two_rows(dest_ref, step, block) - base
        slots = lax.broadcasted_iota(jnp.int32, (window, POOL_BLOCK), 0)
        pick = jnp.where(slots == dest, 1.0, 0.0).astype(BF16)
        at = pl.ds(pl.multiple_of(block * POOL_BLOCK, POOL_BLOCK), POOL_BLOCK)
        inner = pl.ds(pl.multiple_of(index * POOL_BLOCK, POOL_BLOCK), POOL_BLOCK)
        after = pl.ds(pl.multiple_of(base + 16, 16), window - 16)
        packed = jnp.dot(pick, pool_ref[inner, :], preferred_element_type=F32).astype(BF16)
        side = lax.dot_general(pick, parts_ref[:, at], NT, preferred_element_type=F32).astype(BF16)
        for rows, target in ((packed, out_ref), (side, side_out)):
            target[pl.ds(base, 16), :] += rows[:16]
            target[after, :] = rows[16:]

    def walk(window, width):
        for part, pool_ref in enumerate((first_ref, second_ref)):

            @pl.loop(0, half // width)
            def _(group, part=part, pool_ref=pool_ref):
                if loads and part == 1:
                    for i in range(width):
                        pool_copy(pool_hbm, second_ref, 1, width * group + i, arrived).wait()
                for i in range(width):
                    place(pool_ref, part, width * group + i, window)

    @pl.when(narrow)
    def _():
        walk(WINDOW, 4)

    @pl.when(jnp.logical_not(narrow))
    def _():
        walk(POOL_BLOCK + 16, 1)

    eye = lax.broadcasted_iota(jnp.int32, (3 * targets, LANES), 0) == lax.broadcasted_iota(
        jnp.int32, (3 * targets, LANES), 1
    )
    eye = jnp.where(eye, 1.0, 0.0).astype(BF16)
    for first in range(0, per_step, tile):
        rows = out_ref[first : first + tile, :].astype(F32)
        square = rows * rows
        narrow_sum = square[:, :LANES]
        for lane in range(LANES, features, LANES):
            narrow_sum = narrow_sum + square[:, lane : lane + LANES]
        norm = jnp.sum(jnp.transpose(narrow_sum), axis=0, keepdims=True)
        norm_ref[:, first : first + tile] = jnp.broadcast_to(norm, (8, tile))
        parts = lax.dot_general(eye, side_out[first : first + tile, :], NT, preferred_element_type=F32)
        coef_ref[:, first : first + tile] = (
            parts[:targets] + parts[targets : 2 * targets] + parts[2 * targets :]
        )


def compact(step, off, dest, pool, parts, pool_hbm, per_step, targets):
    features = pool_hbm.shape[1]
    length = round_up(per_step, 16) + POOL_BLOCK + 16
    outs = [
        pltpu.VMEM((length, features), BF16),
        pltpu.VMEM((8, per_step), F32),
        pltpu.VMEM((targets, per_step), F32),
    ]
    scratch = [pltpu.VMEM((length, LANES), BF16)]
    operands = [off, dest, *[held(half) for half in pool], held(parts)]
    specs = [pl.BlockSpec(memory_space=pltpu.SMEM), *in_vmem(len(operands) - 1)]
    if step == 0:
        half = pool[0].shape
        outs.append(pltpu.VMEM(half, BF16))
        scratch.append(pltpu.SemaphoreType.DMA((half[0] // POOL_BLOCK,)))
        specs.append(pl.BlockSpec(memory_space=pltpu.HBM))
        operands.append(in_hbm(pool_hbm))
    return pl.pallas_call(
        functools.partial(compact_kernel, step, per_step, targets),
        name="compact",
        in_specs=specs,
        out_specs=in_vmem(len(outs)),
        out_shape=tuple(outs),
        scratch_shapes=scratch,
        compiler_params=params(),
        cost_estimate=pl.CostEstimate(flops=2 * 10**9, bytes_accessed=6 * 10**6, transcendentals=0),
    )(*operands)


def block_kernel(first_step, targets, quarter, group, scale, offset, me_ref, chosen_ref, norm_ref, *refs):
    count = len(group)
    chunk_refs = refs[:count]
    outs = refs[count:]
    slots = [me_ref[0] ^ have for have in group]
    outs_count = 3 if first_step else 2
    sums_in = outs[1] if len(outs) > outs_count else None
    outs = outs[-outs_count:]
    k_ref, sums_ref = outs[:2]
    per_step = sums_ref.shape[1]
    square_row = targets if first_step else 0
    tile = math.gcd(per_step, TILE)

    rows = jnp.concatenate([ref[:quarter, :] for ref in chunk_refs], axis=0)
    wide_rows = rows.astype(F32)
    row_norm = jnp.sum(wide_rows * wide_rows, axis=1, keepdims=True) * (scale * LOG2E) - offset * LOG2E
    columns = []
    for i, ref in enumerate(chunk_refs):
        parts = ref[quarter : quarter + 3, quarter : 2 * quarter].astype(F32)
        weight = jnp.sum(parts, axis=0, keepdims=True)
        columns.append(jnp.transpose(jnp.broadcast_to(weight, (8, quarter)))[:, :1])
        if first_step:
            side_ref = outs[2]
            side_ref[slots[i], :targets, :] = ref[quarter : quarter + targets, :quarter].astype(F32)
            side_ref[slots[i], targets:, :] = jnp.broadcast_to(
                weight, (side_ref.shape[1] - targets, quarter)
            )
    weight_column = jnp.concatenate(columns, axis=0)
    weighted = jnp.concatenate([ref[quarter : quarter + targets, :quarter] for ref in chunk_refs], axis=1)

    for first in range(0, per_step, tile):
        dots = lax.dot_general(rows, chosen_ref[first : first + tile, :], NT, preferred_element_type=F32)
        centre = norm_ref[:1, first : first + tile] * (scale * LOG2E)
        k_low = jnp.exp2(dots * (2.0 * scale * LOG2E) - row_norm - centre).astype(BF16)
        for i in range(count):
            k_ref[slots[i], :, first : first + tile] = k_low[i * quarter : (i + 1) * quarter]
        wide = k_low.astype(F32)
        updates = [(square_row, 1, jnp.sum(weight_column * (wide * wide), axis=0, keepdims=True))]
        if first_step:
            updates.append((0, targets, jnp.dot(weighted, k_low, preferred_element_type=F32)))
        for row, size, value in updates:
            if sums_in is not None:
                value = value + sums_in[row : row + size, first : first + tile]
            sums_ref[row : row + size, first : first + tile] = value


def block_call(first_step, me, group, chunks, chosen, norm, state, targets, row_devices, scale, offset):
    features = chosen.shape[1]
    per_step = norm.shape[1]
    count = len(chunks)
    quarter = chunks[0].shape[0] - round_up(targets, 16)
    operands = [me, held(chosen), held(norm), *chunks]
    outs = [
        pltpu.VMEM((row_devices, quarter, per_step), BF16),
        pltpu.VMEM((round_up(targets + 1, 8) if first_step else 8, per_step), F32),
    ]
    if first_step:
        outs.append(pltpu.VMEM((row_devices, round_up(targets + 1, 8), quarter), F32))
    aliases = {}
    if state is not None:
        aliases = {len(operands) + i: i for i in range(len(outs))}
        operands += [held(x) for x in state]
    entries = count * quarter * per_step
    return pl.pallas_call(
        functools.partial(block_kernel, first_step, targets, quarter, group, scale, offset),
        name="kernel_block",
        in_specs=[pl.BlockSpec(memory_space=pltpu.SMEM)] + in_vmem(len(operands) - 1),
        out_specs=in_vmem(len(outs)),
        out_shape=tuple(outs),
        input_output_aliases=aliases,
        compiler_params=params(),
        cost_estimate=pl.CostEstimate(
            flops=2 * entries * features, bytes_accessed=2 * entries, transcendentals=entries
        ),
    )(*operands)


def pass_cost(k_step, targets):
    entries = math.prod(k_step.shape)
    return pl.CostEstimate(flops=2 * targets * entries, bytes_accessed=2 * entries, transcendentals=0)


def change_kernel(targets, first, last, me_ref, sums_ref, coef_ref, k_ref, side_ref, *refs):
    before_ref = None if first else refs[0]
    outs = list(refs if first else refs[1:])
    delta_ref, change_ref = outs[:2]
    total = sums_ref[0]
    for i in range(1, sums_ref.shape[0]):
        total = total + sums_ref[i]
    delta = (total[:targets] - RIDGE * coef_ref[...]) / (total[targets : targets + 1] + RIDGE)
    delta_ref[...] = delta
    low = delta.astype(BF16)

    def body(i, _):
        change = lax.dot_general(low, k_ref[i], NT, preferred_element_type=F32)
        relative = i ^ me_ref[0]
        if not last:
            outs[2][i] = change * side_ref[i, targets : targets + 1, :]
        change_ref[relative] = change if first else change + before_ref[relative]
        return 0

    lax.fori_loop(0, k_ref.shape[0], body, 0, unroll=2)


def change_call(me, sums, coef, k_step, side, last, targets, before=None):
    row_devices, quarter, per_step = k_step.shape
    operands = [me, sums, coef, held(k_step), side]
    if before is not None:
        operands.append(before)
    change = jax.ShapeDtypeStruct((row_devices, targets, quarter), F32)
    outs = (jax.ShapeDtypeStruct((targets, per_step), F32), change) + (() if last else (change,))
    return pl.pallas_call(
        functools.partial(change_kernel, targets, before is None, last),
        name="change",
        in_specs=[pl.BlockSpec(memory_space=pltpu.SMEM)] + in_vmem(len(operands) - 1),
        out_specs=in_vmem(len(outs)),
        out_shape=outs,
        compiler_params=params(),
        cost_estimate=pass_cost(k_step, targets),
    )(*operands)


def gradient_kernel(targets, moved_ref, side_ref, k_ref, square_ref, out_ref):
    out_ref[:targets, :] = jnp.zeros((targets, out_ref.shape[1]), F32)
    out_ref[targets : targets + 1, :] = square_ref[:1, :]

    def body(i, _):
        weighted = (side_ref[i, :targets, :] - moved_ref[i]).astype(BF16)
        out_ref[:targets, :] += jnp.dot(weighted, k_ref[i], preferred_element_type=F32)
        return 0

    lax.fori_loop(0, k_ref.shape[0], body, 0, unroll=2)


def gradient_call(moved, side, k_step, squares, targets):
    return pl.pallas_call(
        functools.partial(gradient_kernel, targets),
        name="gradient",
        in_specs=in_vmem(4),
        out_specs=in_vmem(1)[0],
        out_shape=jax.ShapeDtypeStruct((round_up(targets + 1, 8), k_step.shape[2]), F32),
        compiler_params=params(),
        cost_estimate=pass_cost(k_step, targets),
    )(moved, side, held(k_step), squares)


def scatter_kernel(targets, step, off_ref, dest_ref, coef_ref, delta_ref, out_ref, parts_ref):
    per_step = delta_ref.shape[1]
    blocks = out_ref.shape[1] // POOL_BLOCK
    window = POOL_BLOCK + LANES
    for part, value in enumerate(split3(delta_ref[...])):
        parts_ref[part * targets : (part + 1) * targets, :per_step] = value
    parts_ref[:, per_step:] = jnp.zeros((3 * targets, parts_ref.shape[1] - per_step), BF16)

    @pl.loop(0, blocks // 4)
    def _(four):
        for i in range(4):
            block = 4 * four + i
            columns = pl.ds(pl.multiple_of(block * POOL_BLOCK, POOL_BLOCK), POOL_BLOCK)
            base = pl.multiple_of((off_ref[step, block] // LANES) * LANES, LANES)
            dest = two_rows(dest_ref, step, block) - base
            slots = lax.broadcasted_iota(jnp.int32, (window, POOL_BLOCK), 0)
            pick = jnp.where(slots == dest, 1.0, 0.0).astype(BF16)
            moved = jnp.dot(parts_ref[:, pl.ds(base, window)], pick, preferred_element_type=F32)
            moved = moved[:targets] + moved[targets : 2 * targets] + moved[2 * targets :]
            out_ref[:, columns] = coef_ref[:, columns] + moved


def scatter_call(off, dest, coefs, delta, step):
    targets, per_step = delta.shape
    length = round_up(per_step, LANES) + POOL_BLOCK + LANES
    return pl.pallas_call(
        functools.partial(scatter_kernel, targets, step),
        name="scatter",
        in_specs=[pl.BlockSpec(memory_space=pltpu.SMEM)] + in_vmem(3),
        out_specs=in_vmem(1)[0],
        out_shape=jax.ShapeDtypeStruct(coefs.shape, F32),
        scratch_shapes=[pltpu.VMEM((3 * targets, length), BF16)],
        compiler_params=params(),
        cost_estimate=pl.CostEstimate(flops=10**9, bytes_accessed=10**6, transcendentals=0),
    )(off, dest, coefs, delta)


def swap(value, axis, bit):
    count = lax.axis_size(axis)
    return lax.ppermute(value, axis, [(i, i ^ bit) for i in range(count)])


def own_buffer(value):
    return lax.optimization_barrier(value + lax.optimization_barrier(jnp.zeros((), value.dtype)))


def bits_of(count):
    return [1 << k for k in range(count.bit_length() - 1)]


def last_hop(chunk, row_devices):
    return 2 if (chunk, row_devices) == (3, 8) else chunk & -chunk


def groups_of(row_devices, step):
    if row_devices == 8:
        return FIRST_GROUPS if step == 0 else LATER_GROUPS
    return [(have,) for have in range(row_devices)]


def local(samples, weights, targets, predictions, centres, coefs, block_index):
    rows_dev, features = samples.shape
    pool_dev = centres.shape[0]
    steps, slice_len = block_index.shape
    target_count = targets.shape[0]
    row_devices, cent_devices = lax.axis_size("rows"), lax.axis_size("cent")
    my_row, my_cent = lax.axis_index("rows"), lax.axis_index("cent")
    quarter = rows_dev // cent_devices
    per_step = slice_len * cent_devices // row_devices
    sharpness = 1.3 / math.sqrt(8.0 * features)
    offset = 2.0 * features * sharpness - 1.5 - 0.5 * math.log(rows_dev * row_devices)

    at = my_cent * quarter
    own_rows = lax.dynamic_slice_in_dim(samples, at, quarter, 0)
    own_weight = lax.dynamic_slice_in_dim(weights, at, quarter, 0)[None, :]
    own_target = lax.dynamic_slice_in_dim(targets, at, quarter, 1)
    own_pred = lax.dynamic_slice_in_dim(predictions, at, quarter, 1)
    weighted = (own_weight * (own_target - own_pred)).astype(BF16)
    side_count = round_up(target_count, 16)
    weight_parts = jnp.concatenate(split3_outside(own_weight), axis=0)
    side_block = jnp.concatenate(
        [
            jnp.pad(weighted, ((0, side_count - target_count), (0, 0))),
            jnp.pad(weight_parts, ((0, side_count - 3), (0, features - 2 * quarter))),
        ],
        axis=1,
    )
    chunks = {0: jnp.concatenate([own_rows, side_block], axis=0)}

    high_count = pool_dev // LANES
    place = block_index - my_row * pool_dev
    inside = (place >= 0) & (place < pool_dev)
    high = jnp.where(inside, place // LANES, -1)
    low = jnp.where(inside, place % LANES, 0)
    high_hot = (high[:, None, :] == jnp.arange(high_count)[None, :, None]).astype(BF16)
    low_hot = (low[:, None, :] == jnp.arange(LANES)[None, :, None]).astype(BF16)
    member = jnp.einsum("shl,sgl->shg", high_hot, low_hot, preferred_element_type=F32).astype(BF16)
    for bit in bits_of(cent_devices):
        member = member + swap(member, "cent", bit)

    for chunk in sorted(range(1, row_devices), key=lambda chunk: (bin(chunk).count("1"), chunk)):
        bit = last_hop(chunk, row_devices)
        source = chunks[chunk ^ bit]
        if bit == 1 and chunk ^ bit == row_devices // 2:
            source = own_buffer(source)
        chunks[chunk] = swap(source, "rows", bit)

    upper = (jnp.arange(LANES)[:, None] <= jnp.arange(LANES)[None, :]).astype(BF16)
    before = (jnp.arange(high_count)[:, None] > jnp.arange(high_count)[None, :]).astype(BF16)
    running = jnp.einsum("shg,gk->shk", member, upper, preferred_element_type=F32)
    row_count = running[:, :, -1:]
    row_start = jnp.einsum("hi,sik->shk", before, row_count.astype(BF16), preferred_element_type=F32)
    rank = row_start + running - 1.0
    dest = jnp.where(member > 0, rank, -65536.0).astype(jnp.int32)
    limits = jnp.arange(pool_dev // POOL_BLOCK + 1) * (POOL_BLOCK // LANES)
    earlier = (limits[:, None] > jnp.arange(high_count)[None, :]).astype(BF16)
    off = jnp.einsum("bi,sik->sb", earlier, row_count.astype(BF16), preferred_element_type=F32)
    off = off.astype(jnp.int32)

    me = my_row.astype(jnp.int32)[None]
    blocks = []
    own_coefs = []
    first_half, parts = load_call(centres, coefs)
    pool = [first_half]
    for step in range(steps):
        chosen, norm, own_coef, *more = compact(
            step, off, dest, pool, parts, centres, per_step, target_count
        )
        pool += more
        own_coefs.append(own_coef)
        state = None
        for group in groups_of(row_devices, step):
            state = block_call(
                step == 0, me, group, [chunks[have] for have in group], chosen, norm, state,
                target_count, row_devices, sharpness, offset,
            )
        blocks.append(state)

    info = blocks[0][2]
    sums = blocks[0][1]
    total_change = None
    deltas = []
    for step in range(steps):
        if step > 0:
            bits = bits_of(row_devices)
            for first in range(0, len(bits), 2):
                low = share.astype(BF16)
                pair = bits[first : first + 2]
                for bit in pair + ([sum(pair)] if len(pair) > 1 else []):
                    share = share + swap(low, "rows", bit).astype(F32)
            moved = share if step == 1 else moved + share
            sums = gradient_call(moved, info, blocks[step][0], blocks[step][1], target_count)
        delta, total_change, *more = change_call(
            me, lax.all_gather(sums, "cent"), own_coefs[step], blocks[step][0], info,
            step == steps - 1, target_count, total_change,
        )
        share = more[0] if more else None
        deltas.append(delta)
    coef_now = coefs
    for step in reversed(range(steps)):
        coef_now = scatter_call(off, dest, coef_now, deltas[step], step)

    pieces = total_change
    bits = bits_of(row_devices)
    for first in range(0, len(bits), 2):
        pair = bits[first : first + 2]
        count = 2 ** len(pair)
        pieces = pieces.reshape(pieces.shape[0] // count, count, target_count, quarter)
        kept = pieces[:, 0]
        for k in range(1, count):
            kept = kept + swap(pieces[:, k], "rows", k * pair[0])
        pieces = kept
    own_change = pieces[0]
    full = lax.all_gather(own_change, "cent")
    full = full.transpose(1, 0, 2).reshape(target_count, rows_dev)
    return (coef_now, predictions + full)


def solution(mesh):
    in_specs = (
        P("rows", None),
        P("rows"),
        P(None, "rows"),
        P(None, "rows"),
        P("rows", None),
        P(None, "rows"),
        P(None, "cent"),
    )
    out_specs = (P(None, "rows"), P(None, "rows"))
    return jax.shard_map(local, mesh=mesh, in_specs=in_specs, out_specs=out_specs, check_vma=False)
```

```python
import functools
import math

import jax
import jax.numpy as jnp
from jax import lax
from jax.experimental import pallas as pl
from jax.experimental.pallas import tpu as pltpu
from jax.sharding import PartitionSpec as P

RIDGE = 1.0
LANES = 128
POOL_BLOCK = 256
WINDOW = 144
TILE = 512
FIRST_GROUPS = [(0, 1), (2, 4), (5, 6), (3, 7)]
LATER_GROUPS = [(0, 1), (2, 4), (5, 6), (3, 7)]
KERNEL_VMEM = 16 * 2**20
LOG2E = math.log2(math.e)
NT = (((1,), (1,)), ((), ()))
F32 = jnp.float32
BF16 = jnp.bfloat16


def split3(x):
    first = x.astype(BF16)
    rest = x - first.astype(F32)
    second = rest.astype(BF16)
    third = (rest - second.astype(F32)).astype(BF16)
    return first, second, third


def split3_outside(x):
    first = lax.reduce_precision(x, 8, 7)
    rest = x - first
    second = lax.reduce_precision(rest, 8, 7)
    third = rest - second
    return first.astype(BF16), second.astype(BF16), third.astype(BF16)


def round_up(value, multiple):
    return -(-value // multiple) * multiple


def in_vmem(count):
    return [pl.BlockSpec(memory_space=pltpu.VMEM)] * count


def in_hbm(x):
    return pltpu.with_memory_space_constraint(x, pltpu.HBM)


def held(x):
    return pltpu.with_memory_space_constraint(x, pltpu.VMEM)


def params():
    return pltpu.CompilerParams(vmem_limit_bytes=KERNEL_VMEM)


def two_rows(ref, step, block):
    row = 2 * block
    return jnp.concatenate([ref[step, pl.ds(row, 1), :], ref[step, pl.ds(row + 1, 1), :]], axis=1)


def pool_copy(source, target, half, block, done):
    at = pl.ds(pl.multiple_of(block * POOL_BLOCK, POOL_BLOCK), POOL_BLOCK)
    start = half * target.shape[0] + block * POOL_BLOCK
    start = pl.multiple_of(start, POOL_BLOCK)
    return pltpu.make_async_copy(source.at[pl.ds(start, POOL_BLOCK), :], target.at[at, :], done.at[block])


def load_kernel(targets, pool_hbm, coefs_hbm, pool_ref, parts_ref, coefs_ref, arrived, coefs_arrived):
    copies = [pool_copy(pool_hbm, pool_ref, 0, block, arrived) for block in range(arrived.shape[0])]
    coefs_copy = pltpu.make_async_copy(coefs_hbm, coefs_ref, coefs_arrived)
    coefs_copy.start()
    for copy in copies:
        copy.start()
    coefs_copy.wait()
    parts_ref[3 * targets :, :] = jnp.zeros((LANES - 3 * targets, parts_ref.shape[1]), BF16)
    for part, value in enumerate(split3(coefs_ref[...])):
        parts_ref[part * targets : (part + 1) * targets, :] = value
    for copy in copies:
        copy.wait()


def load_call(pool, coefs):
    return pl.pallas_call(
        functools.partial(load_kernel, coefs.shape[0]),
        name="load",
        in_specs=[pl.BlockSpec(memory_space=pltpu.HBM)] * 2,
        out_specs=in_vmem(2),
        out_shape=(
            pltpu.VMEM((pool.shape[0] // 2, pool.shape[1]), BF16),
            pltpu.VMEM((LANES, pool.shape[0]), BF16),
        ),
        scratch_shapes=[
            pltpu.VMEM(coefs.shape, F32),
            pltpu.SemaphoreType.DMA((pool.shape[0] // POOL_BLOCK // 2,)),
            pltpu.SemaphoreType.DMA,
        ],
        compiler_params=params(),
        cost_estimate=pl.CostEstimate(flops=10**6, bytes_accessed=3 * 10**6, transcendentals=0),
    )(in_hbm(pool), in_hbm(coefs))


def compact_kernel(step, per_step, targets, off_ref, dest_ref, *refs):
    loads = step == 0
    if loads:
        first_ref, parts_ref, pool_hbm, out_ref, norm_ref, coef_ref, second_ref, side_out, arrived = refs
    else:
        first_ref, second_ref, parts_ref, out_ref, norm_ref, coef_ref, side_out = refs
    features = out_ref.shape[1]
    half = first_ref.shape[0] // POOL_BLOCK
    blocks = 2 * half
    tile = math.gcd(per_step, 512)

    if loads:
        for block in range(half):
            pool_copy(pool_hbm, second_ref, 1, block, arrived).start()
    widest = 0
    for block in range(blocks):
        widest = jnp.maximum(widest, off_ref[step, block + 1] - (off_ref[step, block] // 16) * 16)
    narrow = widest <= WINDOW
    out_ref[:16, :] = jnp.zeros((16, features), BF16)
    side_out[:16, :] = jnp.zeros((16, LANES), BF16)

    def place(pool_ref, part, index, window):
        block = part * half + index
        base = pl.multiple_of((off_ref[step, block] // 16) * 16, 16)
        dest = two_rows(dest_ref, step, block) - base
        slots = lax.broadcasted_iota(jnp.int32, (window, POOL_BLOCK), 0)
        pick = jnp.where(slots == dest, 1.0, 0.0).astype(BF16)
        at = pl.ds(pl.multiple_of(block * POOL_BLOCK, POOL_BLOCK), POOL_BLOCK)
        inner = pl.ds(pl.multiple_of(index * POOL_BLOCK, POOL_BLOCK), POOL_BLOCK)
        after = pl.ds(pl.multiple_of(base + 16, 16), window - 16)
        packed = jnp.dot(pick, pool_ref[inner, :], preferred_element_type=F32).astype(BF16)
        side = lax.dot_general(pick, parts_ref[:, at], NT, preferred_element_type=F32).astype(BF16)
        for rows, target in ((packed, out_ref), (side, side_out)):
            target[pl.ds(base, 16), :] += rows[:16]
            target[after, :] = rows[16:]

    def walk(window, width):
        for part, pool_ref in enumerate((first_ref, second_ref)):

            @pl.loop(0, half // width)
            def _(group, part=part, pool_ref=pool_ref):
                if loads and part == 1:
                    for i in range(width):
                        pool_copy(pool_hbm, second_ref, 1, width * group + i, arrived).wait()
                for i in range(width):
                    place(pool_ref, part, width * group + i, window)

    @pl.when(narrow)
    def _():
        walk(WINDOW, 4)

    @pl.when(jnp.logical_not(narrow))
    def _():
        walk(POOL_BLOCK + 16, 1)

    eye = lax.broadcasted_iota(jnp.int32, (3 * targets, LANES), 0) == lax.broadcasted_iota(
        jnp.int32, (3 * targets, LANES), 1
    )
    eye = jnp.where(eye, 1.0, 0.0).astype(BF16)
    for first in range(0, per_step, tile):
        rows = out_ref[first : first + tile, :].astype(F32)
        square = rows * rows
        narrow_sum = square[:, :LANES]
        for lane in range(LANES, features, LANES):
            narrow_sum = narrow_sum + square[:, lane : lane + LANES]
        norm = jnp.sum(jnp.transpose(narrow_sum), axis=0, keepdims=True)
        norm_ref[:, first : first + tile] = jnp.broadcast_to(norm, (8, tile))
        parts = lax.dot_general(eye, side_out[first : first + tile, :], NT, preferred_element_type=F32)
        coef_ref[:, first : first + tile] = (
            parts[:targets] + parts[targets : 2 * targets] + parts[2 * targets :]
        )


def compact(step, off, dest, pool, parts, pool_hbm, per_step, targets):
    features = pool_hbm.shape[1]
    length = round_up(per_step, 16) + POOL_BLOCK + 16
    outs = [
        pltpu.VMEM((length, features), BF16),
        pltpu.VMEM((8, per_step), F32),
        pltpu.VMEM((targets, per_step), F32),
    ]
    scratch = [pltpu.VMEM((length, LANES), BF16)]
    operands = [off, dest, *[held(half) for half in pool], held(parts)]
    specs = [pl.BlockSpec(memory_space=pltpu.SMEM), *in_vmem(len(operands) - 1)]
    if step == 0:
        half = pool[0].shape
        outs.append(pltpu.VMEM(half, BF16))
        scratch.append(pltpu.SemaphoreType.DMA((half[0] // POOL_BLOCK,)))
        specs.append(pl.BlockSpec(memory_space=pltpu.HBM))
        operands.append(in_hbm(pool_hbm))
    return pl.pallas_call(
        functools.partial(compact_kernel, step, per_step, targets),
        name="compact",
        in_specs=specs,
        out_specs=in_vmem(len(outs)),
        out_shape=tuple(outs),
        scratch_shapes=scratch,
        compiler_params=params(),
        cost_estimate=pl.CostEstimate(flops=2 * 10**9, bytes_accessed=6 * 10**6, transcendentals=0),
    )(*operands)


def block_kernel(first_step, targets, quarter, group, scale, offset, me_ref, chosen_ref, norm_ref, *refs):
    count = len(group)
    chunk_refs = refs[:count]
    outs = refs[count:]
    slots = [me_ref[0] ^ have for have in group]
    outs_count = 3 if first_step else 2
    sums_in = outs[1] if len(outs) > outs_count else None
    outs = outs[-outs_count:]
    k_ref, sums_ref = outs[:2]
    per_step = sums_ref.shape[1]
    square_row = targets if first_step else 0
    tile = math.gcd(per_step, TILE)

    rows = jnp.concatenate([ref[:quarter, :] for ref in chunk_refs], axis=0)
    wide_rows = rows.astype(F32)
    row_norm = jnp.sum(wide_rows * wide_rows, axis=1, keepdims=True) * (scale * LOG2E) - offset * LOG2E
    columns = []
    for i, ref in enumerate(chunk_refs):
        parts = ref[quarter : quarter + 3, quarter : 2 * quarter].astype(F32)
        weight = jnp.sum(parts, axis=0, keepdims=True)
        columns.append(jnp.transpose(jnp.broadcast_to(weight, (8, quarter)))[:, :1])
        if first_step:
            side_ref = outs[2]
            side_ref[slots[i], :targets, :] = ref[quarter : quarter + targets, :quarter].astype(F32)
            side_ref[slots[i], targets:, :] = jnp.broadcast_to(
                weight, (side_ref.shape[1] - targets, quarter)
            )
    weight_column = jnp.concatenate(columns, axis=0)
    weighted = jnp.concatenate([ref[quarter : quarter + targets, :quarter] for ref in chunk_refs], axis=1)

    for first in range(0, per_step, tile):
        dots = lax.dot_general(rows, chosen_ref[first : first + tile, :], NT, preferred_element_type=F32)
        centre = norm_ref[:1, first : first + tile] * (scale * LOG2E)
        k_low = jnp.exp2(dots * (2.0 * scale * LOG2E) - row_norm - centre).astype(BF16)
        for i in range(count):
            k_ref[slots[i], :, first : first + tile] = k_low[i * quarter : (i + 1) * quarter]
        wide = k_low.astype(F32)
        updates = [(square_row, 1, jnp.sum(weight_column * (wide * wide), axis=0, keepdims=True))]
        if first_step:
            updates.append((0, targets, jnp.dot(weighted, k_low, preferred_element_type=F32)))
        for row, size, value in updates:
            if sums_in is not None:
                value = value + sums_in[row : row + size, first : first + tile]
            sums_ref[row : row + size, first : first + tile] = value


def block_call(first_step, me, group, chunks, chosen, norm, state, targets, row_devices, scale, offset):
    features = chosen.shape[1]
    per_step = norm.shape[1]
    count = len(chunks)
    quarter = chunks[0].shape[0] - round_up(targets, 16)
    operands = [me, held(chosen), held(norm), *chunks]
    outs = [
        pltpu.VMEM((row_devices, quarter, per_step), BF16),
        pltpu.VMEM((round_up(targets + 1, 8) if first_step else 8, per_step), F32),
    ]
    if first_step:
        outs.append(pltpu.VMEM((row_devices, round_up(targets + 1, 8), quarter), F32))
    aliases = {}
    if state is not None:
        aliases = {len(operands) + i: i for i in range(len(outs))}
        operands += [held(x) for x in state]
    entries = count * quarter * per_step
    return pl.pallas_call(
        functools.partial(block_kernel, first_step, targets, quarter, group, scale, offset),
        name="kernel_block",
        in_specs=[pl.BlockSpec(memory_space=pltpu.SMEM)] + in_vmem(len(operands) - 1),
        out_specs=in_vmem(len(outs)),
        out_shape=tuple(outs),
        input_output_aliases=aliases,
        compiler_params=params(),
        cost_estimate=pl.CostEstimate(
            flops=2 * entries * features, bytes_accessed=2 * entries, transcendentals=entries
        ),
    )(*operands)


def pass_cost(k_step, targets):
    entries = math.prod(k_step.shape)
    return pl.CostEstimate(flops=2 * targets * entries, bytes_accessed=2 * entries, transcendentals=0)


def change_kernel(targets, first, last, me_ref, sums_ref, coef_ref, k_ref, side_ref, *refs):
    before_ref = None if first else refs[0]
    outs = list(refs if first else refs[1:])
    delta_ref, change_ref = outs[:2]
    total = sums_ref[0]
    for i in range(1, sums_ref.shape[0]):
        total = total + sums_ref[i]
    delta = (total[:targets] - RIDGE * coef_ref[...]) / (total[targets : targets + 1] + RIDGE)
    delta_ref[...] = delta
    low = delta.astype(BF16)

    def body(i, _):
        change = lax.dot_general(low, k_ref[i], NT, preferred_element_type=F32)
        relative = i ^ me_ref[0]
        if not last:
            outs[2][i] = change * side_ref[i, targets : targets + 1, :]
        change_ref[relative] = change if first else change + before_ref[relative]
        return 0

    lax.fori_loop(0, k_ref.shape[0], body, 0, unroll=2)


def change_call(me, sums, coef, k_step, side, last, targets, before=None):
    row_devices, quarter, per_step = k_step.shape
    operands = [me, sums, coef, held(k_step), side]
    if before is not None:
        operands.append(before)
    change = jax.ShapeDtypeStruct((row_devices, targets, quarter), F32)
    outs = (jax.ShapeDtypeStruct((targets, per_step), F32), change) + (() if last else (change,))
    return pl.pallas_call(
        functools.partial(change_kernel, targets, before is None, last),
        name="change",
        in_specs=[pl.BlockSpec(memory_space=pltpu.SMEM)] + in_vmem(len(operands) - 1),
        out_specs=in_vmem(len(outs)),
        out_shape=outs,
        compiler_params=params(),
        cost_estimate=pass_cost(k_step, targets),
    )(*operands)


def gradient_kernel(targets, moved_ref, side_ref, k_ref, square_ref, out_ref):
    out_ref[:targets, :] = jnp.zeros((targets, out_ref.shape[1]), F32)
    out_ref[targets : targets + 1, :] = square_ref[:1, :]

    def body(i, _):
        weighted = (side_ref[i, :targets, :] - moved_ref[i]).astype(BF16)
        out_ref[:targets, :] += jnp.dot(weighted, k_ref[i], preferred_element_type=F32)
        return 0

    lax.fori_loop(0, k_ref.shape[0], body, 0, unroll=2)


def gradient_call(moved, side, k_step, squares, targets):
    return pl.pallas_call(
        functools.partial(gradient_kernel, targets),
        name="gradient",
        in_specs=in_vmem(4),
        out_specs=in_vmem(1)[0],
        out_shape=jax.ShapeDtypeStruct((round_up(targets + 1, 8), k_step.shape[2]), F32),
        compiler_params=params(),
        cost_estimate=pass_cost(k_step, targets),
    )(moved, side, held(k_step), squares)


def scatter_kernel(targets, step, off_ref, dest_ref, coef_ref, delta_ref, out_ref, parts_ref):
    per_step = delta_ref.shape[1]
    blocks = out_ref.shape[1] // POOL_BLOCK
    window = POOL_BLOCK + LANES
    for part, value in enumerate(split3(delta_ref[...])):
        parts_ref[part * targets : (part + 1) * targets, :per_step] = value
    parts_ref[:, per_step:] = jnp.zeros((3 * targets, parts_ref.shape[1] - per_step), BF16)

    @pl.loop(0, blocks // 4)
    def _(four):
        for i in range(4):
            block = 4 * four + i
            columns = pl.ds(pl.multiple_of(block * POOL_BLOCK, POOL_BLOCK), POOL_BLOCK)
            base = pl.multiple_of((off_ref[step, block] // LANES) * LANES, LANES)
            dest = two_rows(dest_ref, step, block) - base
            slots = lax.broadcasted_iota(jnp.int32, (window, POOL_BLOCK), 0)
            pick = jnp.where(slots == dest, 1.0, 0.0).astype(BF16)
            moved = jnp.dot(parts_ref[:, pl.ds(base, window)], pick, preferred_element_type=F32)
            moved = moved[:targets] + moved[targets : 2 * targets] + moved[2 * targets :]
            out_ref[:, columns] = coef_ref[:, columns] + moved


def scatter_call(off, dest, coefs, delta, step):
    targets, per_step = delta.shape
    length = round_up(per_step, LANES) + POOL_BLOCK + LANES
    return pl.pallas_call(
        functools.partial(scatter_kernel, targets, step),
        name="scatter",
        in_specs=[pl.BlockSpec(memory_space=pltpu.SMEM)] + in_vmem(3),
        out_specs=in_vmem(1)[0],
        out_shape=jax.ShapeDtypeStruct(coefs.shape, F32),
        scratch_shapes=[pltpu.VMEM((3 * targets, length), BF16)],
        compiler_params=params(),
        cost_estimate=pl.CostEstimate(flops=10**9, bytes_accessed=10**6, transcendentals=0),
    )(off, dest, coefs, delta)


def swap(value, axis, bit):
    count = lax.axis_size(axis)
    return lax.ppermute(value, axis, [(i, i ^ bit) for i in range(count)])


def own_buffer(value):
    return lax.optimization_barrier(value + lax.optimization_barrier(jnp.zeros((), value.dtype)))


def bits_of(count):
    return [1 << k for k in range(count.bit_length() - 1)]


def last_hop(chunk, row_devices):
    return 2 if (chunk, row_devices) == (3, 8) else chunk & -chunk


def groups_of(row_devices, step):
    if row_devices == 8:
        return FIRST_GROUPS if step == 0 else LATER_GROUPS
    return [(have,) for have in range(row_devices)]


def local(samples, weights, targets, predictions, centres, coefs, block_index):
    rows_dev, features = samples.shape
    pool_dev = centres.shape[0]
    steps, slice_len = block_index.shape
    target_count = targets.shape[0]
    row_devices, cent_devices = lax.axis_size("rows"), lax.axis_size("cent")
    my_row, my_cent = lax.axis_index("rows"), lax.axis_index("cent")
    quarter = rows_dev // cent_devices
    per_step = slice_len * cent_devices // row_devices
    sharpness = 1.3 / math.sqrt(8.0 * features)
    offset = 2.0 * features * sharpness - 1.5 - 0.5 * math.log(rows_dev * row_devices)

    at = my_cent * quarter
    own_rows = lax.dynamic_slice_in_dim(samples, at, quarter, 0)
    own_weight = lax.dynamic_slice_in_dim(weights, at, quarter, 0)[None, :]
    own_target = lax.dynamic_slice_in_dim(targets, at, quarter, 1)
    own_pred = lax.dynamic_slice_in_dim(predictions, at, quarter, 1)
    weighted = (own_weight * (own_target - own_pred)).astype(BF16)
    side_count = round_up(target_count, 16)
    weight_parts = jnp.concatenate(split3_outside(own_weight), axis=0)
    side_block = jnp.concatenate(
        [
            jnp.pad(weighted, ((0, side_count - target_count), (0, 0))),
            jnp.pad(weight_parts, ((0, side_count - 3), (0, features - 2 * quarter))),
        ],
        axis=1,
    )
    chunks = {0: jnp.concatenate([own_rows, side_block], axis=0)}

    high_count = pool_dev // LANES
    place = block_index - my_row * pool_dev
    inside = (place >= 0) & (place < pool_dev)
    high = jnp.where(inside, place // LANES, -1)
    low = jnp.where(inside, place % LANES, 0)
    high_hot = (high[:, None, :] == jnp.arange(high_count)[None, :, None]).astype(BF16)
    low_hot = (low[:, None, :] == jnp.arange(LANES)[None, :, None]).astype(BF16)
    member = jnp.einsum("shl,sgl->shg", high_hot, low_hot, preferred_element_type=F32).astype(BF16)
    for bit in bits_of(cent_devices):
        member = member + swap(member, "cent", bit)

    for chunk in sorted(range(1, row_devices), key=lambda chunk: (bin(chunk).count("1"), chunk)):
        bit = last_hop(chunk, row_devices)
        source = chunks[chunk ^ bit]
        if bit == 1 and chunk ^ bit == row_devices // 2:
            source = own_buffer(source)
        chunks[chunk] = swap(source, "rows", bit)

    upper = (jnp.arange(LANES)[:, None] <= jnp.arange(LANES)[None, :]).astype(BF16)
    before = (jnp.arange(high_count)[:, None] > jnp.arange(high_count)[None, :]).astype(BF16)
    running = jnp.einsum("shg,gk->shk", member, upper, preferred_element_type=F32)
    row_count = running[:, :, -1:]
    row_start = jnp.einsum("hi,sik->shk", before, row_count.astype(BF16), preferred_element_type=F32)
    rank = row_start + running - 1.0
    dest = jnp.where(member > 0, rank, -65536.0).astype(jnp.int32)
    limits = jnp.arange(pool_dev // POOL_BLOCK + 1) * (POOL_BLOCK // LANES)
    earlier = (limits[:, None] > jnp.arange(high_count)[None, :]).astype(BF16)
    off = jnp.einsum("bi,sik->sb", earlier, row_count.astype(BF16), preferred_element_type=F32)
    off = off.astype(jnp.int32)

    me = my_row.astype(jnp.int32)[None]
    blocks = []
    own_coefs = []
    first_half, parts = load_call(centres, coefs)
    pool = [first_half]
    for step in range(steps):
        chosen, norm, own_coef, *more = compact(
            step, off, dest, pool, parts, centres, per_step, target_count
        )
        pool += more
        own_coefs.append(own_coef)
        state = None
        for group in groups_of(row_devices, step):
            state = block_call(
                step == 0, me, group, [chunks[have] for have in group], chosen, norm, state,
                target_count, row_devices, sharpness, offset,
            )
        blocks.append(state)

    info = blocks[0][2]
    sums = blocks[0][1]
    total_change = None
    deltas = []
    for step in range(steps):
        if step > 0:
            bits = bits_of(row_devices)
            for first in range(0, len(bits), 2):
                low = share.astype(BF16)
                pair = bits[first : first + 2]
                for bit in pair + ([sum(pair)] if len(pair) > 1 else []):
                    share = share + swap(low, "rows", bit).astype(F32)
            moved = share if step == 1 else moved + share
            sums = gradient_call(moved, info, blocks[step][0], blocks[step][1], target_count)
        delta, total_change, *more = change_call(
            me, lax.all_gather(sums, "cent"), own_coefs[step], blocks[step][0], info,
            step == steps - 1, target_count, total_change,
        )
        share = more[0] if more else None
        deltas.append(delta)
    coef_now = coefs
    for step in reversed(range(steps)):
        coef_now = scatter_call(off, dest, coef_now, deltas[step], step)

    pieces = total_change
    bits = bits_of(row_devices)
    for first in range(0, len(bits), 2):
        pair = bits[first : first + 2]
        count = 2 ** len(pair)
        pieces = pieces.reshape(pieces.shape[0] // count, count, target_count, quarter)
        kept = pieces[:, 0]
        for k in range(1, count):
            kept = kept + swap(pieces[:, k], "rows", k * pair[0])
        pieces = kept
    own_change = pieces[0]
    full = own_change
    for bit in bits_of(cent_devices):
        other = swap(full, "cent", bit)
        high = (my_cent & bit) > 0
        full = jnp.concatenate([jnp.where(high, other, full), jnp.where(high, full, other)], axis=1)
    return (coef_now, predictions + full)


def solution(mesh):
    in_specs = (
        P("rows", None),
        P("rows"),
        P(None, "rows"),
        P(None, "rows"),
        P("rows", None),
        P(None, "rows"),
        P(None, "cent"),
    )
    out_specs = (P(None, "rows"), P(None, "rows"))
    return jax.shard_map(local, mesh=mesh, in_specs=in_specs, out_specs=out_specs, check_vma=False)
```

```python
import functools
import math

import jax
import jax.numpy as jnp
from jax import lax
from jax.experimental import pallas as pl
from jax.experimental.pallas import tpu as pltpu
from jax.sharding import PartitionSpec as P

RIDGE = 1.0
LANES = 128
POOL_BLOCK = 256
WINDOW = 144
TILE = 512
FIRST_GROUPS = [(0, 1), (2, 4), (5, 6), (3, 7)]
LATER_GROUPS = [(0, 1), (2, 4), (5, 6), (3, 7)]
KERNEL_VMEM = 16 * 2**20
LOG2E = math.log2(math.e)
NT = (((1,), (1,)), ((), ()))
F32 = jnp.float32
BF16 = jnp.bfloat16


def split3(x):
    first = x.astype(BF16)
    rest = x - first.astype(F32)
    second = rest.astype(BF16)
    third = (rest - second.astype(F32)).astype(BF16)
    return first, second, third


def round_up(value, multiple):
    return -(-value // multiple) * multiple


def in_vmem(count):
    return [pl.BlockSpec(memory_space=pltpu.VMEM)] * count


def in_hbm(x):
    return pltpu.with_memory_space_constraint(x, pltpu.HBM)


def held(x):
    return pltpu.with_memory_space_constraint(x, pltpu.VMEM)


def params():
    return pltpu.CompilerParams(vmem_limit_bytes=KERNEL_VMEM)


def two_rows(ref, step, block):
    row = 2 * block
    return jnp.concatenate([ref[step, pl.ds(row, 1), :], ref[step, pl.ds(row + 1, 1), :]], axis=1)


def own_kernel(quarter, at_ref, rows_hbm, weight_hbm, target_hbm, pred_hbm, out_ref, weight_ref, target_ref, pred_ref, done):
    targets = target_ref.shape[0]
    at = pl.ds(pl.multiple_of(at_ref[0] * quarter, quarter), quarter)
    copies = [
        pltpu.make_async_copy(rows_hbm.at[at, :], out_ref.at[pl.ds(0, quarter), :], done.at[0]),
        pltpu.make_async_copy(weight_hbm.at[:, at], weight_ref, done.at[1]),
        pltpu.make_async_copy(target_hbm.at[:, at], target_ref, done.at[2]),
        pltpu.make_async_copy(pred_hbm.at[:, at], pred_ref, done.at[3]),
    ]
    for copy in copies:
        copy.start()
    rows = out_ref.shape[0] - quarter
    out_ref[quarter:, :] = jnp.zeros((rows, out_ref.shape[1]), BF16)
    for copy in copies[1:]:
        copy.wait()
    weight = weight_ref[...]
    weighted = (weight * (target_ref[...] - pred_ref[...])).astype(BF16)
    out_ref[quarter : quarter + targets, :quarter] = weighted
    row = lax.broadcasted_iota(jnp.int32, (rows, quarter), 0)
    parts = jnp.zeros((rows, quarter), F32)
    for i, part in enumerate(split3(weight)):
        parts = jnp.where(row == i, part.astype(F32), parts)
    out_ref[quarter:, quarter : 2 * quarter] = parts.astype(BF16)
    copies[0].wait()


def own_call(my_cent, samples, weights, targets, predictions, quarter):
    target_count = targets.shape[0]
    return pl.pallas_call(
        functools.partial(own_kernel, quarter),
        name="own",
        in_specs=[pl.BlockSpec(memory_space=pltpu.SMEM)] + [pl.BlockSpec(memory_space=pltpu.HBM)] * 4,
        out_specs=in_vmem(1)[0],
        out_shape=jax.ShapeDtypeStruct((quarter + round_up(target_count, 16), samples.shape[1]), BF16),
        scratch_shapes=[
            pltpu.VMEM((1, quarter), F32),
            pltpu.VMEM((target_count, quarter), F32),
            pltpu.VMEM((target_count, quarter), F32),
            pltpu.SemaphoreType.DMA((4,)),
        ],
        compiler_params=params(),
        cost_estimate=pl.CostEstimate(flops=10**5, bytes_accessed=10**6, transcendentals=0),
    )(
        my_cent.astype(jnp.int32)[None], in_hbm(samples), in_hbm(weights[None, :]),
        in_hbm(targets), in_hbm(predictions),
    )


def pool_copy(source, target, half, block, done):
    at = pl.ds(pl.multiple_of(block * POOL_BLOCK, POOL_BLOCK), POOL_BLOCK)
    start = half * target.shape[0] + block * POOL_BLOCK
    start = pl.multiple_of(start, POOL_BLOCK)
    return pltpu.make_async_copy(source.at[pl.ds(start, POOL_BLOCK), :], target.at[at, :], done.at[block])


def load_kernel(targets, pool_hbm, coefs_hbm, pool_ref, parts_ref, coefs_ref, arrived, coefs_arrived):
    copies = [pool_copy(pool_hbm, pool_ref, 0, block, arrived) for block in range(arrived.shape[0])]
    coefs_copy = pltpu.make_async_copy(coefs_hbm, coefs_ref, coefs_arrived)
    coefs_copy.start()
    for copy in copies:
        copy.start()
    coefs_copy.wait()
    parts_ref[3 * targets :, :] = jnp.zeros((LANES - 3 * targets, parts_ref.shape[1]), BF16)
    for part, value in enumerate(split3(coefs_ref[...])):
        parts_ref[part * targets : (part + 1) * targets, :] = value
    for copy in copies:
        copy.wait()


def load_call(pool, coefs):
    return pl.pallas_call(
        functools.partial(load_kernel, coefs.shape[0]),
        name="load",
        in_specs=[pl.BlockSpec(memory_space=pltpu.HBM)] * 2,
        out_specs=in_vmem(2),
        out_shape=(
            pltpu.VMEM((pool.shape[0] // 2, pool.shape[1]), BF16),
            pltpu.VMEM((LANES, pool.shape[0]), BF16),
        ),
        scratch_shapes=[
            pltpu.VMEM(coefs.shape, F32),
            pltpu.SemaphoreType.DMA((pool.shape[0] // POOL_BLOCK // 2,)),
            pltpu.SemaphoreType.DMA,
        ],
        compiler_params=params(),
        cost_estimate=pl.CostEstimate(flops=10**6, bytes_accessed=3 * 10**6, transcendentals=0),
    )(in_hbm(pool), in_hbm(coefs))


def compact_kernel(step, per_step, targets, off_ref, dest_ref, *refs):
    loads = step == 0
    if loads:
        first_ref, parts_ref, pool_hbm, out_ref, norm_ref, coef_ref, second_ref, side_out, arrived = refs
    else:
        first_ref, second_ref, parts_ref, out_ref, norm_ref, coef_ref, side_out = refs
    features = out_ref.shape[1]
    half = first_ref.shape[0] // POOL_BLOCK
    blocks = 2 * half
    tile = math.gcd(per_step, 512)

    if loads:
        for block in range(half):
            pool_copy(pool_hbm, second_ref, 1, block, arrived).start()
    widest = 0
    for block in range(blocks):
        widest = jnp.maximum(widest, off_ref[step, block + 1] - (off_ref[step, block] // 16) * 16)
    narrow = widest <= WINDOW
    out_ref[:16, :] = jnp.zeros((16, features), BF16)
    side_out[:16, :] = jnp.zeros((16, LANES), BF16)

    def place(pool_ref, part, index, window):
        block = part * half + index
        base = pl.multiple_of((off_ref[step, block] // 16) * 16, 16)
        dest = two_rows(dest_ref, step, block) - base
        slots = lax.broadcasted_iota(jnp.int32, (window, POOL_BLOCK), 0)
        pick = jnp.where(slots == dest, 1.0, 0.0).astype(BF16)
        at = pl.ds(pl.multiple_of(block * POOL_BLOCK, POOL_BLOCK), POOL_BLOCK)
        inner = pl.ds(pl.multiple_of(index * POOL_BLOCK, POOL_BLOCK), POOL_BLOCK)
        after = pl.ds(pl.multiple_of(base + 16, 16), window - 16)
        packed = jnp.dot(pick, pool_ref[inner, :], preferred_element_type=F32).astype(BF16)
        side = lax.dot_general(pick, parts_ref[:, at], NT, preferred_element_type=F32).astype(BF16)
        for rows, target in ((packed, out_ref), (side, side_out)):
            target[pl.ds(base, 16), :] += rows[:16]
            target[after, :] = rows[16:]

    def walk(window, width):
        for part, pool_ref in enumerate((first_ref, second_ref)):

            @pl.loop(0, half // width)
            def _(group, part=part, pool_ref=pool_ref):
                if loads and part == 1:
                    for i in range(width):
                        pool_copy(pool_hbm, second_ref, 1, width * group + i, arrived).wait()
                for i in range(width):
                    place(pool_ref, part, width * group + i, window)

    @pl.when(narrow)
    def _():
        walk(WINDOW, 4)

    @pl.when(jnp.logical_not(narrow))
    def _():
        walk(POOL_BLOCK + 16, 1)

    eye = lax.broadcasted_iota(jnp.int32, (3 * targets, LANES), 0) == lax.broadcasted_iota(
        jnp.int32, (3 * targets, LANES), 1
    )
    eye = jnp.where(eye, 1.0, 0.0).astype(BF16)
    for first in range(0, per_step, tile):
        rows = out_ref[first : first + tile, :].astype(F32)
        square = rows * rows
        narrow_sum = square[:, :LANES]
        for lane in range(LANES, features, LANES):
            narrow_sum = narrow_sum + square[:, lane : lane + LANES]
        norm = jnp.sum(jnp.transpose(narrow_sum), axis=0, keepdims=True)
        norm_ref[:, first : first + tile] = jnp.broadcast_to(norm, (8, tile))
        parts = lax.dot_general(eye, side_out[first : first + tile, :], NT, preferred_element_type=F32)
        coef_ref[:, first : first + tile] = (
            parts[:targets] + parts[targets : 2 * targets] + parts[2 * targets :]
        )


def compact(step, off, dest, pool, parts, pool_hbm, per_step, targets):
    features = pool_hbm.shape[1]
    length = round_up(per_step, 16) + POOL_BLOCK + 16
    outs = [
        pltpu.VMEM((length, features), BF16),
        pltpu.VMEM((8, per_step), F32),
        pltpu.VMEM((targets, per_step), F32),
    ]
    scratch = [pltpu.VMEM((length, LANES), BF16)]
    operands = [off, dest, *[held(half) for half in pool], held(parts)]
    specs = [pl.BlockSpec(memory_space=pltpu.SMEM), *in_vmem(len(operands) - 1)]
    if step == 0:
        half = pool[0].shape
        outs.append(pltpu.VMEM(half, BF16))
        scratch.append(pltpu.SemaphoreType.DMA((half[0] // POOL_BLOCK,)))
        specs.append(pl.BlockSpec(memory_space=pltpu.HBM))
        operands.append(in_hbm(pool_hbm))
    return pl.pallas_call(
        functools.partial(compact_kernel, step, per_step, targets),
        name="compact",
        in_specs=specs,
        out_specs=in_vmem(len(outs)),
        out_shape=tuple(outs),
        scratch_shapes=scratch,
        compiler_params=params(),
        cost_estimate=pl.CostEstimate(flops=2 * 10**9, bytes_accessed=6 * 10**6, transcendentals=0),
    )(*operands)


def block_kernel(first_step, targets, quarter, group, scale, offset, me_ref, chosen_ref, norm_ref, *refs):
    count = len(group)
    chunk_refs = refs[:count]
    outs = refs[count:]
    slots = [me_ref[0] ^ have for have in group]
    outs_count = 3 if first_step else 2
    sums_in = outs[1] if len(outs) > outs_count else None
    outs = outs[-outs_count:]
    k_ref, sums_ref = outs[:2]
    per_step = sums_ref.shape[1]
    square_row = targets if first_step else 0
    tile = math.gcd(per_step, TILE)

    rows = jnp.concatenate([ref[:quarter, :] for ref in chunk_refs], axis=0)
    wide_rows = rows.astype(F32)
    row_norm = jnp.sum(wide_rows * wide_rows, axis=1, keepdims=True) * (scale * LOG2E) - offset * LOG2E
    columns = []
    for i, ref in enumerate(chunk_refs):
        parts = ref[quarter : quarter + 3, quarter : 2 * quarter].astype(F32)
        weight = jnp.sum(parts, axis=0, keepdims=True)
        columns.append(jnp.transpose(jnp.broadcast_to(weight, (8, quarter)))[:, :1])
        if first_step:
            side_ref = outs[2]
            side_ref[slots[i], :targets, :] = ref[quarter : quarter + targets, :quarter].astype(F32)
            side_ref[slots[i], targets:, :] = jnp.broadcast_to(
                weight, (side_ref.shape[1] - targets, quarter)
            )
    weight_column = jnp.concatenate(columns, axis=0)
    weighted = jnp.concatenate([ref[quarter : quarter + targets, :quarter] for ref in chunk_refs], axis=1)

    for first in range(0, per_step, tile):
        dots = lax.dot_general(rows, chosen_ref[first : first + tile, :], NT, preferred_element_type=F32)
        centre = norm_ref[:1, first : first + tile] * (scale * LOG2E)
        k_low = jnp.exp2(dots * (2.0 * scale * LOG2E) - row_norm - centre).astype(BF16)
        for i in range(count):
            k_ref[slots[i], :, first : first + tile] = k_low[i * quarter : (i + 1) * quarter]
        wide = k_low.astype(F32)
        updates = [(square_row, 1, jnp.sum(weight_column * (wide * wide), axis=0, keepdims=True))]
        if first_step:
            updates.append((0, targets, jnp.dot(weighted, k_low, preferred_element_type=F32)))
        for row, size, value in updates:
            if sums_in is not None:
                value = value + sums_in[row : row + size, first : first + tile]
            sums_ref[row : row + size, first : first + tile] = value


def block_call(first_step, me, group, chunks, chosen, norm, state, targets, row_devices, scale, offset):
    features = chosen.shape[1]
    per_step = norm.shape[1]
    count = len(chunks)
    quarter = chunks[0].shape[0] - round_up(targets, 16)
    operands = [me, held(chosen), held(norm), *chunks]
    outs = [
        pltpu.VMEM((row_devices, quarter, per_step), BF16),
        pltpu.VMEM((round_up(targets + 1, 8) if first_step else 8, per_step), F32),
    ]
    if first_step:
        outs.append(pltpu.VMEM((row_devices, round_up(targets + 1, 8), quarter), F32))
    aliases = {}
    if state is not None:
        aliases = {len(operands) + i: i for i in range(len(outs))}
        operands += [held(x) for x in state]
    entries = count * quarter * per_step
    return pl.pallas_call(
        functools.partial(block_kernel, first_step, targets, quarter, group, scale, offset),
        name="kernel_block",
        in_specs=[pl.BlockSpec(memory_space=pltpu.SMEM)] + in_vmem(len(operands) - 1),
        out_specs=in_vmem(len(outs)),
        out_shape=tuple(outs),
        input_output_aliases=aliases,
        compiler_params=params(),
        cost_estimate=pl.CostEstimate(
            flops=2 * entries * features, bytes_accessed=2 * entries, transcendentals=entries
        ),
    )(*operands)


def pass_cost(k_step, targets):
    entries = math.prod(k_step.shape)
    return pl.CostEstimate(flops=2 * targets * entries, bytes_accessed=2 * entries, transcendentals=0)


def change_kernel(targets, first, last, me_ref, sums_ref, coef_ref, k_ref, side_ref, *refs):
    before_ref = None if first else refs[0]
    outs = list(refs if first else refs[1:])
    delta_ref, change_ref = outs[:2]
    total = sums_ref[0]
    for i in range(1, sums_ref.shape[0]):
        total = total + sums_ref[i]
    delta = (total[:targets] - RIDGE * coef_ref[...]) / (total[targets : targets + 1] + RIDGE)
    delta_ref[...] = delta
    low = delta.astype(BF16)

    def body(i, _):
        change = lax.dot_general(low, k_ref[i], NT, preferred_element_type=F32)
        relative = i ^ me_ref[0]
        if not last:
            outs[2][i] = change * side_ref[i, targets : targets + 1, :]
        change_ref[relative] = change if first else change + before_ref[relative]
        return 0

    lax.fori_loop(0, k_ref.shape[0], body, 0, unroll=2)


def change_call(me, sums, coef, k_step, side, last, targets, before=None):
    row_devices, quarter, per_step = k_step.shape
    operands = [me, sums, coef, held(k_step), side]
    if before is not None:
        operands.append(before)
    change = jax.ShapeDtypeStruct((row_devices, targets, quarter), F32)
    outs = (jax.ShapeDtypeStruct((targets, per_step), F32), change) + (() if last else (change,))
    return pl.pallas_call(
        functools.partial(change_kernel, targets, before is None, last),
        name="change",
        in_specs=[pl.BlockSpec(memory_space=pltpu.SMEM)] + in_vmem(len(operands) - 1),
        out_specs=in_vmem(len(outs)),
        out_shape=outs,
        compiler_params=params(),
        cost_estimate=pass_cost(k_step, targets),
    )(*operands)


def gradient_kernel(targets, moved_ref, side_ref, k_ref, square_ref, out_ref):
    out_ref[:targets, :] = jnp.zeros((targets, out_ref.shape[1]), F32)
    out_ref[targets : targets + 1, :] = square_ref[:1, :]

    def body(i, _):
        weighted = (side_ref[i, :targets, :] - moved_ref[i]).astype(BF16)
        out_ref[:targets, :] += jnp.dot(weighted, k_ref[i], preferred_element_type=F32)
        return 0

    lax.fori_loop(0, k_ref.shape[0], body, 0, unroll=2)


def gradient_call(moved, side, k_step, squares, targets):
    return pl.pallas_call(
        functools.partial(gradient_kernel, targets),
        name="gradient",
        in_specs=in_vmem(4),
        out_specs=in_vmem(1)[0],
        out_shape=jax.ShapeDtypeStruct((round_up(targets + 1, 8), k_step.shape[2]), F32),
        compiler_params=params(),
        cost_estimate=pass_cost(k_step, targets),
    )(moved, side, held(k_step), squares)


def scatter_kernel(targets, step, off_ref, dest_ref, coef_ref, delta_ref, out_ref, parts_ref):
    per_step = delta_ref.shape[1]
    blocks = out_ref.shape[1] // POOL_BLOCK
    window = POOL_BLOCK + LANES
    for part, value in enumerate(split3(delta_ref[...])):
        parts_ref[part * targets : (part + 1) * targets, :per_step] = value
    parts_ref[:, per_step:] = jnp.zeros((3 * targets, parts_ref.shape[1] - per_step), BF16)

    @pl.loop(0, blocks // 4)
    def _(four):
        for i in range(4):
            block = 4 * four + i
            columns = pl.ds(pl.multiple_of(block * POOL_BLOCK, POOL_BLOCK), POOL_BLOCK)
            base = pl.multiple_of((off_ref[step, block] // LANES) * LANES, LANES)
            dest = two_rows(dest_ref, step, block) - base
            slots = lax.broadcasted_iota(jnp.int32, (window, POOL_BLOCK), 0)
            pick = jnp.where(slots == dest, 1.0, 0.0).astype(BF16)
            moved = jnp.dot(parts_ref[:, pl.ds(base, window)], pick, preferred_element_type=F32)
            moved = moved[:targets] + moved[targets : 2 * targets] + moved[2 * targets :]
            out_ref[:, columns] = coef_ref[:, columns] + moved


def scatter_call(off, dest, coefs, delta, step):
    targets, per_step = delta.shape
    length = round_up(per_step, LANES) + POOL_BLOCK + LANES
    return pl.pallas_call(
        functools.partial(scatter_kernel, targets, step),
        name="scatter",
        in_specs=[pl.BlockSpec(memory_space=pltpu.SMEM)] + in_vmem(3),
        out_specs=in_vmem(1)[0],
        out_shape=jax.ShapeDtypeStruct(coefs.shape, F32),
        scratch_shapes=[pltpu.VMEM((3 * targets, length), BF16)],
        compiler_params=params(),
        cost_estimate=pl.CostEstimate(flops=10**9, bytes_accessed=10**6, transcendentals=0),
    )(off, dest, coefs, delta)


def swap(value, axis, bit):
    count = lax.axis_size(axis)
    return lax.ppermute(value, axis, [(i, i ^ bit) for i in range(count)])


def own_buffer(value):
    return lax.optimization_barrier(value + lax.optimization_barrier(jnp.zeros((), value.dtype)))


def bits_of(count):
    return [1 << k for k in range(count.bit_length() - 1)]


def last_hop(chunk, row_devices):
    return 2 if (chunk, row_devices) == (3, 8) else chunk & -chunk


def groups_of(row_devices, step):
    if row_devices == 8:
        return FIRST_GROUPS if step == 0 else LATER_GROUPS
    return [(have,) for have in range(row_devices)]


def local(samples, weights, targets, predictions, centres, coefs, block_index):
    rows_dev, features = samples.shape
    pool_dev = centres.shape[0]
    steps, slice_len = block_index.shape
    target_count = targets.shape[0]
    row_devices, cent_devices = lax.axis_size("rows"), lax.axis_size("cent")
    my_row, my_cent = lax.axis_index("rows"), lax.axis_index("cent")
    quarter = rows_dev // cent_devices
    per_step = slice_len * cent_devices // row_devices
    sharpness = 1.3 / math.sqrt(8.0 * features)
    offset = 2.0 * features * sharpness - 1.5 - 0.5 * math.log(rows_dev * row_devices)

    chunks = {0: own_call(my_cent, samples, weights, targets, predictions, quarter)}

    high_count = pool_dev // LANES
    place = block_index - my_row * pool_dev
    inside = (place >= 0) & (place < pool_dev)
    high = jnp.where(inside, place // LANES, -1)
    low = jnp.where(inside, place % LANES, 0)
    high_hot = (high[:, None, :] == jnp.arange(high_count)[None, :, None]).astype(BF16)
    low_hot = (low[:, None, :] == jnp.arange(LANES)[None, :, None]).astype(BF16)
    member = jnp.einsum("shl,sgl->shg", high_hot, low_hot, preferred_element_type=F32).astype(BF16)
    for bit in bits_of(cent_devices):
        member = member + swap(member, "cent", bit)

    for chunk in sorted(range(1, row_devices), key=lambda chunk: (bin(chunk).count("1"), chunk)):
        bit = last_hop(chunk, row_devices)
        source = chunks[chunk ^ bit]
        if bit == 1 and chunk ^ bit == row_devices // 2:
            source = own_buffer(source)
        chunks[chunk] = swap(source, "rows", bit)

    upper = (jnp.arange(LANES)[:, None] <= jnp.arange(LANES)[None, :]).astype(BF16)
    before = (jnp.arange(high_count)[:, None] > jnp.arange(high_count)[None, :]).astype(BF16)
    running = jnp.einsum("shg,gk->shk", member, upper, preferred_element_type=F32)
    row_count = running[:, :, -1:]
    row_start = jnp.einsum("hi,sik->shk", before, row_count.astype(BF16), preferred_element_type=F32)
    rank = row_start + running - 1.0
    dest = jnp.where(member > 0, rank, -65536.0).astype(jnp.int32)
    limits = jnp.arange(pool_dev // POOL_BLOCK + 1) * (POOL_BLOCK // LANES)
    earlier = (limits[:, None] > jnp.arange(high_count)[None, :]).astype(BF16)
    off = jnp.einsum("bi,sik->sb", earlier, row_count.astype(BF16), preferred_element_type=F32)
    off = off.astype(jnp.int32)

    me = my_row.astype(jnp.int32)[None]
    blocks = []
    own_coefs = []
    first_half, parts = load_call(centres, coefs)
    pool = [first_half]
    for step in range(steps):
        chosen, norm, own_coef, *more = compact(
            step, off, dest, pool, parts, centres, per_step, target_count
        )
        pool += more
        own_coefs.append(own_coef)
        state = None
        for group in groups_of(row_devices, step):
            state = block_call(
                step == 0, me, group, [chunks[have] for have in group], chosen, norm, state,
                target_count, row_devices, sharpness, offset,
            )
        blocks.append(state)

    info = blocks[0][2]
    sums = blocks[0][1]
    total_change = None
    deltas = []
    for step in range(steps):
        if step > 0:
            bits = bits_of(row_devices)
            for first in range(0, len(bits), 2):
                low = share.astype(BF16)
                pair = bits[first : first + 2]
                for bit in pair + ([sum(pair)] if len(pair) > 1 else []):
                    share = share + swap(low, "rows", bit).astype(F32)
            moved = share if step == 1 else moved + share
            sums = gradient_call(moved, info, blocks[step][0], blocks[step][1], target_count)
        delta, total_change, *more = change_call(
            me, lax.all_gather(sums, "cent"), own_coefs[step], blocks[step][0], info,
            step == steps - 1, target_count, total_change,
        )
        share = more[0] if more else None
        deltas.append(delta)
    coef_now = coefs
    for step in reversed(range(steps)):
        coef_now = scatter_call(off, dest, coef_now, deltas[step], step)

    pieces = total_change
    bits = bits_of(row_devices)
    for first in range(0, len(bits), 2):
        pair = bits[first : first + 2]
        count = 2 ** len(pair)
        pieces = pieces.reshape(pieces.shape[0] // count, count, target_count, quarter)
        kept = pieces[:, 0]
        for k in range(1, count):
            kept = kept + swap(pieces[:, k], "rows", k * pair[0])
        pieces = kept
    own_change = pieces[0]
    full = own_change
    for bit in bits_of(cent_devices):
        other = swap(full, "cent", bit)
        high = (my_cent & bit) > 0
        full = jnp.concatenate([jnp.where(high, other, full), jnp.where(high, full, other)], axis=1)
    return (coef_now, predictions + full)


def solution(mesh):
    in_specs = (
        P("rows", None),
        P("rows"),
        P(None, "rows"),
        P(None, "rows"),
        P("rows", None),
        P(None, "rows"),
        P(None, "cent"),
    )
    out_specs = (P(None, "rows"), P(None, "rows"))
    return jax.shard_map(local, mesh=mesh, in_specs=in_specs, out_specs=out_specs, check_vma=False)
```
